128 devices in a mesh: dp: 16 (over y_lo, z, core), tensor: 8 (over x, y_hi).
Axes of the slice: x: 4, y: 4 (y_hi: 2, y_lo: 2; y = y_hi * 2 + y_lo), z: 4, core: 2. Of those that a mesh axis runs over, the one named last changes fastest.
Arguments:
- hidden_in: float32 [20480, 1024], P(('dp', 'tensor')), may hold values from -6 to 6
- w_qkv: bfloat16 [1024, 2, 3, 1024], P('dp', None, None, 'tensor'), may hold values from -0.1875 to 0.1875
- w_attn_out: bfloat16 [1024, 2, 1024], P('dp', None, 'tensor'), may hold values from -0.75 to 0.75
- w_up: bfloat16 [1024, 2, 4096], P('dp', None, 'tensor'), may hold values from -0.1875 to 0.1875
- w_down: bfloat16 [1024, 2, 4096], P('dp', None, 'tensor'), may hold values from -0.09375 to 0.09375
- qv_bias: bfloat16 [64, 2, 2, 16], P('dp', None, None, 'tensor'), may hold values from -3 to 3
- up_bias: bfloat16 [64, 2, 64], P('dp', None, 'tensor'), may hold values from -3 to 3
- ln_gain: bfloat16 [1024, 2, 2], P('dp'), may hold values from 0.5 to 1.5
- row_bias: bfloat16 [1024, 2, 4], P('dp'), may hold values from -3 to 3
- cotangent: float32 [20480, 1024], P(('dp', 'tensor')), may hold values from -1.5 to 1.5
Outputs:
- hidden_out: float32 [20480, 1024], P(('dp', 'tensor'))
- grad_in: float32 [20480, 1024], P(('dp', 'tensor'))
- grad_w_qkv: float32 [1024, 2, 3, 1024], P('dp', None, None, 'tensor')
- grad_w_attn_out: float32 [1024, 2, 1024], P('dp', None, 'tensor')
- grad_w_up: float32 [1024, 2, 4096], P('dp', None, 'tensor')
- grad_w_down: float32 [1024, 2, 4096], P('dp', None, 'tensor')
- grad_qv_bias: float32 [64, 2, 2, 16], P('dp', None, None, 'tensor')
- grad_up_bias: float32 [64, 2, 64], P('dp', None, 'tensor')
- grad_ln_gain: float32 [1024, 2, 2], P('dp')
- grad_row_bias: float32 [1024, 2, 4], P('dp')
The draws below stay inside these ranges and needn't reach their ends.
All inputs are finite; a program needn't handle non-finite values.
Results may differ from the reference program's by a relative error of at most 0.03.
Values may be sent and summed in bfloat16 or wider, within the bound.
No kernel may reach another device: no remote copies, remote signals or barrier semaphores. Data moves between devices by JAX's collectives and lax.ppermute only.
A program may use at most 192 MiB of HBM per device.

```python
from functools import partial
import jax
import jax.numpy as jnp
from jax import lax

D = 1024
HEADS = 16
HEAD_DIM = 64
FF = 4096
L = 2
LEN = 160
TOKENS = 20480


def block_levels(key, shape, split, low, top_value):
    loudness, own = 1.0, jax.random.fold_in(key, 6)
    for axis_at, blocks in split:
        draws = jnp.exp(jax.random.uniform(jax.random.fold_in(own, axis_at), (blocks,), jnp.float32, low / len(split), top_value / len(split)))
        loudness = loudness * jnp.repeat(draws, shape[axis_at] // blocks).reshape([-1 if axis == axis_at else 1 for axis in range(len(shape))])
    return loudness


def gaussian(stream_key, dims, deviation, reach, cuts=(), held_as=jnp.bfloat16):
    entries = jax.random.normal(stream_key, dims, jnp.float32) * deviation
    if len(cuts) > 0:
        entries = block_levels(stream_key, dims, cuts, -0.22, 0.18) * entries
    return jnp.clip(entries, min=-reach, max=reach).astype(held_as)


def setup_inputs(seed: int = 0) -> dict:
    seeds = jax.random.split(jax.random.key(seed), 11)
    return {
        "hidden_in": gaussian(seeds[0], (TOKENS, D), 1.0, 6.0, ((0, 128),), jnp.float32),
        "w_qkv": gaussian(seeds[1], (D, L, 3, D), D ** -0.5, 0.1875, ((0, 16), (3, 8))),
        "w_attn_out": gaussian(seeds[2], (D, L, D), (D // 16) ** -0.5, 0.75, ((0, 16), (2, 8))),
        "w_up": gaussian(seeds[3], (D, L, FF), D ** -0.5, 0.1875, ((0, 16), (2, 8))),
        "w_down": gaussian(seeds[4], (D, L, FF), FF ** -0.5, 0.09375, ((0, 16), (2, 8))),
        "qv_bias": gaussian(seeds[5], (HEAD_DIM, L, 2, HEADS), 0.5, 3.0, ((0, 16), (3, 8))),
        "up_bias": gaussian(seeds[6], (HEAD_DIM, L, FF // HEAD_DIM), 0.5, 3.0, ((0, 16), (2, 8))),
        "ln_gain": jnp.clip(1.0 + 0.1 * jax.random.normal(seeds[7], (D, L, 2), jnp.float32), 0.5, 1.5).astype(jnp.bfloat16),
        "row_bias": gaussian(seeds[8], (D, L, 4), 0.5, 3.0, ((0, 16),)),
        "cotangent": gaussian(seeds[9], (TOKENS, D), 0.25, 1.5, ((0, 128),), jnp.float32),
    }


epsilon = 1e-05

def to_half(values):
    return lax.optimization_barrier(values.astype(jnp.bfloat16))

def narrow(values):
    return to_half(values).astype(jnp.float32)

def norm_parts(hidden, gain, shift):
    center = lax.optimization_barrier(jnp.mean(hidden, axis=-1, keepdims=True))
    centered = hidden - center
    variance = lax.optimization_barrier(jnp.mean(centered * centered, axis=-1, keepdims=True))
    inverse = lax.rsqrt(variance + epsilon)
    normed = centered * inverse
    return (normed, inverse, normed * gain + shift)

def norm_back(upstream, normed, inverse, gain):
    scaled = upstream * gain
    center = lax.optimization_barrier(jnp.mean(scaled, axis=-1, keepdims=True))
    spread = lax.optimization_barrier(jnp.mean(scaled * normed, axis=-1, keepdims=True))
    result = inverse * (scaled - center - normed * spread)
    return (result, lax.optimization_barrier(jnp.sum(upstream * normed, axis=0)), lax.optimization_barrier(jnp.sum(upstream, axis=0)))

def alibi_scores(query, keys, slopes):
    length = query.shape[1]
    scores = jnp.einsum('sqhd,skhd->shqk', query, keys) * query.shape[3] ** (-0.5)
    row_index = lax.broadcasted_iota(jnp.int32, (length, length), 0)
    col_index = lax.broadcasted_iota(jnp.int32, (length, length), 1)
    offset = (col_index - row_index).astype(jnp.float32)
    scores = scores + slopes[None, :, None, None] * offset[None, None]
    return jnp.where((col_index <= row_index)[None, None], scores, -jnp.inf)

def attend_block(block, slopes):
    query_part = block[:, :, 0].astype(jnp.float32)
    key_part = block[:, :, 1].astype(jnp.float32)
    value_part = block[:, :, 2].astype(jnp.float32)
    scores = alibi_scores(query_part, key_part, slopes)
    highest = lax.optimization_barrier(jnp.max(scores, axis=-1, keepdims=True))
    log_total = highest + jnp.log(lax.optimization_barrier(jnp.sum(jnp.exp(scores - highest), axis=-1, keepdims=True)))
    chance = narrow(jnp.exp(scores - log_total))
    context = jnp.einsum('shqk,skhd->sqhd', chance, value_part)
    return (to_half(context), log_total)

def attend_back(inputs, slopes):
    block, log_total, d_context = inputs
    query_part = block[:, :, 0].astype(jnp.float32)
    key_part = block[:, :, 1].astype(jnp.float32)
    value_part = block[:, :, 2].astype(jnp.float32)
    d_wide = d_context.astype(jnp.float32)
    chance = jnp.exp(alibi_scores(query_part, key_part, slopes) - log_total)
    d_value = jnp.einsum('shqk,sqhd->skhd', narrow(chance), d_wide)
    d_chance = jnp.einsum('sqhd,skhd->shqk', d_wide, value_part)
    inner_sum = lax.optimization_barrier(jnp.sum(chance * d_chance, axis=-1, keepdims=True))
    d_scores = narrow(chance * (d_chance - inner_sum) * query_part.shape[3] ** (-0.5))
    d_query = jnp.einsum('shqk,skhd->sqhd', d_scores, key_part)
    d_key = jnp.einsum('shqk,sqhd->skhd', d_scores, query_part)
    return (d_query, d_key, d_value)

def reference(hidden_in, w_qkv, w_attn_out, w_up, w_down, qv_bias, up_bias, ln_gain, row_bias, cotangent):
    token_count = hidden_in.shape[0]
    seq_count = token_count // LEN
    slopes = jnp.exp2(-8.0 * (jnp.arange(HEADS).astype(jnp.float32) + 1.0) / HEADS)
    hidden = hidden_in
    stored = []
    for layer_index in range(L):
        gains = ln_gain[:, layer_index].astype(jnp.float32)
        shifts = row_bias[:, layer_index].astype(jnp.float32)
        qv_wide = jnp.transpose(qv_bias[:, layer_index].astype(jnp.float32), (1, 2, 0)).reshape(2, D)
        qkv_shift = jnp.stack([qv_wide[0], jnp.zeros_like(qv_wide[0]), qv_wide[1]])
        raise_shift = jnp.transpose(up_bias[:, layer_index].astype(jnp.float32)).reshape(FF)
        w_mix = w_qkv[:, layer_index].astype(jnp.float32)
        w_back = w_attn_out[:, layer_index].astype(jnp.float32)
        w_raise = w_up[:, layer_index].astype(jnp.float32)
        w_lower = w_down[:, layer_index].astype(jnp.float32)
        normed_one, inverse_one, first = norm_parts(hidden, gains[:, 0], shifts[:, 0])
        first = narrow(first)
        packed = to_half(jnp.einsum('nd,dtc->ntc', first, w_mix) + qkv_shift)
        blocks = packed.reshape(seq_count, 1, LEN, 3, HEADS, HEAD_DIM)
        context, log_total = lax.map(lambda block: attend_block(block, slopes), blocks)
        context_flat = context.reshape(token_count, D).astype(jnp.float32)
        mixed = hidden + jnp.einsum('nc,dc->nd', context_flat, w_back) + shifts[:, 2]
        normed_two, inverse_two, second = norm_parts(mixed, gains[:, 1], shifts[:, 1])
        second = narrow(second)
        raised = jnp.einsum('nd,df->nf', second, w_raise) + raise_shift
        activated = narrow(jax.nn.gelu(raised, approximate=True))
        hidden = mixed + jnp.einsum('nf,df->nd', activated, w_lower) + shifts[:, 3]
        stored.append((normed_one, inverse_one, first, packed, log_total, context, context_flat, normed_two, inverse_two, second, raised, activated))
    hidden_out = hidden
    upstream = cotangent
    results = [None] * L
    for layer_index in reversed(range(L)):
        normed_one, inverse_one, first, packed, log_total, context, context_flat, normed_two, inverse_two, second, raised, activated = stored[layer_index]
        gains = ln_gain[:, layer_index].astype(jnp.float32)
        w_mix = w_qkv[:, layer_index].astype(jnp.float32)
        w_back = w_attn_out[:, layer_index].astype(jnp.float32)
        w_raise = w_up[:, layer_index].astype(jnp.float32)
        w_lower = w_down[:, layer_index].astype(jnp.float32)
        d_out = narrow(upstream)
        g_lower_shift = lax.optimization_barrier(jnp.sum(upstream, axis=0))
        d_active = jnp.einsum('nd,df->nf', d_out, w_lower)
        unused, pull = jax.vjp(partial(jax.nn.gelu, approximate=True), raised)
        d_raised = pull(d_active)[0]
        d_raised_half = narrow(d_raised)
        g_lower = jnp.einsum('nd,nf->df', d_out, activated)
        g_raise = jnp.einsum('nd,nf->df', second, d_raised_half)
        g_raise_shift = lax.optimization_barrier(jnp.sum(d_raised, axis=0))
        d_second = jnp.einsum('nf,df->nd', d_raised_half, w_raise)
        d_norm_two, g_gain_two, g_shift_two = norm_back(d_second, normed_two, inverse_two, gains[:, 1])
        d_mixed = upstream + d_norm_two
        d_mixed_half = narrow(d_mixed)
        g_back_shift = lax.optimization_barrier(jnp.sum(d_mixed, axis=0))
        d_context = to_half(jnp.einsum('nd,dc->nc', d_mixed_half, w_back))
        g_back = jnp.einsum('nd,nc->dc', d_mixed_half, context_flat)
        blocks = packed.reshape(seq_count, 1, LEN, 3, HEADS, HEAD_DIM)
        d_blocks = d_context.reshape(seq_count, 1, LEN, HEADS, HEAD_DIM)
        d_query, d_key, d_value = lax.map(lambda inputs: attend_back(inputs, slopes), (blocks, log_total, d_blocks))
        d_query = d_query.reshape(token_count, D)
        d_key = d_key.reshape(token_count, D)
        d_value = d_value.reshape(token_count, D)
        d_packed = narrow(jnp.stack([d_query, d_key, d_value], axis=1))
        g_mix = jnp.einsum('nd,ntc->dtc', first, d_packed)
        g_qv = jnp.stack([lax.optimization_barrier(jnp.sum(d_query, axis=0)), lax.optimization_barrier(jnp.sum(d_value, axis=0))])
        d_first = jnp.einsum('ntc,dtc->nd', d_packed, w_mix)
        d_norm_one, g_gain_one, g_shift_one = norm_back(d_first, normed_one, inverse_one, gains[:, 0])
        upstream = d_mixed + d_norm_one
        g_qv_rows = jnp.transpose(g_qv.reshape(2, HEADS, HEAD_DIM), (2, 0, 1))
        g_raise_rows = jnp.transpose(g_raise_shift.reshape(FF // HEAD_DIM, HEAD_DIM))
        g_gains = jnp.stack([g_gain_one, g_gain_two], axis=1)
        g_shifts = jnp.stack([g_shift_one, g_shift_two, g_back_shift, g_lower_shift], axis=1)
        results[layer_index] = (g_mix, g_back, g_raise, g_lower, g_qv_rows, g_raise_rows, g_gains, g_shifts)
    stacked = tuple((jnp.stack([results[position][member] for position in range(L)], axis=1) for member in range(8)))
    return (hidden_out, upstream, stacked[0], stacked[1], stacked[2], stacked[3], stacked[4], stacked[5], stacked[6], stacked[7])
```

```python
import itertools
from functools import partial

import jax
import jax.numpy as jnp
import numpy as np
from jax import lax
from jax.experimental import pallas as pl
from jax.experimental.pallas import tpu as pltpu
from jax.sharding import Mesh
from jax.sharding import PartitionSpec as P

AXES = ("ylo", "z", "core", "x", "yhi")
SIZES = (2, 4, 2, 4, 2)
DP = ("ylo", "z", "core")
TENSOR = ("x", "yhi")
ORDERS = ("xyz", "yzx", "zxy")
LAYERS = 2
TOK = 160
D = 1024
HEADS = 16
EPS = 1e-05
BF, F32 = jnp.bfloat16, jnp.float32
HIGH = lax.Precision.HIGHEST


def pairs(axis, step):
    out = []
    for ylo, z, core, x, yhi in itertools.product(*map(range, SIZES)):
        c = {"x": x, "y": 2 * yhi + ylo, "z": z, "core": core}
        if axis == "core":
            c["core"] ^= 1
        else:
            c[axis] ^= 1 if (step == 1) == (core == 0) else 3
        src = np.ravel_multi_index((ylo, z, core, x, yhi), SIZES)
        dst = np.ravel_multi_index((c["y"] & 1, c["z"], c["core"], c["x"], c["y"] >> 1), SIZES)
        out.append((int(src), int(dst)))
    return out


def swap(v, axis, step=0):
    return lax.ppermute(v, AXES, pairs(axis, step))


def gather(parts):
    bufs = list(parts)
    res = [None] * len(parts)
    for n in range(6):
        recv = [swap(b, ORDERS[i][n // 2], n % 2 + 1) for i, b in enumerate(bufs)]
        if n < 5:
            bufs = [jnp.stack([b, r]) for b, r in zip(bufs, recv)]
        else:
            for i in range(len(parts)):
                res[i] = (bufs[i], recv[i], swap(bufs[i], "core"), swap(recv[i], "core"))
    return res


def plus(a, b):
    return (a.astype(F32) + b.astype(F32)).astype(BF)


def scatter_one(grad, order):
    own_lo, own_hi, oth_lo, oth_hi = grad
    hi = plus(own_hi, swap(oth_hi, "core"))
    lo = plus(own_lo, swap(oth_lo, "core"))
    for n in reversed(range(6)):
        r = swap(hi, order[n // 2], n % 2 + 1)
        if n == 0:
            return lo.astype(F32) + r.astype(F32)
        s = plus(lo, r)
        lo, hi = s[0], s[1]


def norm(h):
    center = jnp.mean(h, axis=-1, keepdims=True)
    c = h - center
    var = jnp.mean(c * c, axis=-1, keepdims=True)
    inv = lax.rsqrt(var + EPS)
    return c * inv, inv


def dot(a, b):
    return lax.dot_general(a, b, (((1,), (0,)), ((), ())), preferred_element_type=F32)


def dot_nt(a, b):
    return lax.dot_general(a, b, (((1,), (1,)), ((), ())), preferred_element_type=F32)


def dot_tn(a, b):
    return lax.dot_general(a, b, (((0,), (0,)), ((), ())), preferred_element_type=F32)


def turned(x):
    return jnp.transpose(x.astype(F32)).astype(BF)


BITS = tuple(itertools.product((0, 1), repeat=2))


def placed_at(core, half, y2, y1):
    if y1 == y2:
        return y1
    c = core if half == 0 else 1 - core
    return c if y1 else 1 - c


def each_block(part, step, quad):
    a, b = step // 2, step % 2
    for half in (0, 1):
        lo, hi = quad[2 * half], quad[2 * half + 1]
        for (z2, z1), (y2, y1) in itertools.product(BITS, BITS):
            row = half * 8 + (y1 ^ y2) * 4 + z2 * 2 + z1
            if part == 0:
                yield None, half, y2, y1, row, (lo, hi)[z2], (z1 * 4 + y2 * 2 + y1, 0)
            elif part == 2:
                yield None, half, y2, y1, row, (lo, hi)[y2], (y1, 0, z2 * 2 + z1)
            else:
                which = a if half == 0 else b
                for x2 in (0, 1):
                    yield which == x2, half, y2, y1, row, (lo, hi)[x2], (0, z2 * 2 + z1, y2 * 2 + y1)


def by_condition(part, step, quad, fn):
    if part != 1:
        for _, *rest in each_block(part, step, quad):
            fn(*rest)
        return
    groups = {}
    for cond, half, *rest in each_block(part, step, quad):
        groups.setdefault((half, id(rest[3])), (cond, []))[1].append((half, *rest))
    for cond, items in groups.values():

        @pl.when(cond)
        def _(items=items):
            for it in items:
                fn(*it)


def assemble(part, step, core, quad, w_ref):
    def put(half, y2, y1, row, ref, index):
        w_ref[placed_at(core, half, y2, y1), row * 64 : row * 64 + 64, :] = ref[index]

    by_condition(part, step, quad, put)


def disassemble(part, step, core, quad, w_ref):
    def get(half, y2, y1, row, ref, index):
        ref[index] = w_ref[placed_at(core, half, y2, y1), row * 64 : row * 64 + 64, :]

    by_condition(part, step, quad, get)


def merged(part, quad):
    shape = {0: (8, 4, 64, 512), 1: (2, 4, 4, 64, 512), 2: (2, 4, 4, 64, 512)}[part]
    return tuple(q.reshape(shape) for q in quad)


def unmerged(quad):
    return tuple(q.reshape(2, 2, 2, 2, 2, 64, 512) for q in quad)


def quad_shapes(part):
    shape = {0: (8, 4, 64, 512), 1: (2, 4, 4, 64, 512), 2: (2, 4, 4, 64, 512)}[part]
    return [jax.ShapeDtypeStruct(shape, BF)] * 4


def quad_specs(part):
    def own(s):
        return s

    def oth(s):
        return (s % 2) * 2 + s // 2

    if part == 0:
        return [
            pl.BlockSpec((8, 1, 64, 512), lambda s, *_, f=f: (0, f(s), 0, 0))
            for f in (own, own, oth, oth)
        ]
    if part == 2:
        return [
            pl.BlockSpec((2, 1, 4, 64, 512), lambda s, *_, f=f: (0, f(s), 0, 0, 0))
            for f in (own, own, oth, oth)
        ]
    maps = (
        lambda s: jnp.minimum(s, 1),
        lambda s: jnp.maximum(s - 2, 0),
        lambda s: s // 2,
        lambda s: s // 2,
    )
    return [
        pl.BlockSpec((1, 4, 4, 64, 512), lambda s, *_, f=f: (f(s), 0, 0, 0, 0)) for f in maps
    ]


def whole(shape):
    zeros = (0,) * len(shape)
    return pl.BlockSpec(shape, lambda s, *_: zeros)


def per_step(shape):
    zeros = (0,) * (len(shape) - 1)
    return pl.BlockSpec((1, *shape[1:]), lambda s, *_: (s, *zeros))


def call(body, name, core, slopes, ins, in_specs, outs, out_specs, scratch):
    return pl.pallas_call(
        body,
        name=name,
        out_shape=outs,
        grid_spec=pltpu.PrefetchScalarGridSpec(
            num_scalar_prefetch=2,
            grid=(4,),
            in_specs=in_specs,
            out_specs=out_specs,
            scratch_shapes=scratch,
        ),
        compiler_params=pltpu.CompilerParams(
            dimension_semantics=("arbitrary",), vmem_limit_bytes=48 << 20
        ),
    )(core, slopes, *ins)


def sds(shape, dtype=F32):
    return jax.ShapeDtypeStruct(shape, dtype)


def scores_of(q, k, slope):
    s = dot_nt(q, k) * 0.125
    row = lax.broadcasted_iota(jnp.int32, (TOK, TOK), 0)
    col = lax.broadcasted_iota(jnp.int32, (TOK, TOK), 1)
    s = s + slope * (col - row).astype(F32)
    return jnp.where(col <= row, s, -jnp.inf)


def chance_of(q, k, slope):
    s = scores_of(q, k, slope)
    e = jnp.exp(s - jnp.max(s, axis=-1, keepdims=True))
    return e / jnp.sum(e, axis=-1, keepdims=True)


def attn_fwd_body(core_ref, slope_ref, h_ref, vec_ref, bias_ref, *rest):
    quad, (qkv_ref, ctx_ref, hm_ref), (w_ref, a_ref) = rest[:4], rest[4:7], rest[7:]
    s, core = pl.program_id(0), core_ref[0]

    @pl.when(s == 0)
    def _():
        n, _ = norm(h_ref[...])
        a_ref[...] = (n * vec_ref[0:1, :] + vec_ref[1:2, :]).astype(BF)
        hm_ref[...] = h_ref[...] + vec_ref[4:5, :]

    assemble(0, s, core, quad, w_ref)
    total = jnp.zeros((TOK, D), F32)
    for g in (0, 1):
        qkv = (dot(a_ref[...], w_ref[g, :, 0:384]) + bias_ref[0, g : g + 1, :]).astype(BF)
        qkv_ref[0, g] = qkv
        ctx = []
        for hd in (0, 1):
            q, k, v = (qkv[:, j * 128 + hd * 64 : j * 128 + hd * 64 + 64] for j in range(3))
            p = chance_of(q, k, slope_ref[s * 4 + g * 2 + hd]).astype(BF)
            ctx.append(dot(p, v))
        ctx = jnp.concatenate(ctx, axis=1).astype(BF)
        ctx_ref[0, g] = ctx
        total = total + dot_nt(ctx, w_ref[g, :, 384:512])
    hm_ref[...] += total


def attn_fwd(core, slopes, h, vec, bias, quad):
    return call(
        attn_fwd_body,
        "attn_fwd",
        core,
        slopes,
        (h, vec, bias, *merged(0, quad)),
        [whole((TOK, D)), whole((8, D)), per_step((4, 2, 384))] + quad_specs(0),
        [sds((4, 2, TOK, 384), BF), sds((4, 2, TOK, 128), BF), sds((TOK, D))],
        [per_step((4, 2, TOK, 384)), per_step((4, 2, TOK, 128)), whole((TOK, D))],
        [pltpu.VMEM((2, D, 512), BF), pltpu.VMEM((TOK, D), BF)],
    )


C0, C1 = 0.7978845608, 0.044715


def gelu_parts(u):
    t = jnp.tanh(C0 * (u + C1 * (u * u * u)))
    return 0.5 * u * (1.0 + t), t


def feed_fwd_body(core_ref, slope_ref, hm_ref, vec_ref, bias_ref, *rest):
    up, down, (u_ref, out_ref), (wu_ref, wd_ref, m_ref) = rest[:4], rest[4:8], rest[8:10], rest[10:]
    s, core = pl.program_id(0), core_ref[0]

    @pl.when(s == 0)
    def _():
        n, _ = norm(hm_ref[...])
        m_ref[...] = (n * vec_ref[2:3, :] + vec_ref[3:4, :]).astype(BF)
        out_ref[...] = hm_ref[...] + vec_ref[5:6, :]

    assemble(1, s, core, up, wu_ref)
    assemble(2, s, core, down, wd_ref)
    total = jnp.zeros((TOK, D), F32)
    for g in (0, 1):
        u = dot(m_ref[...], wu_ref[g]) + bias_ref[0, g : g + 1, :]
        u_ref[0, g] = u
        act, _ = gelu_parts(u)
        total = total + dot_nt(act.astype(BF), wd_ref[g])
    out_ref[...] += total


def feed_fwd(core, slopes, hm, vec, bias, up, down):
    return call(
        feed_fwd_body,
        "feed_fwd",
        core,
        slopes,
        (hm, vec, bias, *merged(1, up), *merged(2, down)),
        [whole((TOK, D)), whole((8, D)), per_step((4, 2, 512))] + quad_specs(1) + quad_specs(2),
        [sds((4, 2, TOK, 512)), sds((TOK, D))],
        [per_step((4, 2, TOK, 512)), whole((TOK, D))],
        [pltpu.VMEM((2, D, 512), BF), pltpu.VMEM((2, D, 512), BF), pltpu.VMEM((TOK, D), BF)],
    )


def norm_back(up, n, inv, gain):
    scaled = up * gain
    center = jnp.mean(scaled, axis=-1, keepdims=True)
    spread = jnp.mean(scaled * n, axis=-1, keepdims=True)
    return inv * (scaled - center - n * spread)


def col_sum(x):
    return jnp.sum(x, axis=0, keepdims=True)


def feed_bwd_body(core_ref, slope_ref, dh_ref, hm_ref, vec_ref, u_ref, *rest):
    up, down = rest[:4], rest[4:8]
    gup, gdown, (dhm_ref, gbu_ref, gvec_ref) = rest[8:12], rest[12:16], rest[16:19]
    wu_ref, wd_ref, gu_ref, gd_ref, mt_ref, dyt_ref, dm_ref = rest[19:]
    s, core = pl.program_id(0), core_ref[0]

    @pl.when(s == 0)
    def _():
        n, _ = norm(hm_ref[...])
        mt_ref[...] = turned((n * vec_ref[2:3, :] + vec_ref[3:4, :]).astype(BF))
        dyt_ref[...] = turned(dh_ref[...].astype(BF))
        dm_ref[...] = jnp.zeros((TOK, D), F32)

    assemble(1, s, core, up, wu_ref)
    assemble(2, s, core, down, wd_ref)
    dy = dh_ref[...].astype(BF)
    total = jnp.zeros((TOK, D), F32)
    for g in (0, 1):
        u = u_ref[0, g]
        act, t = gelu_parts(u)
        slope = 0.5 * (1.0 + t) + (0.5 * C0) * u * (1.0 - t * t) * (1.0 + (3.0 * C1) * (u * u))
        du = dot(dy, wd_ref[g]) * slope
        gbu_ref[0, g : g + 1, :] = col_sum(du)
        dub = du.astype(BF)
        gd_ref[g] = dot(dyt_ref[...], act.astype(BF)).astype(BF)
        gu_ref[g] = dot(mt_ref[...], dub).astype(BF)
        total = total + dot_nt(dub, wu_ref[g])
    dm_ref[...] += total
    disassemble(1, s, core, gup, gu_ref)
    disassemble(2, s, core, gdown, gd_ref)

    @pl.when(s == 3)
    def _():
        n, inv = norm(hm_ref[...])
        dm, dh = dm_ref[...], dh_ref[...]
        dhm_ref[...] = dh + norm_back(dm, n, inv, vec_ref[2:3, :])
        gvec_ref[...] = jnp.zeros((8, D), F32)
        gvec_ref[0:1, :] = col_sum(dm * n)
        gvec_ref[1:2, :] = col_sum(dm)
        gvec_ref[2:3, :] = col_sum(dh)


def feed_bwd(core, slopes, dh, hm, vec, u, up, down):
    wide = pltpu.VMEM((2, D, 512), BF)
    return call(
        feed_bwd_body,
        "feed_bwd",
        core,
        slopes,
        (dh, hm, vec, u, *merged(1, up), *merged(2, down)),
        [whole((TOK, D)), whole((TOK, D)), whole((8, D)), per_step((4, 2, TOK, 512))]
        + quad_specs(1)
        + quad_specs(2),
        quad_shapes(1) + quad_shapes(2) + [sds((TOK, D)), sds((4, 2, 512)), sds((8, D))],
        quad_specs(1) + quad_specs(2) + [whole((TOK, D)), per_step((4, 2, 512)), whole((8, D))],
        [wide] * 4
        + [pltpu.VMEM((D, TOK), BF), pltpu.VMEM((D, TOK), BF), pltpu.VMEM((TOK, D), F32)],
    )


def attn_bwd_body(core_ref, slope_ref, dhm_ref, h_ref, vec_ref, qkv_ref, ctx_ref, *rest):
    quad, gquad, (dh_ref, gqv_ref, gvec_ref) = rest[:4], rest[4:8], rest[8:11]
    w_ref, gw_ref, at_ref, dzt_ref, da_ref = rest[11:]
    s, core = pl.program_id(0), core_ref[0]

    @pl.when(s == 0)
    def _():
        n, _ = norm(h_ref[...])
        at_ref[...] = turned((n * vec_ref[0:1, :] + vec_ref[1:2, :]).astype(BF))
        dzt_ref[...] = turned(dhm_ref[...].astype(BF))
        da_ref[...] = jnp.zeros((TOK, D), F32)

    assemble(0, s, core, quad, w_ref)
    dz = dhm_ref[...].astype(BF)
    total = jnp.zeros((TOK, D), F32)
    for g in (0, 1):
        qkv = qkv_ref[0, g]
        dctx = dot(dz, w_ref[g, :, 384:512]).astype(BF)
        gw_ref[g, :, 384:512] = dot(dzt_ref[...], ctx_ref[0, g]).astype(BF)
        grads = [[], [], []]
        for hd in (0, 1):
            q, k, v = (qkv[:, j * 128 + hd * 64 : j * 128 + hd * 64 + 64] for j in range(3))
            dc = dctx[:, hd * 64 : hd * 64 + 64]
            p = chance_of(q, k, slope_ref[s * 4 + g * 2 + hd])
            dp = dot_nt(dc, v)
            delta = jnp.sum(p * dp, axis=-1, keepdims=True)
            ds = (p * (dp - delta) * 0.125).astype(BF)
            grads[0].append(dot(ds, k))
            grads[1].append(dot_tn(ds, q))
            grads[2].append(dot_tn(p.astype(BF), dc))
        dqkv = jnp.concatenate([g_ for three in grads for g_ in three], axis=1)
        gqv_ref[0, g : g + 1, :] = col_sum(dqkv)
        dqkv = dqkv.astype(BF)
        gw_ref[g, :, 0:384] = dot(at_ref[...], dqkv).astype(BF)
        total = total + dot_nt(dqkv, w_ref[g, :, 0:384])
    da_ref[...] += total
    disassemble(0, s, core, gquad, gw_ref)

    @pl.when(s == 3)
    def _():
        n, inv = norm(h_ref[...])
        da, dhm = da_ref[...], dhm_ref[...]
        dh_ref[...] = dhm + norm_back(da, n, inv, vec_ref[0:1, :])
        gvec_ref[...] = jnp.zeros((8, D), F32)
        gvec_ref[0:1, :] = col_sum(da * n)
        gvec_ref[1:2, :] = col_sum(da)
        gvec_ref[2:3, :] = col_sum(dhm)


def attn_bwd(core, slopes, dhm, h, vec, qkv, ctx, quad):
    wide = pltpu.VMEM((2, D, 512), BF)
    return call(
        attn_bwd_body,
        "attn_bwd",
        core,
        slopes,
        (dhm, h, vec, qkv, ctx, *merged(0, quad)),
        [
            whole((TOK, D)),
            whole((TOK, D)),
            whole((8, D)),
            per_step((4, 2, TOK, 384)),
            per_step((4, 2, TOK, 128)),
        ]
        + quad_specs(0),
        quad_shapes(0) + [sds((TOK, D)), sds((4, 2, 384)), sds((8, D))],
        quad_specs(0) + [whole((TOK, D)), per_step((4, 2, 384)), whole((8, D))],
        [wide] * 2
        + [pltpu.VMEM((D, TOK), BF), pltpu.VMEM((D, TOK), BF), pltpu.VMEM((TOK, D), F32)],
    )


def orders():
    at = {a: lax.axis_index(a) for a in AXES}
    rows = []
    for half, low, z2, z1 in itertools.product((0, 1), repeat=4):
        core = at["core"] ^ half
        z = at["z"] ^ jnp.where(core == 0, z1 ^ (3 * z2), (3 * z1) ^ z2)
        rows.append(((at["ylo"] ^ low) * 4 + z) * 2 + core)
    cols = []
    for x2, x1, g in itertools.product((0, 1), repeat=3):
        x = at["x"] ^ jnp.where(at["core"] == 0, x1 ^ (3 * x2), (3 * x1) ^ x2)
        cols.append(x * 2 + (at["yhi"] ^ g))
    return at, jnp.stack(rows), jnp.stack(cols)


def one_hot(index, count):
    return (index[:, None] == jnp.arange(count)[None, :]).astype(F32)


def shards(
    hidden_in, w_qkv, w_attn_out, w_up, w_down, qv_bias, up_bias, ln_gain, row_bias, cotangent
):
    at, rows, cols = orders()
    core = at["core"].reshape(1).astype(jnp.int32)
    row_hot, col_hot = one_hot(rows, 16), one_hot(cols, 8)
    lanes = (rows[:, None] * 64 + jnp.arange(64)[None, :]).reshape(-1)
    lane_hot = one_hot(lanes, D)

    def to_own(v):
        return lax.dot_general(v, lane_hot, (((1,), (1,)), ((), ())), precision=HIGH)

    def from_own(v):
        return jnp.dot(v, lane_hot, precision=HIGH)

    heads = cols[:, None] * 2 + jnp.arange(2)[None, :]
    slopes = jnp.exp2(-8.0 * (heads.astype(F32) + 1.0) / HEADS).reshape(-1)

    small = jnp.concatenate([v.reshape(-1) for v in (ln_gain, row_bias, qv_bias, up_bias)])
    small = jnp.pad(small, (0, 1024 - small.size)).reshape(8, 128)
    small = lax.all_gather(small, AXES, axis=0, tiled=False).reshape(16, 8, 1024).astype(F32)
    wide = small[:, 0, :768]
    gains = wide[:, :256].reshape(D, LAYERS, 2)
    shifts = wide[:, 256:].reshape(D, LAYERS, 4)
    qv = small[:, :, 768:800].reshape(16, 8, 4, LAYERS, 2, 2)
    qv = qv.transpose(3, 1, 4, 5, 0, 2).reshape(LAYERS, 8, 2, 128)
    ub = small[:, :, 800:864].reshape(16, 8, 4, LAYERS, 8)
    ub = ub.transpose(3, 1, 4, 0, 2).reshape(LAYERS, 8, 512)

    weights = []
    for l in range(LAYERS):
        part0 = jnp.concatenate([w_qkv[:, l].reshape(64, 384), w_attn_out[:, l]], axis=1)
        weights.append(gather([part0, w_up[:, l], w_down[:, l]]))

    h = to_own(hidden_in)
    dh = to_own(cotangent)
    kept = []
    for l in range(LAYERS):
        vec = jnp.stack([gains[:, l, 0], shifts[:, l, 0], gains[:, l, 1], shifts[:, l, 1]]
                        + [shifts[:, l, 2], shifts[:, l, 3]])
        vec = jnp.pad(to_own(vec), ((0, 2), (0, 0)))
        qv_own = jnp.einsum("st,tjk->sjk", col_hot, qv[l], precision=HIGH)
        bias = jnp.concatenate(
            [qv_own[:, 0], jnp.zeros((8, 128), F32), qv_own[:, 1]], axis=1
        ).reshape(4, 2, 384)
        up_own = jnp.dot(col_hot, ub[l], precision=HIGH).reshape(4, 2, 512)
        mix, up, down = weights[l]
        qkv, ctx, hm = attn_fwd(core, slopes, h, vec, bias, mix)
        u, out = feed_fwd(core, slopes, hm, vec, up_own, up, down)
        kept.append((h, vec, qkv, ctx, hm, u))
        h = out
    hidden_out = from_own(h)

    shares, small_grads = [None] * LAYERS, [None] * LAYERS
    for l in reversed(range(LAYERS)):
        h, vec, qkv, ctx, hm, u = kept[l]
        mix, up, down = weights[l]
        outs = feed_bwd(core, slopes, dh, hm, vec, u, up, down)
        gup, gdown, (dhm, gbu, gvec2) = unmerged(outs[:4]), unmerged(outs[4:8]), outs[8:]
        outs = attn_bwd(core, slopes, dhm, h, vec, qkv, ctx, mix)
        gmix, (dh, gqv, gvec1) = unmerged(outs[:4]), outs[4:]
        shares[l] = [
            scatter_one(g, o) for g, o in zip((gmix, gup, gdown), ORDERS)
        ]
        vectors = jnp.stack([gvec1[0], gvec2[0], gvec1[1], gvec2[1], gvec1[2], gvec2[2]])
        columns = jnp.concatenate([gqv.reshape(8, 384), gbu.reshape(8, 512)], axis=1)
        columns = lax.dot_general(
            col_hot, columns, (((0,), (0,)), ((), ())), precision=HIGH
        )
        small_grads[l] = jnp.concatenate([from_own(vectors).reshape(-1), columns.reshape(-1)])
    grad_in = from_own(dh)

    total = lax.psum(jnp.stack(small_grads), AXES)
    p = (at["ylo"] * 4 + at["z"]) * 2 + at["core"]
    t = at["x"] * 2 + at["yhi"]
    vectors = total[:, : 6 * D].reshape(LAYERS, 6, 16, 64)
    vectors = lax.dynamic_index_in_dim(vectors, p, 2, keepdims=False)
    vectors = vectors.transpose(2, 0, 1)
    columns = total[:, 6 * D :].reshape(LAYERS, 8, 896)
    columns = lax.dynamic_index_in_dim(columns, t, 1, keepdims=False)
    gqv = columns[:, :384].reshape(LAYERS, 3, 2, 16, 4)[:, 0::2]
    gqv = lax.dynamic_index_in_dim(gqv, p, 3, keepdims=False).transpose(3, 0, 1, 2)
    gbu = columns[:, 384:].reshape(LAYERS, 8, 16, 4)
    gbu = lax.dynamic_index_in_dim(gbu, p, 2, keepdims=False).transpose(2, 0, 1)

    mixes = jnp.stack([shares[l][0] for l in range(LAYERS)], axis=1)
    return (
        hidden_out,
        grad_in,
        mixes[:, :, :384].reshape(64, LAYERS, 3, 128),
        mixes[:, :, 384:],
        jnp.stack([shares[l][1] for l in range(LAYERS)], axis=1),
        jnp.stack([shares[l][2] for l in range(LAYERS)], axis=1),
        gqv,
        gbu,
        vectors[:, :, :2],
        vectors[:, :, 2:],
    )


def solution(mesh):
    torus = Mesh(mesh.devices.reshape(SIZES), AXES)
    token = P((*DP, *TENSOR), None)
    placed = (
        token,
        P(DP, None, None, TENSOR),
        P(DP, None, TENSOR),
        P(DP, None, TENSOR),
        P(DP, None, TENSOR),
        P(DP, None, None, TENSOR),
        P(DP, None, TENSOR),
        P(DP, None, None),
        P(DP, None, None),
        token,
    )
    outs = (token, token, *placed[1:9])
    return jax.shard_map(shards, mesh=torus, in_specs=placed, out_specs=outs, check_vma=False)
```

```python
import itertools
from functools import partial

import jax
import jax.numpy as jnp
import numpy as np
from jax import lax
from jax.experimental import pallas as pl
from jax.experimental.pallas import tpu as pltpu
from jax.sharding import Mesh
from jax.sharding import PartitionSpec as P

AXES = ("ylo", "z", "core", "x", "yhi")
SIZES = (2, 4, 2, 4, 2)
DP = ("ylo", "z", "core")
TENSOR = ("x", "yhi")
ORDERS = ("xyz", "yzx", "zxy")
LAYERS = 2
TOK = 160
D = 1024
HEADS = 16
EPS = 1e-05
BF, F32 = jnp.bfloat16, jnp.float32
HIGH = lax.Precision.HIGHEST


def pairs(axis, step):
    out = []
    for ylo, z, core, x, yhi in itertools.product(*map(range, SIZES)):
        c = {"x": x, "y": 2 * yhi + ylo, "z": z, "core": core}
        if axis == "core":
            c["core"] ^= 1
        else:
            c[axis] ^= 1 if (step == 1) == (core == 0) else 3
        src = np.ravel_multi_index((ylo, z, core, x, yhi), SIZES)
        dst = np.ravel_multi_index((c["y"] & 1, c["z"], c["core"], c["x"], c["y"] >> 1), SIZES)
        out.append((int(src), int(dst)))
    return out


def swap(v, axis, step=0):
    return lax.ppermute(v, AXES, pairs(axis, step))


def plain_pairs(axis, flip):
    out = []
    for ylo, z, core, x, yhi in itertools.product(*map(range, SIZES)):
        c = {"x": x, "y": 2 * yhi + ylo, "z": z, "core": core}
        c[axis] ^= flip
        src = np.ravel_multi_index((ylo, z, core, x, yhi), SIZES)
        dst = np.ravel_multi_index((c["y"] & 1, c["z"], c["core"], c["x"], c["y"] >> 1), SIZES)
        out.append((int(src), int(dst)))
    return out


def plain_swap(v, axis, flip):
    return lax.ppermute(v, AXES, plain_pairs(axis, flip))


COMMON = 3


def joined(*values):
    return lax.optimization_barrier(values)


def exchange(bufs, n):
    return [swap(b, ORDERS[i][n // 2], n % 2 + 1) for i, b in enumerate(bufs)]


def doubled(bufs, recv):
    return [jnp.stack([b, r]) for b, r in zip(bufs, recv)]


def over_cores(values):
    return [swap(v, "core") for v in values]


def small_step(n, rows, cols):
    def both(r, c, fn):
        flat = jnp.concatenate([r.reshape(96, 128), c.reshape(-1, 128)])
        got = fn(flat)
        return got[:96].reshape(12, 1024), got[96:].reshape(c.shape)

    if n < 3:
        axis, flip = (("z", 1), ("z", 2), ("y", 1))[n]
        r, c = both(rows, cols, lambda v: plain_swap(v, axis, flip))
        return rows + r, cols + c
    if n == 3:
        return rows, jnp.stack([cols, plain_swap(cols, "y", 2)])
    if n < 6:
        return rows, jnp.stack([cols, swap(cols, "x", n - 3)])
    r, c = both(rows, cols, lambda v: swap(v, "core"))
    return rows + r, cols + c.swapaxes(0, 1)


def sum_small(rows, cols):
    def both(r, c, fn):
        rr, cc = r.reshape(-1, 128), c.reshape(-1, 128)
        got = fn(jnp.concatenate([rr, cc]))
        return got[: rr.shape[0]].reshape(r.shape), got[rr.shape[0] :].reshape(c.shape)

    n = cols.shape[-1]
    rows = rows.reshape(12, 2, 512)
    r, c = both(rows[:, 1], cols, lambda v: swap(v, "core"))
    rows, cols = rows[:, 0] + r, cols + c.swapaxes(0, 1)
    for step in (2, 1):
        r, c = both(rows, cols[1], lambda v: swap(v, "x", step))
        rows, cols = rows + r, cols[0] + c
    r, c = both(rows, cols[1], lambda v: plain_swap(v, "y", 2))
    rows, cols = rows + r, cols[0] + c
    rows = rows.reshape(12, 2, 256)
    r, c = both(rows[:, 1], cols, lambda v: plain_swap(v, "y", 1))
    rows, cols = rows[:, 0] + r, cols + c
    for step in (2, 1):
        rows = rows.reshape(12, 2, -1)
        away = rows[:, 1]
        width = away.shape[-1]
        away = jnp.pad(away, ((0, 0), (0, 128 - width)))
        r, c = both(away, cols, lambda v: swap(v, "z", step))
        rows, cols = rows[:, 0] + r[:, :width], cols + c
    return rows, cols


def plus(a, b):
    return (a.astype(F32) + b.astype(F32)).astype(BF)


def halved(lo, hi, order, n):
    s = plus(lo, swap(hi, order[n // 2], n % 2 + 1))
    return s[0], s[1]


def scatter_both(sums, order):
    s = jnp.stack(sums, axis=3)
    for n in reversed(range(COMMON)):
        lo, hi = s[0], s[1]
        r = swap(hi, order[n // 2], n % 2 + 1)
        if n:
            s = plus(lo, r)
        else:
            return jnp.swapaxes(lo.astype(F32) + r.astype(F32), 0, 1)


def norm(h):
    center = jnp.mean(h, axis=-1, keepdims=True)
    c = h - center
    var = jnp.mean(c * c, axis=-1, keepdims=True)
    inv = lax.rsqrt(var + EPS)
    return c * inv, inv


def dot(a, b):
    return lax.dot_general(a, b, (((1,), (0,)), ((), ())), preferred_element_type=F32)


def dot_nt(a, b):
    return lax.dot_general(a, b, (((1,), (1,)), ((), ())), preferred_element_type=F32)


def dot_tn(a, b):
    return lax.dot_general(a, b, (((0,), (0,)), ((), ())), preferred_element_type=F32)


def turned(x):
    return jnp.transpose(x.astype(F32)).astype(BF)


BITS = tuple(itertools.product((0, 1), repeat=2))


def placed_at(core, half, y2, y1):
    if y1 == y2:
        return y1
    c = core if half == 0 else 1 - core
    return c if y1 else 1 - c


def each_block(part, step, quad):
    a, b = step // 2, step % 2
    for half in (0, 1):
        lo, hi = quad[2 * half], quad[2 * half + 1]
        for (z2, z1), (y2, y1) in itertools.product(BITS, BITS):
            row = half * 8 + (y1 ^ y2) * 4 + z2 * 2 + z1
            if part == 0:
                yield None, half, y2, y1, row, (lo, hi)[z2], (z1 * 4 + y2 * 2 + y1, 0)
            elif part == 2:
                yield None, half, y2, y1, row, (lo, hi)[y2], (y1, 0, z2 * 2 + z1)
            else:
                which = a if half == 0 else b
                for x2 in (0, 1):
                    yield which == x2, half, y2, y1, row, (lo, hi)[x2], (0, z2 * 2 + z1, y2 * 2 + y1)


def by_condition(part, step, quad, fn):
    if part != 1:
        for _, *rest in each_block(part, step, quad):
            fn(*rest)
        return
    groups = {}
    for cond, half, *rest in each_block(part, step, quad):
        groups.setdefault((half, id(rest[3])), (cond, []))[1].append((half, *rest))
    for cond, items in groups.values():

        @pl.when(cond)
        def _(items=items):
            for it in items:
                fn(*it)


def assemble(part, step, core, quad, w_ref):
    def put(half, y2, y1, row, ref, index):
        w_ref[placed_at(core, half, y2, y1), row * 64 : row * 64 + 64, :] = ref[index]

    by_condition(part, step, quad, put)


def disassemble(part, step, core, quad, w_ref):
    def get(half, y2, y1, row, ref, index):
        ref[index] = w_ref[placed_at(core, half, y2, y1), row * 64 : row * 64 + 64, :]

    by_condition(part, step, quad, get)


def merged(part, quad):
    shape = {0: (8, 4, 64, 512), 1: (2, 4, 4, 64, 512), 2: (2, 4, 4, 64, 512)}[part]
    return tuple(q.reshape(shape) for q in quad)


def unmerged(quad):
    return tuple(q.reshape(2, 2, 2, 2, 2, 64, 512) for q in quad)


def quad_shapes(part):
    shape = {0: (8, 4, 64, 512), 1: (2, 4, 4, 64, 512), 2: (2, 4, 4, 64, 512)}[part]
    return [jax.ShapeDtypeStruct(shape, BF)] * 4


def quad_specs(part):
    def own(s):
        return s

    def oth(s):
        return (s % 2) * 2 + s // 2

    if part == 0:
        return [
            pl.BlockSpec((8, 1, 64, 512), lambda s, *_, f=f: (0, f(s), 0, 0))
            for f in (own, own, oth, oth)
        ]
    if part == 2:
        return [
            pl.BlockSpec((2, 1, 4, 64, 512), lambda s, *_, f=f: (0, f(s), 0, 0, 0))
            for f in (own, own, oth, oth)
        ]
    maps = (
        lambda s: jnp.minimum(s, 1),
        lambda s: jnp.maximum(s - 2, 0),
        lambda s: s // 2,
        lambda s: s // 2,
    )
    return [
        pl.BlockSpec((1, 4, 4, 64, 512), lambda s, *_, f=f: (f(s), 0, 0, 0, 0)) for f in maps
    ]


def whole(shape):
    zeros = (0,) * len(shape)
    return pl.BlockSpec(shape, lambda s, *_: zeros)


def per_step(shape):
    zeros = (0,) * (len(shape) - 1)
    return pl.BlockSpec((1, *shape[1:]), lambda s, *_: (s, *zeros))


def call(body, name, core, slopes, ins, in_specs, outs, out_specs, scratch):
    return pl.pallas_call(
        body,
        name=name,
        out_shape=outs,
        grid_spec=pltpu.PrefetchScalarGridSpec(
            num_scalar_prefetch=2,
            grid=(4,),
            in_specs=in_specs,
            out_specs=out_specs,
            scratch_shapes=scratch,
        ),
        compiler_params=pltpu.CompilerParams(
            dimension_semantics=("arbitrary",), vmem_limit_bytes=48 << 20
        ),
    )(core, slopes, *ins)


def sds(shape, dtype=F32):
    return jax.ShapeDtypeStruct(shape, dtype)


def scores_of(q, k, slope):
    s = dot_nt(q, k) * 0.125
    row = lax.broadcasted_iota(jnp.int32, (TOK, TOK), 0)
    col = lax.broadcasted_iota(jnp.int32, (TOK, TOK), 1)
    s = s + slope * (col - row).astype(F32)
    return jnp.where(col <= row, s, -jnp.inf)


def chance_of(q, k, slope):
    s = scores_of(q, k, slope)
    e = jnp.exp(s - jnp.max(s, axis=-1, keepdims=True))
    return e / jnp.sum(e, axis=-1, keepdims=True)


def attn_fwd_body(core_ref, slope_ref, h_ref, vec_ref, bias_ref, *rest):
    quad, (qkv_ref, ctx_ref, hm_ref), (w_ref, a_ref) = rest[:4], rest[4:7], rest[7:]
    s, core = pl.program_id(0), core_ref[0]

    @pl.when(s == 0)
    def _():
        n, _ = norm(h_ref[...])
        a_ref[...] = (n * vec_ref[0:1, :] + vec_ref[1:2, :]).astype(BF)
        hm_ref[...] = h_ref[...] + vec_ref[4:5, :]

    assemble(0, s, core, quad, w_ref)
    total = jnp.zeros((TOK, D), F32)
    for g in (0, 1):
        qkv = (dot(a_ref[...], w_ref[g, :, 0:384]) + bias_ref[0, g : g + 1, :]).astype(BF)
        qkv_ref[0, g] = qkv
        ctx = []
        for hd in (0, 1):
            q, k, v = (qkv[:, j * 128 + hd * 64 : j * 128 + hd * 64 + 64] for j in range(3))
            p = chance_of(q, k, slope_ref[s * 4 + g * 2 + hd]).astype(BF)
            ctx.append(dot(p, v))
        ctx = jnp.concatenate(ctx, axis=1).astype(BF)
        ctx_ref[0, g] = ctx
        total = total + dot_nt(ctx, w_ref[g, :, 384:512])
    hm_ref[...] += total


def attn_fwd(core, slopes, h, vec, bias, quad):
    return call(
        attn_fwd_body,
        "attn_fwd",
        core,
        slopes,
        (h, vec, bias, *merged(0, quad)),
        [whole((TOK, D)), whole((8, D)), per_step((4, 2, 384))] + quad_specs(0),
        [sds((4, 2, TOK, 384), BF), sds((4, 2, TOK, 128), BF), sds((TOK, D))],
        [per_step((4, 2, TOK, 384)), per_step((4, 2, TOK, 128)), whole((TOK, D))],
        [pltpu.VMEM((2, D, 512), BF), pltpu.VMEM((TOK, D), BF)],
    )


C0, C1 = 0.7978845608, 0.044715


def gelu_parts(u):
    t = jnp.tanh(C0 * (u + C1 * (u * u * u)))
    return 0.5 * u * (1.0 + t), t


def feed_fwd_body(core_ref, slope_ref, hm_ref, vec_ref, bias_ref, *rest):
    up, down, (u_ref, out_ref), (wu_ref, wd_ref, m_ref) = rest[:4], rest[4:8], rest[8:10], rest[10:]
    s, core = pl.program_id(0), core_ref[0]

    @pl.when(s == 0)
    def _():
        n, _ = norm(hm_ref[...])
        m_ref[...] = (n * vec_ref[2:3, :] + vec_ref[3:4, :]).astype(BF)
        out_ref[...] = hm_ref[...] + vec_ref[5:6, :]

    assemble(1, s, core, up, wu_ref)
    assemble(2, s, core, down, wd_ref)
    total = jnp.zeros((TOK, D), F32)
    for g in (0, 1):
        u = dot(m_ref[...], wu_ref[g]) + bias_ref[0, g : g + 1, :]
        u_ref[0, g] = u
        act, _ = gelu_parts(u)
        total = total + dot_nt(act.astype(BF), wd_ref[g])
    out_ref[...] += total


def feed_fwd(core, slopes, hm, vec, bias, up, down):
    return call(
        feed_fwd_body,
        "feed_fwd",
        core,
        slopes,
        (hm, vec, bias, *merged(1, up), *merged(2, down)),
        [whole((TOK, D)), whole((8, D)), per_step((4, 2, 512))] + quad_specs(1) + quad_specs(2),
        [sds((4, 2, TOK, 512)), sds((TOK, D))],
        [per_step((4, 2, TOK, 512)), whole((TOK, D))],
        [pltpu.VMEM((2, D, 512), BF), pltpu.VMEM((2, D, 512), BF), pltpu.VMEM((TOK, D), BF)],
    )


def norm_back(up, n, inv, gain):
    scaled = up * gain
    center = jnp.mean(scaled, axis=-1, keepdims=True)
    spread = jnp.mean(scaled * n, axis=-1, keepdims=True)
    return inv * (scaled - center - n * spread)


def col_sum(x):
    return jnp.sum(x, axis=0, keepdims=True)


def feed_bwd_body(core_ref, slope_ref, dh_ref, hm_ref, vec_ref, u_ref, *rest):
    up, down = rest[:4], rest[4:8]
    gup, gdown, (dhm_ref, gbu_ref, gvec_ref) = rest[8:12], rest[12:16], rest[16:19]
    wu_ref, wd_ref, gu_ref, gd_ref, mt_ref, dyt_ref, dm_ref = rest[19:]
    s, core = pl.program_id(0), core_ref[0]

    @pl.when(s == 0)
    def _():
        n, _ = norm(hm_ref[...])
        mt_ref[...] = turned((n * vec_ref[2:3, :] + vec_ref[3:4, :]).astype(BF))
        dyt_ref[...] = turned(dh_ref[...].astype(BF))
        dm_ref[...] = jnp.zeros((TOK, D), F32)

    assemble(1, s, core, up, wu_ref)
    assemble(2, s, core, down, wd_ref)
    dy = dh_ref[...].astype(BF)
    total = jnp.zeros((TOK, D), F32)
    for g in (0, 1):
        u = u_ref[0, g]
        act, t = gelu_parts(u)
        slope = 0.5 * (1.0 + t) + (0.5 * C0) * u * (1.0 - t * t) * (1.0 + (3.0 * C1) * (u * u))
        du = dot(dy, wd_ref[g]) * slope
        gbu_ref[0, g : g + 1, :] = col_sum(du)
        dub = du.astype(BF)
        gd_ref[g] = dot(dyt_ref[...], act.astype(BF)).astype(BF)
        gu_ref[g] = dot(mt_ref[...], dub).astype(BF)
        total = total + dot_nt(dub, wu_ref[g])
    dm_ref[...] += total
    disassemble(1, s, core, gup, gu_ref)
    disassemble(2, s, core, gdown, gd_ref)

    @pl.when(s == 3)
    def _():
        n, inv = norm(hm_ref[...])
        dm, dh = dm_ref[...], dh_ref[...]
        dhm_ref[...] = dh + norm_back(dm, n, inv, vec_ref[2:3, :])
        gvec_ref[...] = jnp.zeros((8, D), F32)
        gvec_ref[0:1, :] = col_sum(dm * n)
        gvec_ref[1:2, :] = col_sum(dm)
        gvec_ref[2:3, :] = col_sum(dh)


def feed_bwd(core, slopes, dh, hm, vec, u, up, down):
    wide = pltpu.VMEM((2, D, 512), BF)
    return call(
        feed_bwd_body,
        "feed_bwd",
        core,
        slopes,
        (dh, hm, vec, u, *merged(1, up), *merged(2, down)),
        [whole((TOK, D)), whole((TOK, D)), whole((8, D)), per_step((4, 2, TOK, 512))]
        + quad_specs(1)
        + quad_specs(2),
        quad_shapes(1) + quad_shapes(2) + [sds((TOK, D)), sds((4, 2, 512)), sds((8, D))],
        quad_specs(1) + quad_specs(2) + [whole((TOK, D)), per_step((4, 2, 512)), whole((8, D))],
        [wide] * 4
        + [pltpu.VMEM((D, TOK), BF), pltpu.VMEM((D, TOK), BF), pltpu.VMEM((TOK, D), F32)],
    )


def attn_bwd_body(core_ref, slope_ref, dhm_ref, h_ref, vec_ref, qkv_ref, ctx_ref, *rest):
    quad, gquad, (dh_ref, gqv_ref, gvec_ref) = rest[:4], rest[4:8], rest[8:11]
    w_ref, gw_ref, at_ref, dzt_ref, da_ref = rest[11:]
    s, core = pl.program_id(0), core_ref[0]

    @pl.when(s == 0)
    def _():
        n, _ = norm(h_ref[...])
        at_ref[...] = turned((n * vec_ref[0:1, :] + vec_ref[1:2, :]).astype(BF))
        dzt_ref[...] = turned(dhm_ref[...].astype(BF))
        da_ref[...] = jnp.zeros((TOK, D), F32)

    assemble(0, s, core, quad, w_ref)
    dz = dhm_ref[...].astype(BF)
    total = jnp.zeros((TOK, D), F32)
    for g in (0, 1):
        qkv = qkv_ref[0, g]
        dctx = dot(dz, w_ref[g, :, 384:512]).astype(BF)
        gw_ref[g, :, 384:512] = dot(dzt_ref[...], ctx_ref[0, g]).astype(BF)
        grads = [[], [], []]
        for hd in (0, 1):
            q, k, v = (qkv[:, j * 128 + hd * 64 : j * 128 + hd * 64 + 64] for j in range(3))
            dc = dctx[:, hd * 64 : hd * 64 + 64]
            p = chance_of(q, k, slope_ref[s * 4 + g * 2 + hd])
            dp = dot_nt(dc, v)
            delta = jnp.sum(p * dp, axis=-1, keepdims=True)
            ds = (p * (dp - delta) * 0.125).astype(BF)
            grads[0].append(dot(ds, k))
            grads[1].append(dot_tn(ds, q))
            grads[2].append(dot_tn(p.astype(BF), dc))
        dqkv = jnp.concatenate([g_ for three in grads for g_ in three], axis=1)
        gqv_ref[0, g : g + 1, :] = col_sum(dqkv)
        dqkv = dqkv.astype(BF)
        gw_ref[g, :, 0:384] = dot(at_ref[...], dqkv).astype(BF)
        total = total + dot_nt(dqkv, w_ref[g, :, 0:384])
    da_ref[...] += total
    disassemble(0, s, core, gquad, gw_ref)

    @pl.when(s == 3)
    def _():
        n, inv = norm(h_ref[...])
        da, dhm = da_ref[...], dhm_ref[...]
        dh_ref[...] = dhm + norm_back(da, n, inv, vec_ref[0:1, :])
        gvec_ref[...] = jnp.zeros((8, D), F32)
        gvec_ref[0:1, :] = col_sum(da * n)
        gvec_ref[1:2, :] = col_sum(da)
        gvec_ref[2:3, :] = col_sum(dhm)


def attn_bwd(core, slopes, dhm, h, vec, qkv, ctx, quad):
    wide = pltpu.VMEM((2, D, 512), BF)
    return call(
        attn_bwd_body,
        "attn_bwd",
        core,
        slopes,
        (dhm, h, vec, qkv, ctx, *merged(0, quad)),
        [
            whole((TOK, D)),
            whole((TOK, D)),
            whole((8, D)),
            per_step((4, 2, TOK, 384)),
            per_step((4, 2, TOK, 128)),
        ]
        + quad_specs(0),
        quad_shapes(0) + [sds((TOK, D)), sds((4, 2, 384)), sds((8, D))],
        quad_specs(0) + [whole((TOK, D)), per_step((4, 2, 384)), whole((8, D))],
        [wide] * 2
        + [pltpu.VMEM((D, TOK), BF), pltpu.VMEM((D, TOK), BF), pltpu.VMEM((TOK, D), F32)],
    )


def orders():
    at = {a: lax.axis_index(a) for a in AXES}
    rows = []
    for half, low, z2, z1 in itertools.product((0, 1), repeat=4):
        core = at["core"] ^ half
        z = at["z"] ^ jnp.where(core == 0, z1 ^ (3 * z2), (3 * z1) ^ z2)
        rows.append(((at["ylo"] ^ low) * 4 + z) * 2 + core)
    cols = []
    for x2, x1, g in itertools.product((0, 1), repeat=3):
        x = at["x"] ^ jnp.where(at["core"] == 0, x1 ^ (3 * x2), (3 * x1) ^ x2)
        cols.append(x * 2 + (at["yhi"] ^ g))
    return at, jnp.stack(rows), jnp.stack(cols)


def one_hot(index, count):
    return (index[:, None] == jnp.arange(count)[None, :]).astype(F32)


def shards(
    hidden_in, w_qkv, w_attn_out, w_up, w_down, qv_bias, up_bias, ln_gain, row_bias, cotangent
):
    at, rows, cols = orders()
    core = at["core"].reshape(1).astype(jnp.int32)
    lanes = (rows[:, None] * 64 + jnp.arange(64)[None, :]).reshape(-1)
    lane_hot = one_hot(lanes, D)

    def to_own(v):
        return lax.dot_general(v, lane_hot, (((1,), (1,)), ((), ())), precision=HIGH)

    def from_own(v):
        return jnp.dot(v, lane_hot, precision=HIGH)

    heads = cols[:, None] * 2 + jnp.arange(2)[None, :]
    slopes = jnp.exp2(-8.0 * (heads.astype(F32) + 1.0) / HEADS).reshape(-1)

    p = (at["ylo"] * 4 + at["z"]) * 2 + at["core"]
    put_row = (jnp.arange(D)[None, :] == p * 64 + jnp.arange(64)[:, None]).astype(BF)
    put_col = (jnp.arange(64)[None, :] == p * 4 + jnp.arange(4)[:, None]).astype(BF)
    own_rows = jnp.concatenate([ln_gain.reshape(64, 4), row_bias.reshape(64, 8)], axis=1)
    own_cols = jnp.concatenate([qv_bias.reshape(4, 2, 4), up_bias], axis=2).reshape(4, 24)
    small = (dot_tn(own_rows, put_row).astype(BF), dot_tn(own_cols, put_col).astype(BF))
    h, dh = to_own(hidden_in), to_own(cotangent)
    bufs = joined(
        jnp.concatenate([w_qkv.reshape(64, LAYERS, 384), w_attn_out], axis=2).swapaxes(0, 1),
        w_up.swapaxes(0, 1),
        w_down.swapaxes(0, 1),
    )
    for n in range(COMMON):
        recv, small = joined(exchange(bufs, n), small_step(n, *small))
        bufs = doubled(bufs, recv)
    first, second = ([b[..., l, :, :] for b in bufs] for l in range(LAYERS))

    for n in (3, 4):
        recv, small = joined(exchange(first, n), small_step(n, *small))
        first = doubled(first, recv)
    first_hi, first_oth, small = joined(
        exchange(first, 5), over_cores(first), small_step(6, *small_step(5, *small))
    )
    whole_rows = to_own(small[0].astype(F32))
    gains, shifts = whole_rows[:4].reshape(2, 2, D), whole_rows[4:].reshape(2, 4, D)
    whole_cols = small[1].astype(F32).reshape(4, 2, LAYERS, 12, 64)
    vecs, qkv_shifts, up_shifts = [], [], []
    for l in range(LAYERS):
        vecs.append(
            jnp.concatenate(
                [gains[l, 0:1], shifts[l, 0:1], gains[l, 1:2], shifts[l, 1:4], jnp.zeros((2, D), F32)]
            )
        )
        qv = whole_cols[:, :, l, :4].reshape(4, 2, 2, 128)
        qkv_shifts.append(
            jnp.concatenate([qv[:, :, 0], jnp.zeros((4, 2, 128), F32), qv[:, :, 1]], axis=2)
        )
        up_shifts.append(whole_cols[:, :, l, 4:].reshape(4, 2, 512))


    mix_oth, recv = joined(swap(first_hi[0], "core"), exchange(second, 3))
    second = doubled(second, recv)
    mix0 = (first[0], first_hi[0], first_oth[0], mix_oth)
    (qkv0, ctx0, hm0), rest_oth, recv = joined(
        attn_fwd(core, slopes, h, vecs[0], qkv_shifts[0], mix0),
        over_cores(first_hi[1:]),
        exchange(second, 4),
    )
    second = doubled(second, recv)
    up0, down0 = ((first[i], first_hi[i], first_oth[i], rest_oth[i - 1]) for i in (1, 2))
    (u0, h1), second_hi, second_oth = joined(
        feed_fwd(core, slopes, hm0, vecs[0], up_shifts[0], up0, down0),
        exchange(second, 5),
        over_cores(second),
    )
    h1, mix_oth, second_hi = joined(h1, swap(second_hi[0], "core"), second_hi)
    mix1 = (second[0], second_hi[0], second_oth[0], mix_oth)
    (qkv1, ctx1, hm1), rest_oth = joined(
        attn_fwd(core, slopes, h1, vecs[1], qkv_shifts[1], mix1), over_cores(second_hi[1:])
    )
    up1, down1 = ((second[i], second_hi[i], second_oth[i], rest_oth[i - 1]) for i in (1, 2))
    u1, out = feed_fwd(core, slopes, hm1, vecs[1], up_shifts[1], up1, down1)
    hidden_out = from_own(out)

    def feed_back(dh, hm, l, u, up, down):
        outs = feed_bwd(core, slopes, dh, hm, vecs[l], u, up, down)
        return unmerged(outs[:4]), unmerged(outs[4:8]), outs[8:]

    def attn_back(dhm, h, l, qkv, ctx, mix):
        outs = attn_bwd(core, slopes, dhm, h, vecs[l], qkv, ctx, mix)
        return unmerged(outs[:4]), outs[4:]

    def core_sum(grad, got):
        return plus(grad[0], got[0]), plus(grad[1], got[1])

    mix_order, up_order, down_order = ORDERS
    gup1, gdown1, (dhm1, gbu1, gvec21) = feed_back(dh, hm1, 1, u1, up1, down1)
    (gmix1, (dh, gqv1, gvec11)), up_got, down_got = joined(
        attn_back(dhm1, h1, 1, qkv1, ctx1, mix1), over_cores(gup1[2:]), over_cores(gdown1[2:])
    )
    up_lo, up_hi = core_sum(gup1, up_got)
    down_lo, down_hi = core_sum(gdown1, down_got)
    (gup0, gdown0, (dhm0, gbu0, gvec20)), up1_s, down1_s, mix_got = joined(
        feed_back(dh, hm0, 0, u0, up0, down0),
        halved(up_lo, up_hi, up_order, 5),
        halved(down_lo, down_hi, down_order, 5),
        over_cores(gmix1[2:]),
    )
    mix_lo, mix_hi = core_sum(gmix1, mix_got)
    (gmix0, (dh, gqv0, gvec10)), up1_s, down1_s, mix1_s, up_got, down_got = joined(
        attn_back(dhm0, h, 0, qkv0, ctx0, mix0),
        halved(*up1_s, up_order, 4),
        halved(*down1_s, down_order, 4),
        halved(mix_lo, mix_hi, mix_order, 5),
        over_cores(gup0[2:]),
        over_cores(gdown0[2:]),
    )
    lay1 = [halved(*mix1_s, mix_order, 4), up1_s, down1_s]
    lay1 = [halved(*v, o, 3) for v, o in zip(lay1, ORDERS)]
    lay0 = [
        core_sum(gmix0, over_cores(gmix0[2:])),
        core_sum(gup0, up_got),
        core_sum(gdown0, down_got),
    ]
    lay0 = [halved(*v, o, 5) for v, o in zip(lay0, ORDERS)]
    rows_back = [
        jnp.concatenate([v1[0:1], v2[0:1], v1[1:2], v2[1:2], v1[2:3], v2[2:3]])
        for v1, v2 in ((gvec10, gvec20), (gvec11, gvec21))
    ]
    cols_back = [
        jnp.concatenate([gqv[:, :, :128], gqv[:, :, 256:], gbu], axis=2)
        for gqv, gbu in ((gqv0, gbu0), (gqv1, gbu1))
    ]
    grad_in = from_own(dh)

    rows_back, cols_back, up_s = joined(
        jnp.concatenate(rows_back),
        jnp.concatenate(cols_back, axis=2).reshape(2, 2, 2, LAYERS * 768),
        lay0[1],
    )
    rows, cols = sum_small(rows_back, cols_back)
    lay0 = [lay0[0], up_s, lay0[2]]
    for n in (4, 3):
        lay0 = [halved(*v, o, n) for v, o in zip(lay0, ORDERS)]
    rows = rows.T.reshape(64, LAYERS, 6)
    cols = lax.dot_general(
        put_col.astype(F32), cols.reshape(24, 64), (((1,), (1,)), ((), ())), precision=HIGH
    ).reshape(4, LAYERS, 12)
    mixes, ups, downs = (
        scatter_both([jnp.stack(lay0[i]), jnp.stack(lay1[i])], ORDERS[i]) for i in range(3)
    )
    return (
        hidden_out,
        grad_in,
        mixes[:, :, :384].reshape(64, LAYERS, 3, 128),
        mixes[:, :, 384:],
        ups,
        downs,
        cols[:, :, :4].reshape(4, LAYERS, 2, 2),
        cols[:, :, 4:],
        rows[:, :, :2],
        rows[:, :, 2:],
    )


def solution(mesh):
    torus = Mesh(mesh.devices.reshape(SIZES), AXES)
    token = P((*DP, *TENSOR), None)
    placed = (
        token,
        P(DP, None, None, TENSOR),
        P(DP, None, TENSOR),
        P(DP, None, TENSOR),
        P(DP, None, TENSOR),
        P(DP, None, None, TENSOR),
        P(DP, None, TENSOR),
        P(DP, None, None),
        P(DP, None, None),
        token,
    )
    outs = (token, token, *placed[1:9])
    return jax.shard_map(shards, mesh=torus, in_specs=placed, out_specs=outs, check_vma=False)
```

```python
import itertools
from functools import partial

import jax
import jax.numpy as jnp
import numpy as np
from jax import lax
from jax.experimental import pallas as pl
from jax.experimental.pallas import tpu as pltpu
from jax.sharding import Mesh
from jax.sharding import PartitionSpec as P

AXES = ("ylo", "z", "core", "x", "yhi")
SIZES = (2, 4, 2, 4, 2)
DP = ("ylo", "z", "core")
TENSOR = ("x", "yhi")
ORDERS = ("xyz", "yzx", "zxy")
LAYERS = 2
TOK = 160
D = 1024
HEADS = 16
EPS = 1e-05
BF, F32 = jnp.bfloat16, jnp.float32
HIGH = lax.Precision.HIGHEST


def pairs(axis, step):
    out = []
    for ylo, z, core, x, yhi in itertools.product(*map(range, SIZES)):
        c = {"x": x, "y": 2 * yhi + ylo, "z": z, "core": core}
        if axis == "core":
            c["core"] ^= 1
        else:
            c[axis] ^= 1 if (step == 1) == (core == 0) else 3
        src = np.ravel_multi_index((ylo, z, core, x, yhi), SIZES)
        dst = np.ravel_multi_index((c["y"] & 1, c["z"], c["core"], c["x"], c["y"] >> 1), SIZES)
        out.append((int(src), int(dst)))
    return out


def swap(v, axis, step=0):
    return lax.ppermute(v, AXES, pairs(axis, step))


def plain_pairs(axis, flip):
    out = []
    for ylo, z, core, x, yhi in itertools.product(*map(range, SIZES)):
        c = {"x": x, "y": 2 * yhi + ylo, "z": z, "core": core}
        c[axis] ^= flip
        src = np.ravel_multi_index((ylo, z, core, x, yhi), SIZES)
        dst = np.ravel_multi_index((c["y"] & 1, c["z"], c["core"], c["x"], c["y"] >> 1), SIZES)
        out.append((int(src), int(dst)))
    return out


def plain_swap(v, axis, flip):
    return lax.ppermute(v, AXES, plain_pairs(axis, flip))


COMMON = 3


def joined(*values):
    return lax.optimization_barrier(values)


def exchange(bufs, n):
    return [swap(b, ORDERS[i][n // 2], n % 2 + 1) for i, b in enumerate(bufs)]


def doubled(bufs, recv):
    return [lax.optimization_barrier(jnp.stack([b, r])) for b, r in zip(bufs, recv)]


def over_cores(values):
    return [swap(v, "core") for v in values]


def over_cores_in_turn(values):
    one, two = over_cores(values[:2])
    one, last = joined(one, values[2])
    return [one, two, swap(last, "core")]


def small_step(n, rows, cols):
    def both(r, c, fn):
        flat = jnp.concatenate([r.reshape(96, 128), c.reshape(-1, 128)])
        got = fn(flat)
        return got[:96].reshape(12, 1024), got[96:].reshape(c.shape)

    if n < 3:
        axis, flip = (("z", 1), ("z", 2), ("y", 1))[n]
        r, c = both(rows, cols, lambda v: plain_swap(v, axis, flip))
        return rows + r, cols + c
    if n == 3:
        return rows, jnp.stack([cols, plain_swap(cols, "y", 2)])
    if n < 6:
        return rows, jnp.stack([cols, swap(cols, "x", n - 3)])
    r, c = both(rows, cols, lambda v: swap(v, "core"))
    return rows + r, cols + c.swapaxes(0, 1)


def sum_small_step(n, rows, cols):
    def both(r, c, fn):
        rr, cc = r.reshape(-1, 128), c.reshape(-1, 128)
        got = fn(jnp.concatenate([rr, cc]))
        return got[: rr.shape[0]].reshape(r.shape), got[rr.shape[0] :].reshape(c.shape)

    if n == 0:
        rows = rows.reshape(12, 2, 512)
        r, c = both(rows[:, 1], cols, lambda v: swap(v, "core"))
        return rows[:, 0] + r, cols + c.swapaxes(0, 1)
    if n < 3:
        step = 3 - n
        rows = rows.reshape(12, 2, 2, -1)
        away = rows[:, :, 1]
        r, c = both(away, cols, lambda v: swap(v, "z", step))
        return (rows[:, :, 0] + r).reshape(12, -1), cols + c
    if n == 3:
        r, c = both(rows, cols[:, :, 1], lambda v: plain_swap(v, "y", 2))
        return rows + r, cols[:, :, 0] + c
    if n == 4:
        rows = rows.reshape(12, 2, 64)
        away = jnp.pad(rows[:, 1], ((0, 0), (0, 64)))
        r, c = both(away, cols, lambda v: plain_swap(v, "y", 1))
        return jnp.pad(rows[:, 0] + r[:, :64], ((0, 0), (0, 64))), cols + c
    r, c = both(rows, cols[1], lambda v: swap(v, "x", 7 - n))
    return rows + r, cols[0] + c


def plus(a, b):
    return (a.astype(F32) + b.astype(F32)).astype(BF)


def halves(lo, recv):
    hi = plus(lo[1], recv[1])
    return plus(lo[0], recv[0]), hi


def norm(h):
    center = jnp.mean(h, axis=-1, keepdims=True)
    c = h - center
    var = jnp.mean(c * c, axis=-1, keepdims=True)
    inv = lax.rsqrt(var + EPS)
    return c * inv, inv


def dot(a, b):
    return lax.dot_general(a, b, (((1,), (0,)), ((), ())), preferred_element_type=F32)


def dot_nt(a, b):
    return lax.dot_general(a, b, (((1,), (1,)), ((), ())), preferred_element_type=F32)


def dot_tn(a, b):
    return lax.dot_general(a, b, (((0,), (0,)), ((), ())), preferred_element_type=F32)


def turned(x):
    return jnp.transpose(x.astype(F32)).astype(BF)


BITS = tuple(itertools.product((0, 1), repeat=2))


def placed_at(core, half, y2, y1):
    if y1 == y2:
        return y1
    c = core if half == 0 else 1 - core
    return c if y1 else 1 - c


def each_block(part, step, quad):
    a, b = step // 2, step % 2
    for half in (0, 1):
        lo, hi = quad[2 * half], quad[2 * half + 1]
        for (z2, z1), (y2, y1) in itertools.product(BITS, BITS):
            row = half * 8 + (y1 ^ y2) * 4 + z2 * 2 + z1
            if part == 0:
                yield None, half, y2, y1, row, (lo, hi)[z2], (z1 * 4 + y2 * 2 + y1, 0)
            elif part == 2:
                yield None, half, y2, y1, row, (lo, hi)[y2], (y1, 0, z2 * 2 + z1)
            else:
                which = a if half == 0 else b
                for x2 in (0, 1):
                    yield which == x2, half, y2, y1, row, (lo, hi)[x2], (0, z2 * 2 + z1, y2 * 2 + y1)


def by_condition(part, step, quad, fn):
    if part != 1:
        for _, *rest in each_block(part, step, quad):
            fn(*rest)
        return
    groups = {}
    for cond, half, *rest in each_block(part, step, quad):
        groups.setdefault((half, id(rest[3])), (cond, []))[1].append((half, *rest))
    for cond, items in groups.values():

        @pl.when(cond)
        def _(items=items):
            for it in items:
                fn(*it)


def assemble(part, step, core, quad, w_ref):
    def put(half, y2, y1, row, ref, index):
        w_ref[placed_at(core, half, y2, y1), row * 64 : row * 64 + 64, :] = ref[index]

    by_condition(part, step, quad, put)


def disassemble(part, step, core, quad, w_ref):
    def get(half, y2, y1, row, ref, index):
        ref[index] = w_ref[placed_at(core, half, y2, y1), row * 64 : row * 64 + 64, :]

    by_condition(part, step, quad, get)


def merged(part, quad):
    shape = {0: (8, 4, 64, 512), 1: (2, 4, 4, 64, 512), 2: (2, 4, 4, 64, 512)}[part]
    return tuple(q.reshape(shape) for q in quad)


def unmerged(quad):
    return tuple(q.reshape(2, 2, 2, 2, 2, 64, 512) for q in quad)


def quad_shapes(part):
    shape = {0: (8, 4, 64, 512), 1: (2, 4, 4, 64, 512), 2: (2, 4, 4, 64, 512)}[part]
    return [jax.ShapeDtypeStruct(shape, BF)] * 4


def quad_specs(part):
    def own(s):
        return s

    def oth(s):
        return (s % 2) * 2 + s // 2

    if part == 0:
        return [
            pl.BlockSpec((8, 1, 64, 512), lambda s, *_, f=f: (0, f(s), 0, 0))
            for f in (own, own, oth, oth)
        ]
    if part == 2:
        return [
            pl.BlockSpec((2, 1, 4, 64, 512), lambda s, *_, f=f: (0, f(s), 0, 0, 0))
            for f in (own, own, oth, oth)
        ]
    maps = (
        lambda s: jnp.minimum(s, 1),
        lambda s: jnp.maximum(s - 2, 0),
        lambda s: s // 2,
        lambda s: s // 2,
    )
    return [
        pl.BlockSpec((1, 4, 4, 64, 512), lambda s, *_, f=f: (f(s), 0, 0, 0, 0)) for f in maps
    ]


def whole(shape):
    zeros = (0,) * len(shape)
    return pl.BlockSpec(shape, lambda s, *_: zeros)


def per_step(shape):
    zeros = (0,) * (len(shape) - 1)
    return pl.BlockSpec((1, *shape[1:]), lambda s, *_: (s, *zeros))


def call(body, name, core, slopes, ins, in_specs, outs, out_specs, scratch):
    return pl.pallas_call(
        body,
        name=name,
        out_shape=outs,
        grid_spec=pltpu.PrefetchScalarGridSpec(
            num_scalar_prefetch=2,
            grid=(4,),
            in_specs=in_specs,
            out_specs=out_specs,
            scratch_shapes=scratch,
        ),
        compiler_params=pltpu.CompilerParams(
            dimension_semantics=("arbitrary",), vmem_limit_bytes=48 << 20
        ),
    )(core, slopes, *ins)


def sds(shape, dtype=F32):
    return jax.ShapeDtypeStruct(shape, dtype)


def scores_of(q, k, slope):
    s = dot_nt(q, k) * 0.125
    row = lax.broadcasted_iota(jnp.int32, (TOK, TOK), 0)
    col = lax.broadcasted_iota(jnp.int32, (TOK, TOK), 1)
    s = s + slope * (col - row).astype(F32)
    return jnp.where(col <= row, s, -jnp.inf)


def chance_of(q, k, slope):
    s = scores_of(q, k, slope)
    e = jnp.exp(s - jnp.max(s, axis=-1, keepdims=True))
    return e / jnp.sum(e, axis=-1, keepdims=True)


def attn_fwd_body(core_ref, slope_ref, h_ref, vec_ref, bias_ref, *rest):
    quad, (qkv_ref, ctx_ref, hm_ref), (w_ref, a_ref) = rest[:4], rest[4:7], rest[7:]
    s, core = pl.program_id(0), core_ref[0]

    @pl.when(s == 0)
    def _():
        n, _ = norm(h_ref[...])
        a_ref[...] = (n * vec_ref[0:1, :] + vec_ref[1:2, :]).astype(BF)
        hm_ref[...] = h_ref[...] + vec_ref[4:5, :]

    assemble(0, s, core, quad, w_ref)
    total = jnp.zeros((TOK, D), F32)
    for g in (0, 1):
        qkv = (dot(a_ref[...], w_ref[g, :, 0:384]) + bias_ref[0, g : g + 1, :]).astype(BF)
        qkv_ref[0, g] = qkv
        ctx = []
        for hd in (0, 1):
            q, k, v = (qkv[:, j * 128 + hd * 64 : j * 128 + hd * 64 + 64] for j in range(3))
            p = chance_of(q, k, slope_ref[s * 4 + g * 2 + hd]).astype(BF)
            ctx.append(dot(p, v))
        ctx = jnp.concatenate(ctx, axis=1).astype(BF)
        ctx_ref[0, g] = ctx
        total = total + dot_nt(ctx, w_ref[g, :, 384:512])
    hm_ref[...] += total


def attn_fwd(core, slopes, h, vec, bias, quad):
    return call(
        attn_fwd_body,
        "attn_fwd",
        core,
        slopes,
        (h, vec, bias, *merged(0, quad)),
        [whole((TOK, D)), whole((8, D)), per_step((4, 2, 384))] + quad_specs(0),
        [sds((4, 2, TOK, 384), BF), sds((4, 2, TOK, 128), BF), sds((TOK, D))],
        [per_step((4, 2, TOK, 384)), per_step((4, 2, TOK, 128)), whole((TOK, D))],
        [pltpu.VMEM((2, D, 512), BF), pltpu.VMEM((TOK, D), BF)],
    )


C0, C1 = 0.7978845608, 0.044715


def gelu_parts(u):
    t = jnp.tanh(C0 * (u + C1 * (u * u * u)))
    return 0.5 * u * (1.0 + t), t


def feed_fwd_body(core_ref, slope_ref, hm_ref, vec_ref, bias_ref, *rest):
    up, down, (u_ref, out_ref), (wu_ref, wd_ref, m_ref) = rest[:4], rest[4:8], rest[8:10], rest[10:]
    s, core = pl.program_id(0), core_ref[0]

    @pl.when(s == 0)
    def _():
        n, _ = norm(hm_ref[...])
        m_ref[...] = (n * vec_ref[2:3, :] + vec_ref[3:4, :]).astype(BF)
        out_ref[...] = hm_ref[...] + vec_ref[5:6, :]

    assemble(1, s, core, up, wu_ref)
    assemble(2, s, core, down, wd_ref)
    total = jnp.zeros((TOK, D), F32)
    for g in (0, 1):
        u = dot(m_ref[...], wu_ref[g]) + bias_ref[0, g : g + 1, :]
        u_ref[0, g] = u
        act, _ = gelu_parts(u)
        total = total + dot_nt(act.astype(BF), wd_ref[g])
    out_ref[...] += total


def feed_fwd(core, slopes, hm, vec, bias, up, down):
    return call(
        feed_fwd_body,
        "feed_fwd",
        core,
        slopes,
        (hm, vec, bias, *merged(1, up), *merged(2, down)),
        [whole((TOK, D)), whole((8, D)), per_step((4, 2, 512))] + quad_specs(1) + quad_specs(2),
        [sds((4, 2, TOK, 512)), sds((TOK, D))],
        [per_step((4, 2, TOK, 512)), whole((TOK, D))],
        [pltpu.VMEM((2, D, 512), BF), pltpu.VMEM((2, D, 512), BF), pltpu.VMEM((TOK, D), BF)],
    )


def norm_back(up, n, inv, gain):
    scaled = up * gain
    center = jnp.mean(scaled, axis=-1, keepdims=True)
    spread = jnp.mean(scaled * n, axis=-1, keepdims=True)
    return inv * (scaled - center - n * spread)


def col_sum(x):
    return jnp.sum(x, axis=0, keepdims=True)


def feed_bwd_body(core_ref, slope_ref, dh_ref, hm_ref, vec_ref, u_ref, *rest):
    up, down = rest[:4], rest[4:8]
    gup, gdown, (dhm_ref, gbu_ref, gvec_ref) = rest[8:12], rest[12:16], rest[16:19]
    wu_ref, wd_ref, gu_ref, gd_ref, mt_ref, dyt_ref, dm_ref = rest[19:]
    s, core = pl.program_id(0), core_ref[0]

    @pl.when(s == 0)
    def _():
        n, _ = norm(hm_ref[...])
        mt_ref[...] = turned((n * vec_ref[2:3, :] + vec_ref[3:4, :]).astype(BF))
        dyt_ref[...] = turned(dh_ref[...].astype(BF))
        dm_ref[...] = jnp.zeros((TOK, D), F32)

    assemble(1, s, core, up, wu_ref)
    assemble(2, s, core, down, wd_ref)
    dy = dh_ref[...].astype(BF)
    total = jnp.zeros((TOK, D), F32)
    for g in (0, 1):
        u = u_ref[0, g]
        act, t = gelu_parts(u)
        slope = 0.5 * (1.0 + t) + (0.5 * C0) * u * (1.0 - t * t) * (1.0 + (3.0 * C1) * (u * u))
        du = dot(dy, wd_ref[g]) * slope
        gbu_ref[0, g : g + 1, :] = col_sum(du)
        dub = du.astype(BF)
        gd_ref[g] = dot(dyt_ref[...], act.astype(BF)).astype(BF)
        gu_ref[g] = dot(mt_ref[...], dub).astype(BF)
        total = total + dot_nt(dub, wu_ref[g])
    dm_ref[...] += total
    disassemble(1, s, core, gup, gu_ref)
    disassemble(2, s, core, gdown, gd_ref)

    @pl.when(s == 3)
    def _():
        n, inv = norm(hm_ref[...])
        dm, dh = dm_ref[...], dh_ref[...]
        dhm_ref[...] = dh + norm_back(dm, n, inv, vec_ref[2:3, :])
        gvec_ref[...] = jnp.zeros((8, D), F32)
        gvec_ref[0:1, :] = col_sum(dm * n)
        gvec_ref[1:2, :] = col_sum(dm)
        gvec_ref[2:3, :] = col_sum(dh)


def feed_bwd(core, slopes, dh, hm, vec, u, up, down):
    wide = pltpu.VMEM((2, D, 512), BF)
    return call(
        feed_bwd_body,
        "feed_bwd",
        core,
        slopes,
        (dh, hm, vec, u, *merged(1, up), *merged(2, down)),
        [whole((TOK, D)), whole((TOK, D)), whole((8, D)), per_step((4, 2, TOK, 512))]
        + quad_specs(1)
        + quad_specs(2),
        quad_shapes(1) + quad_shapes(2) + [sds((TOK, D)), sds((4, 2, 512)), sds((8, D))],
        quad_specs(1) + quad_specs(2) + [whole((TOK, D)), per_step((4, 2, 512)), whole((8, D))],
        [wide] * 4
        + [pltpu.VMEM((D, TOK), BF), pltpu.VMEM((D, TOK), BF), pltpu.VMEM((TOK, D), F32)],
    )


def attn_bwd_body(core_ref, slope_ref, dhm_ref, h_ref, vec_ref, qkv_ref, ctx_ref, *rest):
    quad, gquad, (dh_ref, gqv_ref, gvec_ref) = rest[:4], rest[4:8], rest[8:11]
    w_ref, gw_ref, at_ref, dzt_ref, da_ref = rest[11:]
    s, core = pl.program_id(0), core_ref[0]

    @pl.when(s == 0)
    def _():
        n, _ = norm(h_ref[...])
        at_ref[...] = turned((n * vec_ref[0:1, :] + vec_ref[1:2, :]).astype(BF))
        dzt_ref[...] = turned(dhm_ref[...].astype(BF))
        da_ref[...] = jnp.zeros((TOK, D), F32)

    assemble(0, s, core, quad, w_ref)
    dz = dhm_ref[...].astype(BF)
    total = jnp.zeros((TOK, D), F32)
    for g in (0, 1):
        qkv = qkv_ref[0, g]
        dctx = dot(dz, w_ref[g, :, 384:512]).astype(BF)
        gw_ref[g, :, 384:512] = dot(dzt_ref[...], ctx_ref[0, g]).astype(BF)
        grads = [[], [], []]
        for hd in (0, 1):
            q, k, v = (qkv[:, j * 128 + hd * 64 : j * 128 + hd * 64 + 64] for j in range(3))
            dc = dctx[:, hd * 64 : hd * 64 + 64]
            p = chance_of(q, k, slope_ref[s * 4 + g * 2 + hd])
            dp = dot_nt(dc, v)
            delta = jnp.sum(p * dp, axis=-1, keepdims=True)
            ds = (p * (dp - delta) * 0.125).astype(BF)
            grads[0].append(dot(ds, k))
            grads[1].append(dot_tn(ds, q))
            grads[2].append(dot_tn(p.astype(BF), dc))
        dqkv = jnp.concatenate([g_ for three in grads for g_ in three], axis=1)
        gqv_ref[0, g : g + 1, :] = col_sum(dqkv)
        dqkv = dqkv.astype(BF)
        gw_ref[g, :, 0:384] = dot(at_ref[...], dqkv).astype(BF)
        total = total + dot_nt(dqkv, w_ref[g, :, 0:384])
    da_ref[...] += total
    disassemble(0, s, core, gquad, gw_ref)

    @pl.when(s == 3)
    def _():
        n, inv = norm(h_ref[...])
        da, dhm = da_ref[...], dhm_ref[...]
        dh_ref[...] = dhm + norm_back(da, n, inv, vec_ref[0:1, :])
        gvec_ref[...] = jnp.zeros((8, D), F32)
        gvec_ref[0:1, :] = col_sum(da * n)
        gvec_ref[1:2, :] = col_sum(da)
        gvec_ref[2:3, :] = col_sum(dhm)


def attn_bwd(core, slopes, dhm, h, vec, qkv, ctx, quad):
    wide = pltpu.VMEM((2, D, 512), BF)
    return call(
        attn_bwd_body,
        "attn_bwd",
        core,
        slopes,
        (dhm, h, vec, qkv, ctx, *merged(0, quad)),
        [
            whole((TOK, D)),
            whole((TOK, D)),
            whole((8, D)),
            per_step((4, 2, TOK, 384)),
            per_step((4, 2, TOK, 128)),
        ]
        + quad_specs(0),
        quad_shapes(0) + [sds((TOK, D)), sds((4, 2, 384)), sds((8, D))],
        quad_specs(0) + [whole((TOK, D)), per_step((4, 2, 384)), whole((8, D))],
        [wide] * 2
        + [pltpu.VMEM((D, TOK), BF), pltpu.VMEM((D, TOK), BF), pltpu.VMEM((TOK, D), F32)],
    )


def orders():
    at = {a: lax.axis_index(a) for a in AXES}
    rows = []
    for half, low, z2, z1 in itertools.product((0, 1), repeat=4):
        core = at["core"] ^ half
        z = at["z"] ^ jnp.where(core == 0, z1 ^ (3 * z2), (3 * z1) ^ z2)
        rows.append(((at["ylo"] ^ low) * 4 + z) * 2 + core)
    cols = []
    for x2, x1, g in itertools.product((0, 1), repeat=3):
        x = at["x"] ^ jnp.where(at["core"] == 0, x1 ^ (3 * x2), (3 * x1) ^ x2)
        cols.append(x * 2 + (at["yhi"] ^ g))
    return at, jnp.stack(rows), jnp.stack(cols)


def one_hot(index, count):
    return (index[:, None] == jnp.arange(count)[None, :]).astype(F32)


def shards(
    hidden_in, w_qkv, w_attn_out, w_up, w_down, qv_bias, up_bias, ln_gain, row_bias, cotangent
):
    at, rows, cols = orders()
    core = at["core"].reshape(1).astype(jnp.int32)
    lanes = (rows[:, None] * 64 + jnp.arange(64)[None, :]).reshape(-1)
    lane_hot = one_hot(lanes, D)

    def to_own(v):
        return lax.dot_general(v, lane_hot, (((1,), (1,)), ((), ())), precision=HIGH)

    def from_own(v):
        return jnp.dot(v, lane_hot, precision=HIGH)

    heads = cols[:, None] * 2 + jnp.arange(2)[None, :]
    slopes = jnp.exp2(-8.0 * (heads.astype(F32) + 1.0) / HEADS).reshape(-1)

    p = (at["ylo"] * 4 + at["z"]) * 2 + at["core"]
    put_row = (jnp.arange(D)[None, :] == p * 64 + jnp.arange(64)[:, None]).astype(BF)
    put_col = (jnp.arange(64)[None, :] == p * 4 + jnp.arange(4)[:, None]).astype(BF)
    own_rows = jnp.concatenate([ln_gain.reshape(64, 4), row_bias.reshape(64, 8)], axis=1)
    own_cols = jnp.concatenate([qv_bias.reshape(4, 2, 4), up_bias], axis=2).reshape(4, 24)
    small = (dot_tn(own_rows, put_row).astype(BF), dot_tn(own_cols, put_col).astype(BF))
    def unpacked(small):
        whole_rows = to_own(small[0].astype(F32))
        gains, shifts = whole_rows[:4].reshape(2, 2, D), whole_rows[4:].reshape(2, 4, D)
        whole_cols = small[1].astype(F32).reshape(4, 2, LAYERS, 12, 64)
        vecs, qkv_shifts, up_shifts = [], [], []
        for l in range(LAYERS):
            vecs.append(
                jnp.concatenate(
                    [gains[l, 0:1], shifts[l, 0:1], gains[l, 1:2], shifts[l, 1:4]]
                    + [jnp.zeros((2, D), F32)]
                )
            )
            qv = whole_cols[:, :, l, :4].reshape(4, 2, 2, 128)
            qkv_shifts.append(
                jnp.concatenate([qv[:, :, 0], jnp.zeros((4, 2, 128), F32), qv[:, :, 1]], axis=2)
            )
            up_shifts.append(whole_cols[:, :, l, 4:].reshape(4, 2, 512))
        return vecs, qkv_shifts, up_shifts

    h, dh = to_own(hidden_in), to_own(cotangent)
    bufs = joined(
        jnp.concatenate([w_qkv.reshape(64, LAYERS, 384), w_attn_out], axis=2).swapaxes(0, 1),
        w_up.swapaxes(0, 1),
        w_down.swapaxes(0, 1),
    )
    for n in range(COMMON):
        recv, small = joined(exchange(bufs, n), small_step(n, *small))
        bufs = doubled(bufs, recv)
    first, second = ([b[..., l, :, :] for b in bufs] for l in range(LAYERS))

    recv, small = joined(exchange(first, 3), small_step(3, *small))
    first = doubled(first, recv)
    recv, small, h, dh = joined(exchange(first, 4), small_step(4, *small), h, dh)
    first = doubled(first, recv)
    first_hi, first_oth = joined(exchange(first, 5), over_cores_in_turn(first))

    mix_oth, recv, small = joined(
        swap(first_hi[0], "core"), exchange(second, 3), small_step(6, *small_step(5, *small))
    )
    second = doubled(second, recv)
    vecs, qkv_shifts, up_shifts = unpacked(small)
    mix0 = (first[0], first_hi[0], first_oth[0], mix_oth)
    (qkv0, ctx0, hm0), rest_oth, recv = joined(
        attn_fwd(core, slopes, h, vecs[0], qkv_shifts[0], mix0),
        over_cores(first_hi[1:]),
        exchange(second, 4),
    )
    second = doubled(second, recv)
    up0, down0 = ((first[i], first_hi[i], first_oth[i], rest_oth[i - 1]) for i in (1, 2))
    (u0, h1), second_hi, second_oth = joined(
        feed_fwd(core, slopes, hm0, vecs[0], up_shifts[0], up0, down0),
        exchange(second, 5),
        over_cores_in_turn(second),
    )
    h1, mix_oth, second_hi = joined(h1, swap(second_hi[0], "core"), second_hi)
    mix1 = (second[0], second_hi[0], second_oth[0], mix_oth)
    (qkv1, ctx1, hm1), rest_oth = joined(
        attn_fwd(core, slopes, h1, vecs[1], qkv_shifts[1], mix1), over_cores(second_hi[1:])
    )
    up1, down1 = ((second[i], second_hi[i], second_oth[i], rest_oth[i - 1]) for i in (1, 2))
    u1, out = feed_fwd(core, slopes, hm1, vecs[1], up_shifts[1], up1, down1)

    def feed_back(dh, hm, l, u, up, down):
        outs = feed_bwd(core, slopes, dh, hm, vecs[l], u, up, down)
        return unmerged(outs[:4]), unmerged(outs[4:8]), outs[8:]

    def attn_back(dhm, h, l, qkv, ctx, mix):
        outs = attn_bwd(core, slopes, dhm, h, vecs[l], qkv, ctx, mix)
        return unmerged(outs[:4]), outs[4:]

    def sent(part, hi, n):
        return swap(hi, ORDERS[part][n // 2], n % 2 + 1)

    def core_sums(grads, got):
        return [plus(g, r) for g, r in zip(grads, got)]

    gup1, gdown1, (dhm1, gbu1, gvec21) = feed_back(dh, hm1, 1, u1, up1, down1)
    (gmix1, (dh, gqv1, gvec11)), up_got, down_got = joined(
        attn_back(dhm1, h1, 1, qkv1, ctx1, mix1), over_cores(gup1[2:]), over_cores(gdown1[2:])
    )
    up1_lo, up1_hi = core_sums(gup1, up_got)
    down1_lo, down1_hi = core_sums(gdown1, down_got)
    up_got, down_got = sent(1, up1_hi, 5), sent(2, down1_hi, 5)
    mix1_hi = plus(gmix1[1], swap(gmix1[3], "core"))
    dh, mix1_hi, hm0, out = joined(dh, mix1_hi, hm0, out)
    mix_got = sent(0, mix1_hi, 5)
    mix1_lo = plus(gmix1[0], swap(gmix1[2], "core"))
    (gup0, gdown0, (dhm0, gbu0, gvec20)), up_got, down_got, mix1_lo, hidden_out = joined(
        feed_back(dh, hm0, 0, u0, up0, down0), up_got, down_got, mix1_lo, from_own(out)
    )
    up1_lo, up1_hi = halves(up1_lo, up_got)
    down1_lo, down1_hi = halves(down1_lo, down_got)
    up_got, down_got = sent(1, up1_hi, 4), sent(2, down1_hi, 4)
    mix1_lo, mix1_hi = halves(mix1_lo, mix_got)
    dhm0, mix1_hi = joined(dhm0, mix1_hi)
    mix_got = sent(0, mix1_hi, 4)
    (gmix0, (dh, gqv0, gvec10)), up_got, down_got, mix_got, up0_got, down0_got = joined(
        attn_back(dhm0, h, 0, qkv0, ctx0, mix0),
        up_got,
        down_got,
        mix_got,
        swap(gup0[3], "core"),
        swap(gdown0[3], "core"),
    )
    lay1 = [
        halves(lo, got)
        for lo, got in ((mix1_lo, mix_got), (up1_lo, up_got), (down1_lo, down_got))
    ]
    up0_hi, down0_hi = plus(gup0[1], up0_got), plus(gdown0[1], down0_got)
    rows = jnp.concatenate(
        [
            v
            for v1, v2 in ((gvec10, gvec20), (gvec11, gvec21))
            for v in (v1[0:1], v2[0:1], v1[1:2], v2[1:2], v1[2:3], v2[2:3])
        ]
    )
    cols = jnp.concatenate(
        [
            v
            for gqv, gbu in ((gqv0, gbu0), (gqv1, gbu1))
            for v in (gqv[:, :, :128], gqv[:, :, 256:], gbu)
        ],
        axis=2,
    ).reshape(2, 2, 2, LAYERS * 768)
    mix0_got, got1, up0_hi, down0_hi, (rows, cols) = joined(
        swap(gmix0[3], "core"),
        [sent(i, lay1[i][1], 3) for i in range(3)],
        up0_hi,
        down0_hi,
        sum_small_step(0, rows, cols),
    )
    up_got, down_got = sent(1, up0_hi, 5), sent(2, down0_hi, 5)
    mix_got = sent(0, plus(gmix0[1], mix0_got), 5)
    got, los, (rows, cols), grad_in, lay1 = joined(
        [mix_got, up_got, down_got],
        [plus(g[0], swap(g[2], "core")) for g in (gmix0, gup0, gdown0)],
        sum_small_step(1, rows, cols),
        from_own(dh),
        [plus(s[0], g) for s, g in zip(lay1, got1)],
    )
    lay0 = [halves(lo, g) for lo, g in zip(los, got)]
    got, (rows, cols) = joined(
        [sent(i, lay0[i][1], 4) for i in range(3)], sum_small_step(2, rows, cols)
    )
    lay0 = [halves(s[0], g) for s, g in zip(lay0, got)]
    got, (rows, cols) = joined(
        [sent(i, lay0[i][1], 3) for i in range(3)], sum_small_step(3, rows, cols)
    )
    both = [
        tuple(jnp.stack([plus(s[0][k], g[k]), s1[k]], axis=2) for k in (0, 1))
        for s, g, s1 in zip(lay0, got, lay1)
    ]
    for n in (2, 1):
        got, (rows, cols) = joined(
            [sent(i, both[i][1], n) for i in range(3)], sum_small_step(6 - n, rows, cols)
        )
        both = [halves(s[0], g) for s, g in zip(both, got)]
    got, (rows, cols) = joined(
        [sent(i, both[i][1], 0) for i in range(3)], sum_small_step(6, rows, cols)
    )
    mixes, ups, downs = (
        jnp.swapaxes(s[0].astype(F32) + g.astype(F32), 0, 1) for s, g in zip(both, got)
    )
    rows = rows[:, :64].T.reshape(64, LAYERS, 6)
    cols = lax.dot_general(
        put_col.astype(F32), cols.reshape(24, 64), (((1,), (1,)), ((), ())), precision=HIGH
    ).reshape(4, LAYERS, 12)
    return (
        hidden_out,
        grad_in,
        mixes[:, :, :384].reshape(64, LAYERS, 3, 128),
        mixes[:, :, 384:],
        ups,
        downs,
        cols[:, :, :4].reshape(4, LAYERS, 2, 2),
        cols[:, :, 4:],
        rows[:, :, :2],
        rows[:, :, 2:],
    )


def solution(mesh):
    torus = Mesh(mesh.devices.reshape(SIZES), AXES)
    token = P((*DP, *TENSOR), None)
    placed = (
        token,
        P(DP, None, None, TENSOR),
        P(DP, None, TENSOR),
        P(DP, None, TENSOR),
        P(DP, None, TENSOR),
        P(DP, None, None, TENSOR),
        P(DP, None, TENSOR),
        P(DP, None, None),
        P(DP, None, None),
        token,
    )
    outs = (token, token, *placed[1:9])
    return jax.shard_map(shards, mesh=torus, in_specs=placed, out_specs=outs, check_vma=False)
```

```python
import itertools
from functools import partial

import jax
import jax.numpy as jnp
import numpy as np
from jax import lax
from jax.experimental import pallas as pl
from jax.experimental.pallas import tpu as pltpu
from jax.sharding import Mesh
from jax.sharding import PartitionSpec as P

AXES = ("ylo", "z", "core", "x", "yhi")
SIZES = (2, 4, 2, 4, 2)
DP = ("ylo", "z", "core")
TENSOR = ("x", "yhi")
ORDERS = ("xyz", "yzx", "zxy")
LAYERS = 2
COMMON = 3
TOK = 160
D = 1024
HEADS = 16
EPS = 1e-05
BF, F32 = jnp.bfloat16, jnp.float32
HIGH = lax.Precision.HIGHEST


def pairs(axis, step):
    out = []
    for ylo, z, core, x, yhi in itertools.product(*map(range, SIZES)):
        c = {"x": x, "y": 2 * yhi + ylo, "z": z, "core": core}
        if axis == "core":
            c["core"] ^= 1
        else:
            c[axis] ^= 1 if (step == 1) == (core == 0) else 3
        src = np.ravel_multi_index((ylo, z, core, x, yhi), SIZES)
        dst = np.ravel_multi_index((c["y"] & 1, c["z"], c["core"], c["x"], c["y"] >> 1), SIZES)
        out.append((int(src), int(dst)))
    return out


def swap(v, axis, step=0):
    return lax.ppermute(v, AXES, pairs(axis, step))


def joined(*values):
    return lax.optimization_barrier(values)


def exchange(bufs, n):
    return [swap(b, ORDERS[i][n // 2], n % 2 + 1) for i, b in enumerate(bufs)]


def doubled(bufs, recv):
    return [lax.optimization_barrier(jnp.stack([b, r])) for b, r in zip(bufs, recv)]


def over_cores(values):
    return [swap(v, "core") for v in values]


def over_cores_in_turn(values):
    one, two = over_cores(values[:2])
    one, last = joined(one, values[2])
    return [one, two, swap(last, "core")]


def to_each(v):
    return lax.all_to_all(v, AXES, 0, 0, tiled=True)


def plus(a, b):
    return (a.astype(F32) + b.astype(F32)).astype(BF)


def halves(lo, recv):
    hi = plus(lo[1], recv[1])
    return plus(lo[0], recv[0]), hi


def norm(h):
    center = jnp.mean(h, axis=-1, keepdims=True)
    c = h - center
    var = jnp.mean(c * c, axis=-1, keepdims=True)
    inv = lax.rsqrt(var + EPS)
    return c * inv, inv


def dot(a, b):
    return lax.dot_general(a, b, (((1,), (0,)), ((), ())), preferred_element_type=F32)


def dot_nt(a, b):
    return lax.dot_general(a, b, (((1,), (1,)), ((), ())), preferred_element_type=F32)


def dot_tn(a, b):
    return lax.dot_general(a, b, (((0,), (0,)), ((), ())), preferred_element_type=F32)


def turned(x):
    return jnp.transpose(x.astype(F32)).astype(BF)


BITS = tuple(itertools.product((0, 1), repeat=2))


def placed_at(core, half, y2, y1):
    if y1 == y2:
        return y1
    c = core if half == 0 else 1 - core
    return c if y1 else 1 - c


def each_block(part, step, quad):
    a, b = step // 2, step % 2
    for half in range(len(quad) // 2):
        lo, hi = quad[2 * half], quad[2 * half + 1]
        for (z2, z1), (y2, y1) in itertools.product(BITS, BITS):
            row = half * 8 + (y1 ^ y2) * 4 + z2 * 2 + z1
            if part == 0:
                yield None, half, y2, y1, row, (lo, hi)[z2], (z1 * 4 + y2 * 2 + y1, 0)
            elif part == 2:
                yield None, half, y2, y1, row, (lo, hi)[y2], (y1, 0, z2 * 2 + z1)
            else:
                which = a if half == 0 else b
                for x2 in (0, 1):
                    yield which == x2, half, y2, y1, row, (lo, hi)[x2], (0, z2 * 2 + z1, y2 * 2 + y1)


def by_condition(part, step, quad, fn):
    if part != 1:
        for _, *rest in each_block(part, step, quad):
            fn(*rest)
        return
    groups = {}
    for cond, half, *rest in each_block(part, step, quad):
        groups.setdefault((half, id(rest[3])), (cond, []))[1].append((half, *rest))
    for cond, items in groups.values():

        @pl.when(cond)
        def _(items=items):
            for it in items:
                fn(*it)


def assemble(part, step, core, quad, w_ref):
    def put(half, y2, y1, row, ref, index):
        w_ref[placed_at(core, half, y2, y1), row * 64 : row * 64 + 64, :] = ref[index]

    by_condition(part, step, quad, put)


def disassemble(part, step, core, quad, w_ref):
    def get(half, y2, y1, row, ref, index):
        ref[index] = w_ref[placed_at(core, half, y2, y1), row * 64 : row * 64 + 64, :]

    by_condition(part, step, quad, get)


def merged(part, quad):
    shape = {0: (8, 4, 64, 512), 1: (2, 4, 4, 64, 512), 2: (2, 4, 4, 64, 512)}[part]
    return tuple(q.reshape(shape) for q in quad)


def unmerged(quad):
    return tuple(q.reshape(2, 2, 2, 2, 2, 64, 512) for q in quad)


def quad_shapes(part):
    shape = {0: (8, 4, 64, 512), 1: (2, 4, 4, 64, 512), 2: (2, 4, 4, 64, 512)}[part]
    return [jax.ShapeDtypeStruct(shape, BF)] * 4


def quad_specs(part):
    def own(s):
        return s

    def oth(s):
        return (s % 2) * 2 + s // 2

    if part == 0:
        return [
            pl.BlockSpec((8, 1, 64, 512), lambda s, *_, f=f: (0, f(s), 0, 0))
            for f in (own, own, oth, oth)
        ]
    if part == 2:
        return [
            pl.BlockSpec((2, 1, 4, 64, 512), lambda s, *_, f=f: (0, f(s), 0, 0, 0))
            for f in (own, own, oth, oth)
        ]
    maps = (
        lambda s: jnp.minimum(s, 1),
        lambda s: jnp.maximum(s - 2, 0),
        lambda s: s // 2,
        lambda s: s // 2,
    )
    return [
        pl.BlockSpec((1, 4, 4, 64, 512), lambda s, *_, f=f: (f(s), 0, 0, 0, 0)) for f in maps
    ]


def whole(shape):
    zeros = (0,) * len(shape)
    return pl.BlockSpec(shape, lambda s, *_: zeros)


def per_step(shape):
    zeros = (0,) * (len(shape) - 1)
    return pl.BlockSpec((1, *shape[1:]), lambda s, *_: (s, *zeros))


def call(body, name, core, slopes, ins, in_specs, outs, out_specs, scratch):
    return pl.pallas_call(
        body,
        name=name,
        out_shape=outs,
        grid_spec=pltpu.PrefetchScalarGridSpec(
            num_scalar_prefetch=2,
            grid=(4,),
            in_specs=in_specs,
            out_specs=out_specs,
            scratch_shapes=scratch,
        ),
        cost_estimate=pl.CostEstimate(flops=1 << 20, transcendentals=0, bytes_accessed=1 << 18),
        compiler_params=pltpu.CompilerParams(
            dimension_semantics=("arbitrary",), vmem_limit_bytes=48 << 20
        ),
    )(core, slopes, *ins)


def sds(shape, dtype=F32):
    return jax.ShapeDtypeStruct(shape, dtype)


def scores_of(q, k, slope):
    s = dot_nt(q, k) * 0.125
    row = lax.broadcasted_iota(jnp.int32, (TOK, TOK), 0)
    col = lax.broadcasted_iota(jnp.int32, (TOK, TOK), 1)
    s = s + slope * (col - row).astype(F32)
    return jnp.where(col <= row, s, -jnp.inf)


def chance_of(q, k, slope):
    s = scores_of(q, k, slope)
    e = jnp.exp(s - jnp.max(s, axis=-1, keepdims=True))
    return e / jnp.sum(e, axis=-1, keepdims=True)


def attn_fwd_body(core_ref, slope_ref, h_ref, vec_ref, bias_ref, *rest):
    quad, (qkv_ref, ctx_ref, hm_ref), (w_ref, a_ref) = rest[:4], rest[4:7], rest[7:]
    s, core = pl.program_id(0), core_ref[0]

    @pl.when(s == 0)
    def _():
        n, _ = norm(h_ref[...])
        a_ref[...] = (n * vec_ref[0:1, :] + vec_ref[1:2, :]).astype(BF)
        hm_ref[...] = h_ref[...] + vec_ref[4:5, :]

    assemble(0, s, core, quad, w_ref)
    total = jnp.zeros((TOK, D), F32)
    for g in (0, 1):
        qkv = (dot(a_ref[...], w_ref[g, :, 0:384]) + bias_ref[0, g : g + 1, :]).astype(BF)
        qkv_ref[0, g] = qkv
        ctx = []
        for hd in (0, 1):
            q, k, v = (qkv[:, j * 128 + hd * 64 : j * 128 + hd * 64 + 64] for j in range(3))
            p = chance_of(q, k, slope_ref[s * 4 + g * 2 + hd]).astype(BF)
            ctx.append(dot(p, v))
        ctx = jnp.concatenate(ctx, axis=1).astype(BF)
        ctx_ref[0, g] = ctx
        total = total + dot_nt(ctx, w_ref[g, :, 384:512])
    hm_ref[...] += total


def attn_fwd(core, slopes, h, vec, bias, quad):
    return call(
        attn_fwd_body,
        "attn_fwd",
        core,
        slopes,
        (h, vec, bias, *merged(0, quad)),
        [whole((TOK, D)), whole((8, D)), per_step((4, 2, 384))] + quad_specs(0),
        [sds((4, 2, TOK, 384), BF), sds((4, 2, TOK, 128), BF), sds((TOK, D))],
        [per_step((4, 2, TOK, 384)), per_step((4, 2, TOK, 128)), whole((TOK, D))],
        [pltpu.VMEM((2, D, 512), BF), pltpu.VMEM((TOK, D), BF)],
    )


C0, C1 = 0.7978845608, 0.044715


def gelu_parts(u):
    t = jnp.tanh(C0 * (u + C1 * (u * u * u)))
    return 0.5 * u * (1.0 + t), t


def feed_fwd_body(core_ref, slope_ref, hm_ref, vec_ref, bias_ref, *rest):
    up, down, (u_ref, out_ref), (wu_ref, wd_ref, m_ref) = rest[:4], rest[4:8], rest[8:10], rest[10:]
    s, core = pl.program_id(0), core_ref[0]

    @pl.when(s == 0)
    def _():
        n, _ = norm(hm_ref[...])
        m_ref[...] = (n * vec_ref[2:3, :] + vec_ref[3:4, :]).astype(BF)
        out_ref[...] = hm_ref[...] + vec_ref[5:6, :]

    assemble(1, s, core, up, wu_ref)
    assemble(2, s, core, down, wd_ref)
    total = jnp.zeros((TOK, D), F32)
    for g in (0, 1):
        u = dot(m_ref[...], wu_ref[g]) + bias_ref[0, g : g + 1, :]
        u_ref[0, g] = u
        act, _ = gelu_parts(u)
        total = total + dot_nt(act.astype(BF), wd_ref[g])
    out_ref[...] += total


def feed_fwd(core, slopes, hm, vec, bias, up, down):
    return call(
        feed_fwd_body,
        "feed_fwd",
        core,
        slopes,
        (hm, vec, bias, *merged(1, up), *merged(2, down)),
        [whole((TOK, D)), whole((8, D)), per_step((4, 2, 512))] + quad_specs(1) + quad_specs(2),
        [sds((4, 2, TOK, 512)), sds((TOK, D))],
        [per_step((4, 2, TOK, 512)), whole((TOK, D))],
        [pltpu.VMEM((2, D, 512), BF), pltpu.VMEM((2, D, 512), BF), pltpu.VMEM((TOK, D), BF)],
    )


def norm_back(up, n, inv, gain):
    scaled = up * gain
    center = jnp.mean(scaled, axis=-1, keepdims=True)
    spread = jnp.mean(scaled * n, axis=-1, keepdims=True)
    return inv * (scaled - center - n * spread)


def col_sum(x):
    return jnp.sum(x, axis=0, keepdims=True)


def keep_halves(own_ref, oth_ref, i, x):
    own_ref[i] = x[:, :512]
    oth_ref[i] = x[:, 512:]


def feed_bwd_body(core_ref, slope_ref, dh_ref, hm_ref, vec_ref, u_ref, *rest):
    up, down = rest[:4], rest[4:8]
    dhm_ref, gbu_ref, gvec_ref, ad_ref, own_ref, oth_ref = rest[8:14]
    wu_ref, wd_ref, dm_ref = rest[14:]
    s, core = pl.program_id(0), core_ref[0]
    dy = dh_ref[...].astype(BF)

    @pl.when(s == 0)
    def _():
        n, _ = norm(hm_ref[...])
        m = (n * vec_ref[2:3, :] + vec_ref[3:4, :]).astype(BF)
        keep_halves(own_ref, oth_ref, 0, m)
        keep_halves(own_ref, oth_ref, 1, dy)
        dm_ref[...] = jnp.zeros((TOK, D), F32)

    assemble(1, s, core, up, wu_ref)
    assemble(2, s, core, down, wd_ref)
    total = jnp.zeros((TOK, D), F32)
    for g in (0, 1):
        u = u_ref[0, g]
        act, t = gelu_parts(u)
        slope = 0.5 * (1.0 + t) + (0.5 * C0) * u * (1.0 - t * t) * (1.0 + (3.0 * C1) * (u * u))
        du = dot(dy, wd_ref[g]) * slope
        gbu_ref[0, g : g + 1, :] = col_sum(du)
        dub = du.astype(BF)
        ad_ref[0, g, 0] = dub
        ad_ref[0, g, 1] = act.astype(BF)
        total = total + dot_nt(dub, wu_ref[g])
    dm_ref[...] += total

    @pl.when(s == 3)
    def _():
        n, inv = norm(hm_ref[...])
        dm, dh = dm_ref[...], dh_ref[...]
        dhm_ref[...] = dh + norm_back(dm, n, inv, vec_ref[2:3, :])
        gvec_ref[...] = jnp.zeros((8, D), F32)
        gvec_ref[0:1, :] = col_sum(dm * n)
        gvec_ref[1:2, :] = col_sum(dm)
        gvec_ref[2:3, :] = col_sum(dh)


def feed_bwd(core, slopes, dh, hm, vec, u, up, down):
    half = (2, TOK, 512)
    return call(
        feed_bwd_body,
        "feed_bwd",
        core,
        slopes,
        (dh, hm, vec, u, *merged(1, up), *merged(2, down)),
        [whole((TOK, D)), whole((TOK, D)), whole((8, D)), per_step((4, 2, TOK, 512))]
        + quad_specs(1)
        + quad_specs(2),
        [sds((TOK, D)), sds((4, 2, 512)), sds((8, D)), sds((4, 2, 2, TOK, 512), BF)]
        + [sds(half, BF)] * 2,
        [whole((TOK, D)), per_step((4, 2, 512)), whole((8, D)), per_step((4, 2, 2, TOK, 512))]
        + [whole(half)] * 2,
        [pltpu.VMEM((2, D, 512), BF)] * 2 + [pltpu.VMEM((TOK, D), F32)],
    )


def attn_bwd_body(core_ref, slope_ref, dhm_ref, h_ref, vec_ref, qkv_ref, ctx_ref, *rest):
    quad, (dh_ref, gqv_ref, gvec_ref, dc_ref, own_ref, oth_ref) = rest[:4], rest[4:10]
    w_ref, da_ref = rest[10:]
    s, core = pl.program_id(0), core_ref[0]
    dz = dhm_ref[...].astype(BF)

    @pl.when(s == 0)
    def _():
        n, _ = norm(h_ref[...])
        a = (n * vec_ref[0:1, :] + vec_ref[1:2, :]).astype(BF)
        keep_halves(own_ref, oth_ref, 0, a)
        keep_halves(own_ref, oth_ref, 1, dz)
        da_ref[...] = jnp.zeros((TOK, D), F32)

    assemble(0, s, core, quad, w_ref)
    total = jnp.zeros((TOK, D), F32)
    for g in (0, 1):
        qkv = qkv_ref[0, g]
        dctx = dot(dz, w_ref[g, :, 384:512]).astype(BF)
        grads = [[], [], []]
        for hd in (0, 1):
            q, k, v = (qkv[:, j * 128 + hd * 64 : j * 128 + hd * 64 + 64] for j in range(3))
            dc = dctx[:, hd * 64 : hd * 64 + 64]
            p = chance_of(q, k, slope_ref[s * 4 + g * 2 + hd])
            dp = dot_nt(dc, v)
            delta = jnp.sum(p * dp, axis=-1, keepdims=True)
            ds = (p * (dp - delta) * 0.125).astype(BF)
            grads[0].append(dot(ds, k))
            grads[1].append(dot_tn(ds, q))
            grads[2].append(dot_tn(p.astype(BF), dc))
        dqkv = jnp.concatenate([g_ for three in grads for g_ in three], axis=1)
        gqv_ref[0, g : g + 1, :] = col_sum(dqkv)
        dqkv = dqkv.astype(BF)
        dc_ref[0, g, :, 0:384] = dqkv
        dc_ref[0, g, :, 384:512] = ctx_ref[0, g]
        total = total + dot_nt(dqkv, w_ref[g, :, 0:384])
    da_ref[...] += total

    @pl.when(s == 3)
    def _():
        n, inv = norm(h_ref[...])
        da, dhm = da_ref[...], dhm_ref[...]
        dh_ref[...] = dhm + norm_back(da, n, inv, vec_ref[0:1, :])
        gvec_ref[...] = jnp.zeros((8, D), F32)
        gvec_ref[0:1, :] = col_sum(da * n)
        gvec_ref[1:2, :] = col_sum(da)
        gvec_ref[2:3, :] = col_sum(dhm)


def attn_bwd(core, slopes, dhm, h, vec, qkv, ctx, quad):
    half = (2, TOK, 512)
    return call(
        attn_bwd_body,
        "attn_bwd",
        core,
        slopes,
        (dhm, h, vec, qkv, ctx, *merged(0, quad)),
        [
            whole((TOK, D)),
            whole((TOK, D)),
            whole((8, D)),
            per_step((4, 2, TOK, 384)),
            per_step((4, 2, TOK, 128)),
        ]
        + quad_specs(0),
        [sds((TOK, D)), sds((4, 2, 384)), sds((8, D)), sds((4, 2, TOK, 512), BF)]
        + [sds(half, BF)] * 2,
        [whole((TOK, D)), per_step((4, 2, 384)), whole((8, D)), per_step((4, 2, TOK, 512))]
        + [whole(half)] * 2,
        [pltpu.VMEM((2, D, 512), BF), pltpu.VMEM((TOK, D), F32)],
    )


def both_tokens(mine, theirs):
    return turned(jnp.concatenate([mine, theirs], axis=0))


def feed_grad_body(core_ref, slope_ref, ad_ref, ad2_ref, own_ref, own2_ref, *rest):
    gup, gdown, (mt_ref, dyt_ref, gu_ref, gd_ref) = rest[:2], rest[2:4], rest[4:]
    s, core = pl.program_id(0), core_ref[0]

    @pl.when(s == 0)
    def _():
        mt_ref[...] = both_tokens(own_ref[0], own2_ref[0])
        dyt_ref[...] = both_tokens(own_ref[1], own2_ref[1])

    for g in (0, 1):
        du = jnp.concatenate([ad_ref[0, g, 0], ad2_ref[0, g, 0]], axis=0)
        act = jnp.concatenate([ad_ref[0, g, 1], ad2_ref[0, g, 1]], axis=0)
        gu_ref[g] = dot(mt_ref[...], du).astype(BF)
        gd_ref[g] = dot(dyt_ref[...], act).astype(BF)
    disassemble(1, s, core, gup, gu_ref)
    disassemble(2, s, core, gdown, gd_ref)


def attn_grad_body(core_ref, slope_ref, dc_ref, dc2_ref, own_ref, own2_ref, *rest):
    gmix, (at_ref, dzt_ref, gw_ref) = rest[:2], rest[2:]
    s, core = pl.program_id(0), core_ref[0]

    @pl.when(s == 0)
    def _():
        at_ref[...] = both_tokens(own_ref[0], own2_ref[0])
        dzt_ref[...] = both_tokens(own_ref[1], own2_ref[1])

    for g in (0, 1):
        dc = jnp.concatenate([dc_ref[0, g], dc2_ref[0, g]], axis=0)
        gw_ref[g, :, 0:384] = dot(at_ref[...], dc[:, 0:384]).astype(BF)
        gw_ref[g, :, 384:512] = dot(dzt_ref[...], dc[:, 384:512]).astype(BF)
    disassemble(0, s, core, gmix, gw_ref)


def weight_grads(body, name, parts, core, slopes, cols, cols2, rows, rows2):
    zeros = (0,) * (cols.ndim - 1)
    crossed = pl.BlockSpec((1, *cols.shape[1:]), lambda s, *_: ((s % 2) * 2 + s // 2, *zeros))
    outs = call(
        body,
        name,
        core,
        slopes,
        (cols, cols2, rows, rows2),
        [per_step(cols.shape), crossed, whole(rows.shape), whole(rows.shape)],
        [v for part in parts for v in quad_shapes(part)[:2]],
        [v for part in parts for v in quad_specs(part)[:2]],
        [pltpu.VMEM((512, 2 * TOK), BF)] * 2 + [pltpu.VMEM((2, 512, 512), BF)] * len(parts),
    )
    return [unmerged(outs[2 * i : 2 * i + 2]) for i in range(len(parts))]


def orders():
    at = {a: lax.axis_index(a) for a in AXES}
    rows = []
    for half, low, z2, z1 in itertools.product((0, 1), repeat=4):
        core = at["core"] ^ half
        z = at["z"] ^ jnp.where(core == 0, z1 ^ (3 * z2), (3 * z1) ^ z2)
        rows.append(((at["ylo"] ^ low) * 4 + z) * 2 + core)
    cols = []
    for x2, x1, g in itertools.product((0, 1), repeat=3):
        x = at["x"] ^ jnp.where(at["core"] == 0, x1 ^ (3 * x2), (3 * x1) ^ x2)
        cols.append(x * 2 + (at["yhi"] ^ g))
    return at, jnp.stack(rows), jnp.stack(cols)


def one_hot(index, count):
    return (index[:, None] == jnp.arange(count)[None, :]).astype(F32)


def shards(
    hidden_in, w_qkv, w_attn_out, w_up, w_down, qv_bias, up_bias, ln_gain, row_bias, cotangent
):
    at, rows, cols = orders()
    core = at["core"].reshape(1).astype(jnp.int32)
    lanes = (rows[:, None] * 64 + jnp.arange(64)[None, :]).reshape(-1)
    lane_hot = one_hot(lanes, D)

    def to_own(v):
        return lax.dot_general(v, lane_hot, (((1,), (1,)), ((), ())), precision=HIGH)

    def from_own(v):
        return jnp.dot(v, lane_hot, precision=HIGH)

    heads = cols[:, None] * 2 + jnp.arange(2)[None, :]
    slopes = jnp.exp2(-8.0 * (heads.astype(F32) + 1.0) / HEADS).reshape(-1)

    p = (at["ylo"] * 4 + at["z"]) * 2 + at["core"]
    col_hot = one_hot(cols, 8)
    own_rows = jnp.concatenate([ln_gain.reshape(64, 4), row_bias.reshape(64, 8)], axis=1)
    own_cols = jnp.concatenate([qv_bias.reshape(4, 2, 4), up_bias], axis=2).reshape(4, 24)
    small = jnp.concatenate([own_rows.T.reshape(-1), own_cols.T.reshape(-1)])
    small = jnp.pad(small, (0, 160)).reshape(8, 128)
    at_row = jnp.arange(1536)
    moved = (at_row % 96) // 4 * 64 + at_row // 96 * 4 + at_row % 4
    move = (moved[:, None] == at_row[None, :]).astype(BF)

    def unpacked(small):
        small = small.reshape(16, 8, 8, 128)
        whole_rows = small[:, 0, :6].reshape(16, 12, 64).swapaxes(0, 1).reshape(12, D)
        whole_rows = to_own(whole_rows.astype(F32))
        gains, shifts = whole_rows[:4].reshape(2, 2, D), whole_rows[4:].reshape(2, 4, D)
        whole_cols = dot(small[:, :, 6, :96].swapaxes(0, 1).reshape(8, 1536), move)
        whole_cols = jnp.dot(col_hot, whole_cols, precision=HIGH)
        whole_cols = whole_cols.reshape(4, 2, LAYERS, 12, 64)
        vecs, qkv_shifts, up_shifts = [], [], []
        for l in range(LAYERS):
            vecs.append(
                jnp.concatenate(
                    [gains[l, 0:1], shifts[l, 0:1], gains[l, 1:2], shifts[l, 1:4]]
                    + [jnp.zeros((2, D), F32)]
                )
            )
            qv = whole_cols[:, :, l, :4].reshape(4, 2, 2, 128)
            qkv_shifts.append(
                jnp.concatenate([qv[:, :, 0], jnp.zeros((4, 2, 128), F32), qv[:, :, 1]], axis=2)
            )
            up_shifts.append(whole_cols[:, :, l, 4:].reshape(4, 2, 512))
        return vecs, qkv_shifts, up_shifts

    h, dh = to_own(hidden_in), to_own(cotangent)
    bufs = joined(
        jnp.concatenate([w_qkv.reshape(64, LAYERS, 384), w_attn_out], axis=2).swapaxes(0, 1),
        w_up.swapaxes(0, 1),
        w_down.swapaxes(0, 1),
    )
    for n in range(COMMON):
        (recv,) = joined(exchange(bufs, n))
        bufs = doubled(bufs, recv)
    first, second = ([b[..., l, :, :] for b in bufs] for l in range(LAYERS))

    (recv,) = joined(exchange(first, 3))
    first = doubled(first, recv)
    recv, h, dh = joined(exchange(first, 4), h, dh)
    first = doubled(first, recv)
    first_hi, first_oth, small = joined(
        exchange(first, 5),
        over_cores_in_turn(first),
        to_each(jnp.broadcast_to(small[None], (128, 8, 128))),
    )

    mix_oth, recv = joined(swap(first_hi[0], "core"), exchange(second, 3))
    second = doubled(second, recv)
    vecs, qkv_shifts, up_shifts = unpacked(small)
    mix0 = (first[0], first_hi[0], first_oth[0], mix_oth)
    (qkv0, ctx0, hm0), rest_oth, recv = joined(
        attn_fwd(core, slopes, h, vecs[0], qkv_shifts[0], mix0),
        over_cores(first_hi[1:]),
        exchange(second, 4),
    )
    second = doubled(second, recv)
    up0, down0 = ((first[i], first_hi[i], first_oth[i], rest_oth[i - 1]) for i in (1, 2))
    (u0, h1), second_hi, second_oth = joined(
        feed_fwd(core, slopes, hm0, vecs[0], up_shifts[0], up0, down0),
        exchange(second, 5),
        over_cores_in_turn(second),
    )
    h1, mix_oth, second_hi = joined(h1, swap(second_hi[0], "core"), second_hi)
    mix1 = (second[0], second_hi[0], second_oth[0], mix_oth)
    (qkv1, ctx1, hm1), rest_oth = joined(
        attn_fwd(core, slopes, h1, vecs[1], qkv_shifts[1], mix1), over_cores(second_hi[1:])
    )
    up1, down1 = ((second[i], second_hi[i], second_oth[i], rest_oth[i - 1]) for i in (1, 2))
    u1, out = feed_fwd(core, slopes, hm1, vecs[1], up_shifts[1], up1, down1)

    def sent(part, hi, n):
        return swap(hi, ORDERS[part][n // 2], n % 2 + 1)

    feed_grads = partial(weight_grads, feed_grad_body, "feed_grad", (1, 2), core, slopes)
    attn_grads = partial(weight_grads, attn_grad_body, "attn_grad", (0,), core, slopes)

    dhm1, gbu1, gvec21, ad1, md1, md1_oth = feed_bwd(core, slopes, dh, hm1, vecs[1], u1, up1, down1)
    (dh, gqv1, gvec11, dc1, az1, az1_oth), ad1_got, md1_got = joined(
        attn_bwd(core, slopes, dhm1, h1, vecs[1], qkv1, ctx1, mix1),
        swap(ad1, "core"),
        swap(md1_oth, "core"),
    )
    (gup1, gdown1), dc1_got, az1_got = joined(
        feed_grads(ad1, ad1_got, md1, md1_got), swap(dc1, "core"), swap(az1_oth, "core")
    )
    up_got, down_got = sent(1, gup1[1], 5), sent(2, gdown1[1], 5)
    (gmix1,) = attn_grads(dc1, dc1_got, az1, az1_got)
    dh, gmix1 = joined(dh, gmix1)
    mix_got = sent(0, gmix1[1], 5)
    dhm0, gbu0, gvec20, ad0, md0, md0_oth = feed_bwd(core, slopes, dh, hm0, vecs[0], u0, up0, down0)
    (dh, gqv0, gvec10, dc0, az0, az0_oth), ad0_got, md0_got, got = joined(
        attn_bwd(core, slopes, dhm0, h, vecs[0], qkv0, ctx0, mix0),
        swap(ad0, "core"),
        swap(md0_oth, "core"),
        [mix_got, up_got, down_got],
    )
    lay1 = [halves(g[0], r) for g, r in zip((gmix1, gup1, gdown1), got)]
    ad0, his = joined(ad0, [v[1] for v in lay1])
    (gup0, gdown0), dc0_got, az0_got, got = joined(
        feed_grads(ad0, ad0_got, md0, md0_got),
        swap(dc0, "core"),
        swap(az0_oth, "core"),
        [sent(i, his[i], 4) for i in range(3)],
    )
    up_got, down_got = sent(1, gup0[1], 5), sent(2, gdown0[1], 5)
    (gmix0,) = attn_grads(dc0, dc0_got, az0, az0_got)
    mix_got = sent(0, gmix0[1], 5)
    lay1 = [halves(v[0], r) for v, r in zip(lay1, got)]
    rows = jnp.concatenate(
        [
            v
            for v1, v2 in ((gvec10, gvec20), (gvec11, gvec21))
            for v in (v1[0:1], v2[0:1], v1[1:2], v2[1:2], v1[2:3], v2[2:3])
        ]
    )
    cols = jnp.concatenate(
        [
            v
            for gqv, gbu in ((gqv0, gbu0), (gqv1, gbu1))
            for v in (gqv[:, :, :128], gqv[:, :, 256:], gbu)
        ],
        axis=2,
    ).reshape(8, 1536)
    rows = dot(rows.astype(BF), lane_hot.astype(BF)).astype(BF)
    rows = rows.reshape(12, 16, 64).swapaxes(0, 1).reshape(16, 1, 768)
    cols = dot_nt(dot_tn(col_hot.astype(BF), cols.astype(BF)).astype(BF), move).astype(BF)
    cols = cols.reshape(8, 16, 96).swapaxes(0, 1)
    small = jnp.concatenate([jnp.broadcast_to(rows, (16, 8, 768)), cols], axis=2)
    small = jnp.pad(small, ((0, 0), (0, 0), (0, 160))).reshape(128, 8, 128)
    got, got1, small, grad_in, hidden_out = joined(
        [mix_got, up_got, down_got],
        [sent(i, lay1[i][1], 3) for i in range(3)],
        to_each(small),
        from_own(dh),
        from_own(out),
    )
    small = jnp.sum(small.astype(F32), axis=0).reshape(-1)
    rows = small[:768].reshape(12, 64).T.reshape(64, LAYERS, 6)
    cols = small[768:864].reshape(24, 4).T.reshape(4, LAYERS, 12)
    lay0 = [halves(g[0], r) for g, r in zip((gmix0, gup0, gdown0), got)]
    got, lay1 = joined(
        [sent(i, lay0[i][1], 4) for i in range(3)],
        [plus(s[0], g) for s, g in zip(lay1, got1)],
    )
    lay0 = [halves(s[0], g) for s, g in zip(lay0, got)]
    (got,) = joined([sent(i, lay0[i][1], 3) for i in range(3)])
    both = [
        tuple(jnp.stack([plus(s[0][k], g[k]), s1[k]], axis=2) for k in (0, 1))
        for s, g, s1 in zip(lay0, got, lay1)
    ]
    for n in (2, 1):
        (got,) = joined([sent(i, both[i][1], n) for i in range(3)])
        both = [halves(s[0], g) for s, g in zip(both, got)]
    (got,) = joined([sent(i, both[i][1], 0) for i in range(3)])
    mixes, ups, downs = (
        jnp.swapaxes(s[0].astype(F32) + g.astype(F32), 0, 1) for s, g in zip(both, got)
    )
    return (
        hidden_out,
        grad_in,
        mixes[:, :, :384].reshape(64, LAYERS, 3, 128),
        mixes[:, :, 384:],
        ups,
        downs,
        cols[:, :, :4].reshape(4, LAYERS, 2, 2),
        cols[:, :, 4:],
        rows[:, :, :2],
        rows[:, :, 2:],
    )


def solution(mesh):
    torus = Mesh(mesh.devices.reshape(SIZES), AXES)
    token = P((*DP, *TENSOR), None)
    placed = (
        token,
        P(DP, None, None, TENSOR),
        P(DP, None, TENSOR),
        P(DP, None, TENSOR),
        P(DP, None, TENSOR),
        P(DP, None, None, TENSOR),
        P(DP, None, TENSOR),
        P(DP, None, None),
        P(DP, None, None),
        token,
    )
    outs = (token, token, *placed[1:9])
    return jax.shard_map(shards, mesh=torus, in_specs=placed, out_specs=outs, check_vma=False)
```

```python
import itertools
from functools import partial

import jax
import jax.numpy as jnp
import numpy as np
from jax import lax
from jax.experimental import pallas as pl
from jax.experimental.pallas import tpu as pltpu
from jax.sharding import Mesh
from jax.sharding import PartitionSpec as P

AXES = ("ylo", "z", "core", "x", "yhi")
SIZES = (2, 4, 2, 4, 2)
DP = ("ylo", "z", "core")
TENSOR = ("x", "yhi")
ORDERS = ("xyz", "yzx", "zxy")
LAYERS = 2
COMMON = 4
TOK = 160
D = 1024
HEADS = 16
EPS = 1e-05
BF, F32 = jnp.bfloat16, jnp.float32
HIGH = lax.Precision.HIGHEST


def pairs(axis, step):
    out = []
    for ylo, z, core, x, yhi in itertools.product(*map(range, SIZES)):
        c = {"x": x, "y": 2 * yhi + ylo, "z": z, "core": core}
        if axis == "core":
            c["core"] ^= 1
        else:
            c[axis] ^= 1 if (step == 1) == (core == 0) else 3
        src = np.ravel_multi_index((ylo, z, core, x, yhi), SIZES)
        dst = np.ravel_multi_index((c["y"] & 1, c["z"], c["core"], c["x"], c["y"] >> 1), SIZES)
        out.append((int(src), int(dst)))
    return out


def swap(v, axis, step=0):
    return lax.ppermute(v, AXES, pairs(axis, step))


def joined(*values):
    return lax.optimization_barrier(values)


def exchange(bufs, n):
    return [swap(b, ORDERS[i][n // 2], n % 2 + 1) for i, b in enumerate(bufs)]


def doubled(bufs, recv):
    return [lax.optimization_barrier(jnp.stack([b, r])) for b, r in zip(bufs, recv)]


def over_cores(values):
    return [swap(v, "core") for v in values]


def over_cores_in_turn(values):
    one, two = over_cores(values[:2])
    one, last = joined(one, values[2])
    return [one, two, swap(last, "core")]


def to_each(v):
    return lax.all_to_all(v, AXES, 0, 0, tiled=True)


def plus(a, b):
    return (a.astype(F32) + b.astype(F32)).astype(BF)


def halves(lo, recv):
    hi, lo, recv = joined(plus(lo[1], recv[1]), lo, recv)
    return plus(lo[0], recv[0]), hi


def norm(h):
    center = jnp.mean(h, axis=-1, keepdims=True)
    c = h - center
    var = jnp.mean(c * c, axis=-1, keepdims=True)
    inv = lax.rsqrt(var + EPS)
    return c * inv, inv


def dot(a, b):
    return lax.dot_general(a, b, (((1,), (0,)), ((), ())), preferred_element_type=F32)


def dot_nt(a, b):
    return lax.dot_general(a, b, (((1,), (1,)), ((), ())), preferred_element_type=F32)


def dot_tn(a, b):
    return lax.dot_general(a, b, (((0,), (0,)), ((), ())), preferred_element_type=F32)


def turned(x):
    return jnp.transpose(x.astype(F32)).astype(BF)


BITS = tuple(itertools.product((0, 1), repeat=2))


def placed_at(core, half, y2, y1):
    if y1 == y2:
        return y1
    c = core if half == 0 else 1 - core
    return c if y1 else 1 - c


def each_block(part, step, quad):
    a, b = step // 2, step % 2
    for half in range(len(quad) // 2):
        lo, hi = quad[2 * half], quad[2 * half + 1]
        for (z2, z1), (y2, y1) in itertools.product(BITS, BITS):
            row = half * 8 + (y1 ^ y2) * 4 + z2 * 2 + z1
            if part == 0:
                yield None, half, y2, y1, row, (lo, hi)[z2], (z1 * 4 + y2 * 2 + y1, 0)
            elif part == 2:
                yield None, half, y2, y1, row, (lo, hi)[y2], (y1, 0, z2 * 2 + z1)
            else:
                which = a if half == 0 else b
                for x2 in (0, 1):
                    yield which == x2, half, y2, y1, row, (lo, hi)[x2], (0, z2 * 2 + z1, y2 * 2 + y1)


def by_condition(part, step, quad, fn):
    if part != 1:
        for _, *rest in each_block(part, step, quad):
            fn(*rest)
        return
    groups = {}
    for cond, half, *rest in each_block(part, step, quad):
        groups.setdefault((half, id(rest[3])), (cond, []))[1].append((half, *rest))
    for cond, items in groups.values():

        @pl.when(cond)
        def _(items=items):
            for it in items:
                fn(*it)


def assemble(part, step, core, quad, w_ref):
    def put(half, y2, y1, row, ref, index):
        w_ref[placed_at(core, half, y2, y1), row * 64 : row * 64 + 64, :] = ref[index]

    by_condition(part, step, quad, put)


def disassemble(part, step, core, quad, w_ref):
    def get(half, y2, y1, row, ref, index):
        ref[index] = w_ref[placed_at(core, half, y2, y1), row * 64 : row * 64 + 64, :]

    by_condition(part, step, quad, get)


def merged(part, quad):
    shape = {0: (8, 4, 64, 512), 1: (2, 4, 4, 64, 512), 2: (2, 4, 4, 64, 512)}[part]
    return tuple(q.reshape(shape) for q in quad)


def unmerged(quad):
    return tuple(q.reshape(2, 2, 2, 2, 2, 64, 512) for q in quad)


def quad_shapes(part):
    shape = {0: (8, 4, 64, 512), 1: (2, 4, 4, 64, 512), 2: (2, 4, 4, 64, 512)}[part]
    return [jax.ShapeDtypeStruct(shape, BF)] * 4


def quad_specs(part):
    def own(s):
        return s

    def oth(s):
        return (s % 2) * 2 + s // 2

    if part == 0:
        return [
            pl.BlockSpec((8, 1, 64, 512), lambda s, *_, f=f: (0, f(s), 0, 0))
            for f in (own, own, oth, oth)
        ]
    if part == 2:
        return [
            pl.BlockSpec((2, 1, 4, 64, 512), lambda s, *_, f=f: (0, f(s), 0, 0, 0))
            for f in (own, own, oth, oth)
        ]
    maps = (
        lambda s: jnp.minimum(s, 1),
        lambda s: jnp.maximum(s - 2, 0),
        lambda s: s // 2,
        lambda s: s // 2,
    )
    return [
        pl.BlockSpec((1, 4, 4, 64, 512), lambda s, *_, f=f: (f(s), 0, 0, 0, 0)) for f in maps
    ]


def whole(shape):
    zeros = (0,) * len(shape)
    return pl.BlockSpec(shape, lambda s, *_: zeros)


def per_step(shape):
    zeros = (0,) * (len(shape) - 1)
    return pl.BlockSpec((1, *shape[1:]), lambda s, *_: (s, *zeros))


def call(body, name, core, slopes, ins, in_specs, outs, out_specs, scratch):
    return pl.pallas_call(
        body,
        name=name,
        out_shape=outs,
        grid_spec=pltpu.PrefetchScalarGridSpec(
            num_scalar_prefetch=2,
            grid=(4,),
            in_specs=in_specs,
            out_specs=out_specs,
            scratch_shapes=scratch,
        ),
        cost_estimate=pl.CostEstimate(flops=1 << 20, transcendentals=0, bytes_accessed=1 << 18),
        compiler_params=pltpu.CompilerParams(
            dimension_semantics=("arbitrary",), vmem_limit_bytes=48 << 20
        ),
    )(core, slopes, *ins)


def sds(shape, dtype=F32):
    return jax.ShapeDtypeStruct(shape, dtype)


def scores_of(q, k, slope):
    s = dot_nt(q, k) * 0.125
    row = lax.broadcasted_iota(jnp.int32, (TOK, TOK), 0)
    col = lax.broadcasted_iota(jnp.int32, (TOK, TOK), 1)
    s = s + slope * (col - row).astype(F32)
    return jnp.where(col <= row, s, -jnp.inf)


def chance_of(q, k, slope):
    s = scores_of(q, k, slope)
    e = jnp.exp(s - jnp.max(s, axis=-1, keepdims=True))
    return e * (1.0 / jnp.sum(e, axis=-1, keepdims=True))


def attn_fwd_body(core_ref, slope_ref, h_ref, vec_ref, bias_ref, *rest):
    quad, (qkv_ref, ctx_ref, hm_ref), (w_ref, a_ref) = rest[:4], rest[4:7], rest[7:]
    s, core = pl.program_id(0), core_ref[0]

    @pl.when(s == 0)
    def _():
        n, _ = norm(h_ref[...])
        a_ref[...] = (n * vec_ref[0:1, :] + vec_ref[1:2, :]).astype(BF)
        hm_ref[...] = h_ref[...] + vec_ref[4:5, :]

    assemble(0, s, core, quad, w_ref)
    total = jnp.zeros((TOK, D), F32)
    for g in (0, 1):
        qkv = (dot(a_ref[...], w_ref[g, :, 0:384]) + bias_ref[0, g : g + 1, :]).astype(BF)
        qkv_ref[0, g] = qkv
        ctx = []
        for hd in (0, 1):
            q, k, v = (qkv[:, j * 128 + hd * 64 : j * 128 + hd * 64 + 64] for j in range(3))
            p = chance_of(q, k, slope_ref[s * 4 + g * 2 + hd]).astype(BF)
            ctx.append(dot(p, v))
        ctx = jnp.concatenate(ctx, axis=1).astype(BF)
        ctx_ref[0, g] = ctx
        total = total + dot_nt(ctx, w_ref[g, :, 384:512])
    hm_ref[...] += total


def attn_fwd(core, slopes, h, vec, bias, quad):
    return call(
        attn_fwd_body,
        "attn_fwd",
        core,
        slopes,
        (h, vec, bias, *merged(0, quad)),
        [whole((TOK, D)), whole((8, D)), per_step((4, 2, 384))] + quad_specs(0),
        [sds((4, 2, TOK, 384), BF), sds((4, 2, TOK, 128), BF), sds((TOK, D))],
        [per_step((4, 2, TOK, 384)), per_step((4, 2, TOK, 128)), whole((TOK, D))],
        [pltpu.VMEM((2, D, 512), BF), pltpu.VMEM((TOK, D), BF)],
    )


C0, C1 = 0.7978845608, 0.044715


def gelu_parts(u):
    t = jnp.tanh(C0 * (u + C1 * (u * u * u)))
    return 0.5 * u * (1.0 + t), t


def feed_fwd_body(core_ref, slope_ref, hm_ref, vec_ref, bias_ref, *rest):
    up, down, (u_ref, out_ref), (wu_ref, wd_ref, m_ref) = rest[:4], rest[4:8], rest[8:10], rest[10:]
    s, core = pl.program_id(0), core_ref[0]

    @pl.when(s == 0)
    def _():
        n, _ = norm(hm_ref[...])
        m_ref[...] = (n * vec_ref[2:3, :] + vec_ref[3:4, :]).astype(BF)
        out_ref[...] = hm_ref[...] + vec_ref[5:6, :]

    assemble(1, s, core, up, wu_ref)
    assemble(2, s, core, down, wd_ref)
    total = jnp.zeros((TOK, D), F32)
    for g in (0, 1):
        u = dot(m_ref[...], wu_ref[g]) + bias_ref[0, g : g + 1, :]
        u_ref[0, g] = u
        act, _ = gelu_parts(u)
        total = total + dot_nt(act.astype(BF), wd_ref[g])
    out_ref[...] += total


def feed_fwd(core, slopes, hm, vec, bias, up, down):
    return call(
        feed_fwd_body,
        "feed_fwd",
        core,
        slopes,
        (hm, vec, bias, *merged(1, up), *merged(2, down)),
        [whole((TOK, D)), whole((8, D)), per_step((4, 2, 512))] + quad_specs(1) + quad_specs(2),
        [sds((4, 2, TOK, 512)), sds((TOK, D))],
        [per_step((4, 2, TOK, 512)), whole((TOK, D))],
        [pltpu.VMEM((2, D, 512), BF), pltpu.VMEM((2, D, 512), BF), pltpu.VMEM((TOK, D), BF)],
    )


def norm_back(up, n, inv, gain):
    scaled = up * gain
    center = jnp.mean(scaled, axis=-1, keepdims=True)
    spread = jnp.mean(scaled * n, axis=-1, keepdims=True)
    return inv * (scaled - center - n * spread)


def col_sum(x):
    return jnp.sum(x, axis=0, keepdims=True)


def keep_halves(own_ref, oth_ref, i, x):
    own_ref[i] = x[:, :512]
    oth_ref[i] = x[:, 512:]


def feed_bwd_body(core_ref, slope_ref, dh_ref, hm_ref, vec_ref, u_ref, *rest):
    up, down = rest[:4], rest[4:8]
    dhm_ref, gbu_ref, gvec_ref, ad_ref, own_ref, oth_ref = rest[8:14]
    wu_ref, wd_ref, dm_ref = rest[14:]
    s, core = pl.program_id(0), core_ref[0]
    dy = dh_ref[...].astype(BF)

    @pl.when(s == 0)
    def _():
        n, _ = norm(hm_ref[...])
        m = (n * vec_ref[2:3, :] + vec_ref[3:4, :]).astype(BF)
        keep_halves(own_ref, oth_ref, 0, m)
        keep_halves(own_ref, oth_ref, 1, dy)
        dm_ref[...] = jnp.zeros((TOK, D), F32)

    assemble(1, s, core, up, wu_ref)
    assemble(2, s, core, down, wd_ref)
    total = jnp.zeros((TOK, D), F32)
    for g in (0, 1):
        u = u_ref[0, g]
        act, t = gelu_parts(u)
        slope = 0.5 * (1.0 + t) + (0.5 * C0) * u * (1.0 - t * t) * (1.0 + (3.0 * C1) * (u * u))
        du = dot(dy, wd_ref[g]) * slope
        gbu_ref[0, g : g + 1, :] = col_sum(du)
        dub = du.astype(BF)
        ad_ref[0, g, 0] = dub
        ad_ref[0, g, 1] = act.astype(BF)
        total = total + dot_nt(dub, wu_ref[g])
    dm_ref[...] += total

    @pl.when(s == 3)
    def _():
        n, inv = norm(hm_ref[...])
        dm, dh = dm_ref[...], dh_ref[...]
        dhm_ref[...] = dh + norm_back(dm, n, inv, vec_ref[2:3, :])
        gvec_ref[...] = jnp.zeros((8, D), F32)
        gvec_ref[0:1, :] = col_sum(dm * n)
        gvec_ref[1:2, :] = col_sum(dm)
        gvec_ref[2:3, :] = col_sum(dh)


def feed_bwd(core, slopes, dh, hm, vec, u, up, down):
    half = (2, TOK, 512)
    return call(
        feed_bwd_body,
        "feed_bwd",
        core,
        slopes,
        (dh, hm, vec, u, *merged(1, up), *merged(2, down)),
        [whole((TOK, D)), whole((TOK, D)), whole((8, D)), per_step((4, 2, TOK, 512))]
        + quad_specs(1)
        + quad_specs(2),
        [sds((TOK, D)), sds((4, 2, 512)), sds((8, D)), sds((4, 2, 2, TOK, 512), BF)]
        + [sds(half, BF)] * 2,
        [whole((TOK, D)), per_step((4, 2, 512)), whole((8, D)), per_step((4, 2, 2, TOK, 512))]
        + [whole(half)] * 2,
        [pltpu.VMEM((2, D, 512), BF)] * 2 + [pltpu.VMEM((TOK, D), F32)],
    )


def attn_bwd_body(core_ref, slope_ref, dhm_ref, h_ref, vec_ref, qkv_ref, ctx_ref, *rest):
    quad, (dh_ref, gqv_ref, gvec_ref, dc_ref, own_ref, oth_ref) = rest[:4], rest[4:10]
    w_ref, da_ref = rest[10:]
    s, core = pl.program_id(0), core_ref[0]
    dz = dhm_ref[...].astype(BF)

    @pl.when(s == 0)
    def _():
        n, _ = norm(h_ref[...])
        a = (n * vec_ref[0:1, :] + vec_ref[1:2, :]).astype(BF)
        keep_halves(own_ref, oth_ref, 0, a)
        keep_halves(own_ref, oth_ref, 1, dz)
        da_ref[...] = jnp.zeros((TOK, D), F32)

    assemble(0, s, core, quad, w_ref)
    total = jnp.zeros((TOK, D), F32)
    for g in (0, 1):
        qkv = qkv_ref[0, g]
        dctx = dot(dz, w_ref[g, :, 384:512]).astype(BF)
        grads = [[], [], []]
        for hd in (0, 1):
            q, k, v = (qkv[:, j * 128 + hd * 64 : j * 128 + hd * 64 + 64] for j in range(3))
            dc = dctx[:, hd * 64 : hd * 64 + 64]
            p = chance_of(q, k, slope_ref[s * 4 + g * 2 + hd])
            dp = dot_nt(dc, v)
            delta = jnp.sum(p * dp, axis=-1, keepdims=True)
            ds = (p * (dp - delta) * 0.125).astype(BF)
            grads[0].append(dot(ds, k))
            grads[1].append(dot_tn(ds, q))
            grads[2].append(dot_tn(p.astype(BF), dc))
        dqkv = jnp.concatenate([g_ for three in grads for g_ in three], axis=1)
        gqv_ref[0, g : g + 1, :] = col_sum(dqkv)
        dqkv = dqkv.astype(BF)
        dc_ref[0, g, :, 0:384] = dqkv
        dc_ref[0, g, :, 384:512] = ctx_ref[0, g]
        total = total + dot_nt(dqkv, w_ref[g, :, 0:384])
    da_ref[...] += total

    @pl.when(s == 3)
    def _():
        n, inv = norm(h_ref[...])
        da, dhm = da_ref[...], dhm_ref[...]
        dh_ref[...] = dhm + norm_back(da, n, inv, vec_ref[0:1, :])
        gvec_ref[...] = jnp.zeros((8, D), F32)
        gvec_ref[0:1, :] = col_sum(da * n)
        gvec_ref[1:2, :] = col_sum(da)
        gvec_ref[2:3, :] = col_sum(dhm)


def attn_bwd(core, slopes, dhm, h, vec, qkv, ctx, quad):
    half = (2, TOK, 512)
    return call(
        attn_bwd_body,
        "attn_bwd",
        core,
        slopes,
        (dhm, h, vec, qkv, ctx, *merged(0, quad)),
        [
            whole((TOK, D)),
            whole((TOK, D)),
            whole((8, D)),
            per_step((4, 2, TOK, 384)),
            per_step((4, 2, TOK, 128)),
        ]
        + quad_specs(0),
        [sds((TOK, D)), sds((4, 2, 384)), sds((8, D)), sds((4, 2, TOK, 512), BF)]
        + [sds(half, BF)] * 2,
        [whole((TOK, D)), per_step((4, 2, 384)), whole((8, D)), per_step((4, 2, TOK, 512))]
        + [whole(half)] * 2,
        [pltpu.VMEM((2, D, 512), BF), pltpu.VMEM((TOK, D), F32)],
    )


def both_tokens(mine, theirs):
    return turned(jnp.concatenate([mine, theirs], axis=0))


def feed_grad_body(core_ref, slope_ref, ad_ref, ad2_ref, own_ref, own2_ref, *rest):
    gup, gdown, (mt_ref, dyt_ref, gu_ref, gd_ref) = rest[:2], rest[2:4], rest[4:]
    s, core = pl.program_id(0), core_ref[0]

    @pl.when(s == 0)
    def _():
        mt_ref[...] = both_tokens(own_ref[0], own2_ref[0])
        dyt_ref[...] = both_tokens(own_ref[1], own2_ref[1])

    for g in (0, 1):
        du = jnp.concatenate([ad_ref[0, g, 0], ad2_ref[0, g, 0]], axis=0)
        act = jnp.concatenate([ad_ref[0, g, 1], ad2_ref[0, g, 1]], axis=0)
        gu_ref[g] = dot(mt_ref[...], du).astype(BF)
        gd_ref[g] = dot(dyt_ref[...], act).astype(BF)
    disassemble(1, s, core, gup, gu_ref)
    disassemble(2, s, core, gdown, gd_ref)


def attn_grad_body(core_ref, slope_ref, dc_ref, dc2_ref, own_ref, own2_ref, *rest):
    gmix, (at_ref, dzt_ref, gw_ref) = rest[:2], rest[2:]
    s, core = pl.program_id(0), core_ref[0]

    @pl.when(s == 0)
    def _():
        at_ref[...] = both_tokens(own_ref[0], own2_ref[0])
        dzt_ref[...] = both_tokens(own_ref[1], own2_ref[1])

    for g in (0, 1):
        dc = jnp.concatenate([dc_ref[0, g], dc2_ref[0, g]], axis=0)
        gw_ref[g, :, 0:384] = dot(at_ref[...], dc[:, 0:384]).astype(BF)
        gw_ref[g, :, 384:512] = dot(dzt_ref[...], dc[:, 384:512]).astype(BF)
    disassemble(0, s, core, gmix, gw_ref)


def weight_grads(body, name, parts, core, slopes, cols, cols2, rows, rows2):
    zeros = (0,) * (cols.ndim - 1)
    crossed = pl.BlockSpec((1, *cols.shape[1:]), lambda s, *_: ((s % 2) * 2 + s // 2, *zeros))
    outs = call(
        body,
        name,
        core,
        slopes,
        (cols, cols2, rows, rows2),
        [per_step(cols.shape), crossed, whole(rows.shape), whole(rows.shape)],
        [v for part in parts for v in quad_shapes(part)[:2]],
        [v for part in parts for v in quad_specs(part)[:2]],
        [pltpu.VMEM((512, 2 * TOK), BF)] * 2 + [pltpu.VMEM((2, 512, 512), BF)] * len(parts),
    )
    return [unmerged(outs[2 * i : 2 * i + 2]) for i in range(len(parts))]


def orders():
    at = {a: lax.axis_index(a) for a in AXES}
    rows = []
    for half, low, z2, z1 in itertools.product((0, 1), repeat=4):
        core = at["core"] ^ half
        z = at["z"] ^ jnp.where(core == 0, z1 ^ (3 * z2), (3 * z1) ^ z2)
        rows.append(((at["ylo"] ^ low) * 4 + z) * 2 + core)
    cols = []
    for x2, x1, g in itertools.product((0, 1), repeat=3):
        x = at["x"] ^ jnp.where(at["core"] == 0, x1 ^ (3 * x2), (3 * x1) ^ x2)
        cols.append(x * 2 + (at["yhi"] ^ g))
    return at, jnp.stack(rows), jnp.stack(cols)


def one_hot(index, count):
    return (index[:, None] == jnp.arange(count)[None, :]).astype(F32)


def shards(
    hidden_in, w_qkv, w_attn_out, w_up, w_down, qv_bias, up_bias, ln_gain, row_bias, cotangent
):
    at, rows, cols = orders()
    core = at["core"].reshape(1).astype(jnp.int32)
    lanes = (rows[:, None] * 64 + jnp.arange(64)[None, :]).reshape(-1)
    lane_hot = one_hot(lanes, D)

    def to_own(v):
        return lax.dot_general(v, lane_hot, (((1,), (1,)), ((), ())), precision=HIGH)

    def from_own(v):
        return jnp.dot(v, lane_hot, precision=HIGH)

    heads = cols[:, None] * 2 + jnp.arange(2)[None, :]
    slopes = jnp.exp2(-8.0 * (heads.astype(F32) + 1.0) / HEADS).reshape(-1)

    p = (at["ylo"] * 4 + at["z"]) * 2 + at["core"]
    col_hot = one_hot(cols, 8)
    own_rows = jnp.concatenate([ln_gain.reshape(64, 4), row_bias.reshape(64, 8)], axis=1)
    own_cols = jnp.concatenate([qv_bias.reshape(4, 2, 4), up_bias], axis=2).reshape(4, 24)
    small = jnp.concatenate([own_rows.T.reshape(-1), own_cols.T.reshape(-1)])
    small = jnp.pad(small, (0, 160)).reshape(8, 128)
    at_row = jnp.arange(1536)
    moved = (at_row % 96) // 4 * 64 + at_row // 96 * 4 + at_row % 4
    move = (moved[:, None] == at_row[None, :]).astype(BF)

    def unpacked(small):
        small = small.reshape(16, 8, 8, 128)
        whole_rows = small[:, 0, :6].reshape(16, 12, 64).swapaxes(0, 1).reshape(12, D)
        whole_rows = to_own(whole_rows.astype(F32))
        gains, shifts = whole_rows[:4].reshape(2, 2, D), whole_rows[4:].reshape(2, 4, D)
        whole_cols = dot(small[:, :, 6, :96].swapaxes(0, 1).reshape(8, 1536), move)
        whole_cols = jnp.dot(col_hot, whole_cols, precision=HIGH)
        whole_cols = whole_cols.reshape(4, 2, LAYERS, 12, 64)
        vecs, qkv_shifts, up_shifts = [], [], []
        for l in range(LAYERS):
            vecs.append(
                jnp.concatenate(
                    [gains[l, 0:1], shifts[l, 0:1], gains[l, 1:2], shifts[l, 1:4]]
                    + [jnp.zeros((2, D), F32)]
                )
            )
            qv = whole_cols[:, :, l, :4].reshape(4, 2, 2, 128)
            qkv_shifts.append(
                jnp.concatenate([qv[:, :, 0], jnp.zeros((4, 2, 128), F32), qv[:, :, 1]], axis=2)
            )
            up_shifts.append(whole_cols[:, :, l, 4:].reshape(4, 2, 512))
        return vecs, qkv_shifts, up_shifts

    h, dh = to_own(hidden_in), to_own(cotangent)
    bufs = joined(
        jnp.concatenate([w_qkv.reshape(64, LAYERS, 384), w_attn_out], axis=2).swapaxes(0, 1),
        w_up.swapaxes(0, 1),
        w_down.swapaxes(0, 1),
    )
    for n in range(COMMON):
        (recv,) = joined(exchange(bufs, n))
        bufs = doubled(bufs, recv)
    first, second = ([b[..., l, :, :] for b in bufs] for l in range(LAYERS))

    recv, h, dh = joined(exchange(first, 4), h, dh)
    first = doubled(first, recv)
    first_hi, first_oth, small = joined(
        exchange(first, 5),
        over_cores_in_turn(first),
        to_each(jnp.broadcast_to(small[None], (128, 8, 128))),
    )

    second, mix_oth, first_hi, small = joined(
        second, swap(first_hi[0], "core"), first_hi, unpacked(small)
    )
    vecs, qkv_shifts, up_shifts = small
    mix0 = (first[0], first_hi[0], first_oth[0], mix_oth)
    (qkv0, ctx0, hm0), rest_oth, recv = joined(
        attn_fwd(core, slopes, h, vecs[0], qkv_shifts[0], mix0),
        over_cores(first_hi[1:]),
        exchange(second, 4),
    )
    second = doubled(second, recv)
    up0, down0 = ((first[i], first_hi[i], first_oth[i], rest_oth[i - 1]) for i in (1, 2))
    (u0, h1), second_hi, second_oth = joined(
        feed_fwd(core, slopes, hm0, vecs[0], up_shifts[0], up0, down0),
        exchange(second, 5),
        over_cores_in_turn(second),
    )
    h1, mix_oth, second_hi = joined(h1, swap(second_hi[0], "core"), second_hi)
    mix1 = (second[0], second_hi[0], second_oth[0], mix_oth)
    (qkv1, ctx1, hm1), rest_oth = joined(
        attn_fwd(core, slopes, h1, vecs[1], qkv_shifts[1], mix1), over_cores(second_hi[1:])
    )
    up1, down1 = ((second[i], second_hi[i], second_oth[i], rest_oth[i - 1]) for i in (1, 2))
    u1, out = feed_fwd(core, slopes, hm1, vecs[1], up_shifts[1], up1, down1)

    def sent(part, hi, n):
        return swap(hi, ORDERS[part][n // 2], n % 2 + 1)

    feed_grads = partial(weight_grads, feed_grad_body, "feed_grad", (1, 2), core, slopes)
    attn_grads = partial(weight_grads, attn_grad_body, "attn_grad", (0,), core, slopes)

    dhm1, gbu1, gvec21, ad1, md1, md1_oth = feed_bwd(core, slopes, dh, hm1, vecs[1], u1, up1, down1)
    (dh, gqv1, gvec11, dc1, az1, az1_oth), ad1_got, md1_got = joined(
        attn_bwd(core, slopes, dhm1, h1, vecs[1], qkv1, ctx1, mix1),
        swap(ad1, "core"),
        swap(md1_oth, "core"),
    )
    (gup1, gdown1), dc1_got, az1_got = joined(
        feed_grads(ad1, ad1_got, md1, md1_got), swap(dc1, "core"), swap(az1_oth, "core")
    )
    up_got, down_got = sent(1, gup1[1], 5), sent(2, gdown1[1], 5)
    (gmix1,) = attn_grads(dc1, dc1_got, az1, az1_got)
    dh, gmix1 = joined(dh, gmix1)
    mix_got = sent(0, gmix1[1], 5)
    dhm0, gbu0, gvec20, ad0, md0, md0_oth = feed_bwd(core, slopes, dh, hm0, vecs[0], u0, up0, down0)
    (dh, gqv0, gvec10, dc0, az0, az0_oth), ad0_got, md0_got, got = joined(
        attn_bwd(core, slopes, dhm0, h, vecs[0], qkv0, ctx0, mix0),
        swap(ad0, "core"),
        swap(md0_oth, "core"),
        [mix_got, up_got, down_got],
    )
    his = [plus(g[0][1], r[1]) for g, r in zip((gmix1, gup1, gdown1), got)]
    ad0, his = joined(ad0, his)
    (gup0, gdown0), dc0_got, az0_got, got1, lay1 = joined(
        feed_grads(ad0, ad0_got, md0, md0_got),
        swap(dc0, "core"),
        swap(az0_oth, "core"),
        [sent(i, his[i], 4) for i in range(3)],
        [(g[0][0], r[0]) for g, r in zip((gmix1, gup1, gdown1), got)],
    )
    up_got, down_got = sent(1, gup0[1], 5), sent(2, gdown0[1], 5)
    (gmix0,) = attn_grads(dc0, dc0_got, az0, az0_got)
    mix_got = sent(0, gmix0[1], 5)
    rows = jnp.concatenate(
        [
            v
            for v1, v2 in ((gvec10, gvec20), (gvec11, gvec21))
            for v in (v1[0:1], v2[0:1], v1[1:2], v2[1:2], v1[2:3], v2[2:3])
        ]
    )
    cols = jnp.concatenate(
        [
            v
            for gqv, gbu in ((gqv0, gbu0), (gqv1, gbu1))
            for v in (gqv[:, :, :128], gqv[:, :, 256:], gbu)
        ],
        axis=2,
    ).reshape(8, 1536)
    rows = dot(rows.astype(BF), lane_hot.astype(BF)).astype(BF)
    rows = rows.reshape(12, 16, 64).swapaxes(0, 1).reshape(16, 1, 768)
    cols = dot_nt(dot_tn(col_hot.astype(BF), cols.astype(BF)).astype(BF), move).astype(BF)
    cols = cols.reshape(8, 16, 96).swapaxes(0, 1)
    small = jnp.concatenate([jnp.broadcast_to(rows, (16, 8, 768)), cols], axis=2)
    small = jnp.pad(small, ((0, 0), (0, 0), (0, 160))).reshape(128, 8, 128)
    dc0, lay1, got1 = joined(dc0, lay1, got1)
    got, small, grad_in, hidden_out, lay1 = joined(
        [mix_got, up_got, down_got],
        to_each(small),
        from_own(dh),
        from_own(out),
        [plus(plus(*v), r) for v, r in zip(lay1, got1)],
    )
    small = jnp.sum(small.astype(F32), axis=0).reshape(-1)
    rows = small[:768].reshape(12, 64).T.reshape(64, LAYERS, 6)
    cols = small[768:864].reshape(24, 4).T.reshape(4, LAYERS, 12)
    lay0 = [halves(g[0], r) for g, r in zip((gmix0, gup0, gdown0), got)]
    (got,) = joined([sent(i, lay0[i][1], 4) for i in range(3)])
    both = []
    for (lo, _), r, s1 in zip(lay0, got, lay1):
        hi, lo, r, s1 = joined(jnp.stack([plus(lo[1], r[1]), s1[1]], axis=3), lo, r, s1)
        both.append((jnp.stack([plus(lo[0], r[0]), s1[0]], axis=3), hi))
    for n in (3, 2, 1):
        (got,) = joined([sent(i, both[i][1], n) for i in range(3)])
        both = [halves(s[0], g) for s, g in zip(both, got)]
    (got,) = joined([sent(i, both[i][1], 0) for i in range(3)])
    mixes, ups, downs = (
        jnp.swapaxes(s[0].astype(F32) + g.astype(F32), 0, 1) for s, g in zip(both, got)
    )
    return (
        hidden_out,
        grad_in,
        mixes[:, :, :384].reshape(64, LAYERS, 3, 128),
        mixes[:, :, 384:],
        ups,
        downs,
        cols[:, :, :4].reshape(4, LAYERS, 2, 2),
        cols[:, :, 4:],
        rows[:, :, :2],
        rows[:, :, 2:],
    )


def solution(mesh):
    torus = Mesh(mesh.devices.reshape(SIZES), AXES)
    token = P((*DP, *TENSOR), None)
    placed = (
        token,
        P(DP, None, None, TENSOR),
        P(DP, None, TENSOR),
        P(DP, None, TENSOR),
        P(DP, None, TENSOR),
        P(DP, None, None, TENSOR),
        P(DP, None, TENSOR),
        P(DP, None, None),
        P(DP, None, None),
        token,
    )
    outs = (token, token, *placed[1:9])
    return jax.shard_map(shards, mesh=torus, in_specs=placed, out_specs=outs, check_vma=False)
```

```python
import itertools
from functools import partial

import jax
import jax.numpy as jnp
import numpy as np
from jax import lax
from jax.experimental import pallas as pl
from jax.experimental.pallas import tpu as pltpu
from jax.sharding import Mesh
from jax.sharding import PartitionSpec as P

AXES = ("ylo", "z", "core", "x", "yhi")
SIZES = (2, 4, 2, 4, 2)
DP = ("ylo", "z", "core")
TENSOR = ("x", "yhi")
ORDERS = ("xyz", "yzx", "zxy")
LAYERS = 2
COMMON = 4
TOK = 160
D = 1024
HEADS = 16
EPS = 1e-05
BF, F32 = jnp.bfloat16, jnp.float32
HIGH = lax.Precision.HIGHEST


def pairs(axis, step):
    out = []
    for ylo, z, core, x, yhi in itertools.product(*map(range, SIZES)):
        c = {"x": x, "y": 2 * yhi + ylo, "z": z, "core": core}
        if axis == "core":
            c["core"] ^= 1
        else:
            c[axis] ^= 1 if (step == 1) == (core == 0) else 3
        src = np.ravel_multi_index((ylo, z, core, x, yhi), SIZES)
        dst = np.ravel_multi_index((c["y"] & 1, c["z"], c["core"], c["x"], c["y"] >> 1), SIZES)
        out.append((int(src), int(dst)))
    return out


def swap(v, axis, step=0):
    return lax.ppermute(v, AXES, pairs(axis, step))


def joined(*values):
    return lax.optimization_barrier(values)


def exchange(bufs, n):
    return [swap(b, ORDERS[i][n // 2], n % 2 + 1) for i, b in enumerate(bufs)]


def doubled(bufs, recv):
    return [lax.optimization_barrier(jnp.stack([b, r])) for b, r in zip(bufs, recv)]


def over_cores(values):
    return [swap(v, "core") for v in values]


def over_cores_in_turn(values):
    one, two = over_cores(values[:2])
    one, last = joined(one, values[2])
    return [one, two, swap(last, "core")]


def to_each(v):
    return lax.all_to_all(v, AXES, 0, 0, tiled=True)


def plus(a, b):
    return (a.astype(F32) + b.astype(F32)).astype(BF)


def halves(lo, recv):
    hi, lo, recv = joined(plus(lo[1], recv[1]), lo, recv)
    return plus(lo[0], recv[0]), hi


def norm(h):
    center = jnp.mean(h, axis=-1, keepdims=True)
    c = h - center
    var = jnp.mean(c * c, axis=-1, keepdims=True)
    inv = lax.rsqrt(var + EPS)
    return c * inv, inv


def dot(a, b):
    return lax.dot_general(a, b, (((1,), (0,)), ((), ())), preferred_element_type=F32)


def dot_nt(a, b):
    return lax.dot_general(a, b, (((1,), (1,)), ((), ())), preferred_element_type=F32)


def dot_tn(a, b):
    return lax.dot_general(a, b, (((0,), (0,)), ((), ())), preferred_element_type=F32)


def turned(x):
    return jnp.transpose(x.astype(F32)).astype(BF)


BITS = tuple(itertools.product((0, 1), repeat=2))


def placed_at(core, half, y2, y1):
    if y1 == y2:
        return y1
    c = core if half == 0 else 1 - core
    return c if y1 else 1 - c


def each_block(part, step, quad):
    a, b = step // 2, step % 2
    for half in range(len(quad) // 2):
        lo, hi = quad[2 * half], quad[2 * half + 1]
        for (z2, z1), (y2, y1) in itertools.product(BITS, BITS):
            row = half * 8 + (y1 ^ y2) * 4 + z2 * 2 + z1
            if part == 0:
                yield None, half, y2, y1, row, (lo, hi)[z2], (z1 * 4 + y2 * 2 + y1, 0)
            elif part == 2:
                yield None, half, y2, y1, row, (lo, hi)[y2], (y1, 0, z2 * 2 + z1)
            else:
                which = a if half == 0 else b
                for x2 in (0, 1):
                    yield which == x2, half, y2, y1, row, (lo, hi)[x2], (0, z2 * 2 + z1, y2 * 2 + y1)


def by_condition(part, step, quad, fn):
    if part != 1:
        for _, *rest in each_block(part, step, quad):
            fn(*rest)
        return
    groups = {}
    for cond, half, *rest in each_block(part, step, quad):
        groups.setdefault((half, id(rest[3])), (cond, []))[1].append((half, *rest))
    for cond, items in groups.values():

        @pl.when(cond)
        def _(items=items):
            for it in items:
                fn(*it)


def assemble(part, step, core, quad, w_ref):
    def put(half, y2, y1, row, ref, index):
        w_ref[placed_at(core, half, y2, y1), row * 64 : row * 64 + 64, :] = ref[index]

    by_condition(part, step, quad, put)


def disassemble(part, step, core, quad, w_ref):
    def get(half, y2, y1, row, ref, index):
        ref[index] = w_ref[placed_at(core, half, y2, y1), row * 64 : row * 64 + 64, :]

    by_condition(part, step, quad, get)


def merged(part, quad):
    shape = {0: (8, 4, 64, 512), 1: (2, 4, 4, 64, 512), 2: (2, 4, 4, 64, 512)}[part]
    return tuple(q.reshape(shape) for q in quad)


def unmerged(quad):
    return tuple(q.reshape(2, 2, 2, 2, 2, 64, 512) for q in quad)


def quad_shapes(part):
    shape = {0: (8, 4, 64, 512), 1: (2, 4, 4, 64, 512), 2: (2, 4, 4, 64, 512)}[part]
    return [jax.ShapeDtypeStruct(shape, BF)] * 4


def quad_specs(part):
    def own(s):
        return s

    def oth(s):
        return (s % 2) * 2 + s // 2

    if part == 0:
        return [
            pl.BlockSpec((8, 1, 64, 512), lambda s, *_, f=f: (0, f(s), 0, 0))
            for f in (own, own, oth, oth)
        ]
    if part == 2:
        return [
            pl.BlockSpec((2, 1, 4, 64, 512), lambda s, *_, f=f: (0, f(s), 0, 0, 0))
            for f in (own, own, oth, oth)
        ]
    maps = (
        lambda s: jnp.minimum(s, 1),
        lambda s: jnp.maximum(s - 2, 0),
        lambda s: s // 2,
        lambda s: s // 2,
    )
    return [
        pl.BlockSpec((1, 4, 4, 64, 512), lambda s, *_, f=f: (f(s), 0, 0, 0, 0)) for f in maps
    ]


def whole(shape):
    zeros = (0,) * len(shape)
    return pl.BlockSpec(shape, lambda s, *_: zeros)


def per_step(shape):
    zeros = (0,) * (len(shape) - 1)
    return pl.BlockSpec((1, *shape[1:]), lambda s, *_: (s, *zeros))


def call(body, name, core, slopes, ins, in_specs, outs, out_specs, scratch):
    return pl.pallas_call(
        body,
        name=name,
        out_shape=outs,
        grid_spec=pltpu.PrefetchScalarGridSpec(
            num_scalar_prefetch=2,
            grid=(4,),
            in_specs=in_specs,
            out_specs=out_specs,
            scratch_shapes=scratch,
        ),
        cost_estimate=pl.CostEstimate(flops=1 << 20, transcendentals=0, bytes_accessed=1 << 18),
        compiler_params=pltpu.CompilerParams(
            dimension_semantics=("arbitrary",), vmem_limit_bytes=48 << 20
        ),
    )(core, slopes, *ins)


def sds(shape, dtype=F32):
    return jax.ShapeDtypeStruct(shape, dtype)


def scores_of(q, k, slope):
    s = dot_nt(q, k) * 0.125
    row = lax.broadcasted_iota(jnp.int32, (TOK, TOK), 0)
    col = lax.broadcasted_iota(jnp.int32, (TOK, TOK), 1)
    s = s + slope * (col - row).astype(F32)
    return jnp.where(col <= row, s, -jnp.inf)


def chance_of(q, k, slope):
    s = scores_of(q, k, slope)
    e = jnp.exp(s - jnp.max(s, axis=-1, keepdims=True))
    return e * (1.0 / jnp.sum(e, axis=-1, keepdims=True))


def attn_fwd_body(core_ref, slope_ref, h_ref, vec_ref, bias_ref, *rest):
    quad, (qkv_ref, ctx_ref, hm_ref), (w_ref, a_ref) = rest[:4], rest[4:7], rest[7:]
    s, core = pl.program_id(0), core_ref[0]

    @pl.when(s == 0)
    def _():
        n, _ = norm(h_ref[...])
        a_ref[...] = (n * vec_ref[0:1, :] + vec_ref[1:2, :]).astype(BF)
        hm_ref[...] = h_ref[...] + vec_ref[4:5, :]

    assemble(0, s, core, quad, w_ref)
    total = jnp.zeros((TOK, D), F32)
    for g in (0, 1):
        qkv = (dot(a_ref[...], w_ref[g, :, 0:384]) + bias_ref[0, g : g + 1, :]).astype(BF)
        qkv_ref[0, g] = qkv
        ctx = []
        for hd in (0, 1):
            q, k, v = (qkv[:, j * 128 + hd * 64 : j * 128 + hd * 64 + 64] for j in range(3))
            p = chance_of(q, k, slope_ref[s * 4 + g * 2 + hd]).astype(BF)
            ctx.append(dot(p, v))
        ctx = jnp.concatenate(ctx, axis=1).astype(BF)
        ctx_ref[0, g] = ctx
        total = total + dot_nt(ctx, w_ref[g, :, 384:512])
    hm_ref[...] += total


def attn_fwd(core, slopes, h, vec, bias, quad):
    return call(
        attn_fwd_body,
        "attn_fwd",
        core,
        slopes,
        (h, vec, bias, *merged(0, quad)),
        [whole((TOK, D)), whole((8, D)), per_step((4, 2, 384))] + quad_specs(0),
        [sds((4, 2, TOK, 384), BF), sds((4, 2, TOK, 128), BF), sds((TOK, D))],
        [per_step((4, 2, TOK, 384)), per_step((4, 2, TOK, 128)), whole((TOK, D))],
        [pltpu.VMEM((2, D, 512), BF), pltpu.VMEM((TOK, D), BF)],
    )


C0, C1 = 0.7978845608, 0.044715


def gelu_parts(u):
    t = jnp.tanh(C0 * (u + C1 * (u * u * u)))
    return 0.5 * u * (1.0 + t), t


def feed_fwd_body(core_ref, slope_ref, hm_ref, vec_ref, bias_ref, *rest):
    up, down, (u_ref, out_ref), (wu_ref, wd_ref, m_ref) = rest[:4], rest[4:8], rest[8:10], rest[10:]
    s, core = pl.program_id(0), core_ref[0]

    @pl.when(s == 0)
    def _():
        n, _ = norm(hm_ref[...])
        m_ref[...] = (n * vec_ref[2:3, :] + vec_ref[3:4, :]).astype(BF)
        out_ref[...] = hm_ref[...] + vec_ref[5:6, :]

    assemble(1, s, core, up, wu_ref)
    assemble(2, s, core, down, wd_ref)
    total = jnp.zeros((TOK, D), F32)
    for g in (0, 1):
        u = dot(m_ref[...], wu_ref[g]) + bias_ref[0, g : g + 1, :]
        u_ref[0, g] = u
        act, _ = gelu_parts(u)
        total = total + dot_nt(act.astype(BF), wd_ref[g])
    out_ref[...] += total


def feed_fwd(core, slopes, hm, vec, bias, up, down):
    return call(
        feed_fwd_body,
        "feed_fwd",
        core,
        slopes,
        (hm, vec, bias, *merged(1, up), *merged(2, down)),
        [whole((TOK, D)), whole((8, D)), per_step((4, 2, 512))] + quad_specs(1) + quad_specs(2),
        [sds((4, 2, TOK, 512)), sds((TOK, D))],
        [per_step((4, 2, TOK, 512)), whole((TOK, D))],
        [pltpu.VMEM((2, D, 512), BF), pltpu.VMEM((2, D, 512), BF), pltpu.VMEM((TOK, D), BF)],
    )


def norm_back(up, n, inv, gain):
    scaled = up * gain
    center = jnp.mean(scaled, axis=-1, keepdims=True)
    spread = jnp.mean(scaled * n, axis=-1, keepdims=True)
    return inv * (scaled - center - n * spread)


def col_sum(x):
    return jnp.sum(x, axis=0, keepdims=True)


def keep_halves(own_ref, oth_ref, i, x):
    own_ref[i] = x[:, :512]
    oth_ref[i] = x[:, 512:]


def feed_bwd_body(core_ref, slope_ref, dh_ref, hm_ref, vec_ref, u_ref, *rest):
    up, down = rest[:4], rest[4:8]
    dhm_ref, gbu_ref, gvec_ref, ad_ref, own_ref, oth_ref = rest[8:14]
    wu_ref, wd_ref, dm_ref = rest[14:]
    s, core = pl.program_id(0), core_ref[0]
    dy = dh_ref[...].astype(BF)

    @pl.when(s == 0)
    def _():
        n, _ = norm(hm_ref[...])
        m = (n * vec_ref[2:3, :] + vec_ref[3:4, :]).astype(BF)
        keep_halves(own_ref, oth_ref, 0, m)
        keep_halves(own_ref, oth_ref, 1, dy)
        dm_ref[...] = jnp.zeros((TOK, D), F32)

    assemble(1, s, core, up, wu_ref)
    assemble(2, s, core, down, wd_ref)
    total = jnp.zeros((TOK, D), F32)
    for g in (0, 1):
        u = u_ref[0, g]
        act, t = gelu_parts(u)
        slope = 0.5 * (1.0 + t) + (0.5 * C0) * u * (1.0 - t * t) * (1.0 + (3.0 * C1) * (u * u))
        du = dot(dy, wd_ref[g]) * slope
        gbu_ref[0, g : g + 1, :] = col_sum(du)
        dub = du.astype(BF)
        ad_ref[0, g, 0] = dub
        ad_ref[0, g, 1] = act.astype(BF)
        total = total + dot_nt(dub, wu_ref[g])
    dm_ref[...] += total

    @pl.when(s == 3)
    def _():
        n, inv = norm(hm_ref[...])
        dm, dh = dm_ref[...], dh_ref[...]
        dhm_ref[...] = dh + norm_back(dm, n, inv, vec_ref[2:3, :])
        gvec_ref[...] = jnp.zeros((8, D), F32)
        gvec_ref[0:1, :] = col_sum(dm * n)
        gvec_ref[1:2, :] = col_sum(dm)
        gvec_ref[2:3, :] = col_sum(dh)


def feed_bwd(core, slopes, dh, hm, vec, u, up, down):
    half = (2, TOK, 512)
    return call(
        feed_bwd_body,
        "feed_bwd",
        core,
        slopes,
        (dh, hm, vec, u, *merged(1, up), *merged(2, down)),
        [whole((TOK, D)), whole((TOK, D)), whole((8, D)), per_step((4, 2, TOK, 512))]
        + quad_specs(1)
        + quad_specs(2),
        [sds((TOK, D)), sds((4, 2, 512)), sds((8, D)), sds((4, 2, 2, TOK, 512), BF)]
        + [sds(half, BF)] * 2,
        [whole((TOK, D)), per_step((4, 2, 512)), whole((8, D)), per_step((4, 2, 2, TOK, 512))]
        + [whole(half)] * 2,
        [pltpu.VMEM((2, D, 512), BF)] * 2 + [pltpu.VMEM((TOK, D), F32)],
    )


def attn_bwd_body(core_ref, slope_ref, dhm_ref, h_ref, vec_ref, qkv_ref, ctx_ref, *rest):
    quad, (dh_ref, gqv_ref, gvec_ref, dc_ref, own_ref, oth_ref) = rest[:4], rest[4:10]
    w_ref, da_ref = rest[10:]
    s, core = pl.program_id(0), core_ref[0]
    dz = dhm_ref[...].astype(BF)

    @pl.when(s == 0)
    def _():
        n, _ = norm(h_ref[...])
        a = (n * vec_ref[0:1, :] + vec_ref[1:2, :]).astype(BF)
        keep_halves(own_ref, oth_ref, 0, a)
        keep_halves(own_ref, oth_ref, 1, dz)
        da_ref[...] = jnp.zeros((TOK, D), F32)

    assemble(0, s, core, quad, w_ref)
    total = jnp.zeros((TOK, D), F32)
    for g in (0, 1):
        qkv = qkv_ref[0, g]
        dctx = dot(dz, w_ref[g, :, 384:512]).astype(BF)
        grads = [[], [], []]
        for hd in (0, 1):
            q, k, v = (qkv[:, j * 128 + hd * 64 : j * 128 + hd * 64 + 64] for j in range(3))
            dc = dctx[:, hd * 64 : hd * 64 + 64]
            p = chance_of(q, k, slope_ref[s * 4 + g * 2 + hd])
            dp = dot_nt(dc, v)
            delta = jnp.sum(p * dp, axis=-1, keepdims=True)
            ds = (p * (dp - delta) * 0.125).astype(BF)
            grads[0].append(dot(ds, k))
            grads[1].append(dot_tn(ds, q))
            grads[2].append(dot_tn(p.astype(BF), dc))
        dqkv = jnp.concatenate([g_ for three in grads for g_ in three], axis=1)
        gqv_ref[0, g : g + 1, :] = col_sum(dqkv)
        dqkv = dqkv.astype(BF)
        dc_ref[0, g, :, 0:384] = dqkv
        dc_ref[0, g, :, 384:512] = ctx_ref[0, g]
        total = total + dot_nt(dqkv, w_ref[g, :, 0:384])
    da_ref[...] += total

    @pl.when(s == 3)
    def _():
        n, inv = norm(h_ref[...])
        da, dhm = da_ref[...], dhm_ref[...]
        dh_ref[...] = dhm + norm_back(da, n, inv, vec_ref[0:1, :])
        gvec_ref[...] = jnp.zeros((8, D), F32)
        gvec_ref[0:1, :] = col_sum(da * n)
        gvec_ref[1:2, :] = col_sum(da)
        gvec_ref[2:3, :] = col_sum(dhm)


def attn_bwd(core, slopes, dhm, h, vec, qkv, ctx, quad):
    half = (2, TOK, 512)
    return call(
        attn_bwd_body,
        "attn_bwd",
        core,
        slopes,
        (dhm, h, vec, qkv, ctx, *merged(0, quad)),
        [
            whole((TOK, D)),
            whole((TOK, D)),
            whole((8, D)),
            per_step((4, 2, TOK, 384)),
            per_step((4, 2, TOK, 128)),
        ]
        + quad_specs(0),
        [sds((TOK, D)), sds((4, 2, 384)), sds((8, D)), sds((4, 2, TOK, 512), BF)]
        + [sds(half, BF)] * 2,
        [whole((TOK, D)), per_step((4, 2, 384)), whole((8, D)), per_step((4, 2, TOK, 512))]
        + [whole(half)] * 2,
        [pltpu.VMEM((2, D, 512), BF), pltpu.VMEM((TOK, D), F32)],
    )


def both_tokens(mine, theirs):
    return turned(jnp.concatenate([mine, theirs], axis=0))


def feed_grad_body(core_ref, slope_ref, ad_ref, ad2_ref, own_ref, own2_ref, *rest):
    gup, gdown, (mt_ref, dyt_ref, gu_ref, gd_ref) = rest[:2], rest[2:4], rest[4:]
    s, core = pl.program_id(0), core_ref[0]

    @pl.when(s == 0)
    def _():
        mt_ref[...] = both_tokens(own_ref[0], own2_ref[0])
        dyt_ref[...] = both_tokens(own_ref[1], own2_ref[1])

    for g in (0, 1):
        du = jnp.concatenate([ad_ref[0, g, 0], ad2_ref[0, g, 0]], axis=0)
        act = jnp.concatenate([ad_ref[0, g, 1], ad2_ref[0, g, 1]], axis=0)
        gu_ref[g] = dot(mt_ref[...], du).astype(BF)
        gd_ref[g] = dot(dyt_ref[...], act).astype(BF)
    disassemble(1, s, core, gup, gu_ref)
    disassemble(2, s, core, gdown, gd_ref)


def attn_grad_body(core_ref, slope_ref, dc_ref, dc2_ref, own_ref, own2_ref, *rest):
    gmix, (at_ref, dzt_ref, gw_ref) = rest[:2], rest[2:]
    s, core = pl.program_id(0), core_ref[0]

    @pl.when(s == 0)
    def _():
        at_ref[...] = both_tokens(own_ref[0], own2_ref[0])
        dzt_ref[...] = both_tokens(own_ref[1], own2_ref[1])

    for g in (0, 1):
        dc = jnp.concatenate([dc_ref[0, g], dc2_ref[0, g]], axis=0)
        gw_ref[g, :, 0:384] = dot(at_ref[...], dc[:, 0:384]).astype(BF)
        gw_ref[g, :, 384:512] = dot(dzt_ref[...], dc[:, 384:512]).astype(BF)
    disassemble(0, s, core, gmix, gw_ref)


def weight_grads(body, name, parts, core, slopes, cols, cols2, rows, rows2):
    zeros = (0,) * (cols.ndim - 1)
    crossed = pl.BlockSpec((1, *cols.shape[1:]), lambda s, *_: ((s % 2) * 2 + s // 2, *zeros))
    outs = call(
        body,
        name,
        core,
        slopes,
        (cols, cols2, rows, rows2),
        [per_step(cols.shape), crossed, whole(rows.shape), whole(rows.shape)],
        [v for part in parts for v in quad_shapes(part)[:2]],
        [v for part in parts for v in quad_specs(part)[:2]],
        [pltpu.VMEM((512, 2 * TOK), BF)] * 2 + [pltpu.VMEM((2, 512, 512), BF)] * len(parts),
    )
    return [unmerged(outs[2 * i : 2 * i + 2]) for i in range(len(parts))]


def orders():
    at = {a: lax.axis_index(a) for a in AXES}
    rows = []
    for half, low, z2, z1 in itertools.product((0, 1), repeat=4):
        core = at["core"] ^ half
        z = at["z"] ^ jnp.where(core == 0, z1 ^ (3 * z2), (3 * z1) ^ z2)
        rows.append(((at["ylo"] ^ low) * 4 + z) * 2 + core)
    cols = []
    for x2, x1, g in itertools.product((0, 1), repeat=3):
        x = at["x"] ^ jnp.where(at["core"] == 0, x1 ^ (3 * x2), (3 * x1) ^ x2)
        cols.append(x * 2 + (at["yhi"] ^ g))
    return at, jnp.stack(rows), jnp.stack(cols)


def one_hot(index, count):
    return (index[:, None] == jnp.arange(count)[None, :]).astype(F32)


def shards(
    hidden_in, w_qkv, w_attn_out, w_up, w_down, qv_bias, up_bias, ln_gain, row_bias, cotangent
):
    at, rows, cols = orders()
    core = at["core"].reshape(1).astype(jnp.int32)
    lanes = (rows[:, None] * 64 + jnp.arange(64)[None, :]).reshape(-1)
    lane_hot = one_hot(lanes, D)

    def to_own(v):
        return lax.dot_general(v, lane_hot, (((1,), (1,)), ((), ())), precision=HIGH)

    def from_own(v):
        return jnp.dot(v, lane_hot, precision=HIGH)

    heads = cols[:, None] * 2 + jnp.arange(2)[None, :]
    slopes = jnp.exp2(-8.0 * (heads.astype(F32) + 1.0) / HEADS).reshape(-1)

    p = (at["ylo"] * 4 + at["z"]) * 2 + at["core"]
    col_hot = one_hot(cols, 8)
    own_rows = jnp.concatenate([ln_gain.reshape(64, 4), row_bias.reshape(64, 8)], axis=1)
    own_cols = jnp.concatenate([qv_bias.reshape(4, 2, 4), up_bias], axis=2).reshape(4, 24)
    small = jnp.concatenate([own_rows.T.reshape(-1), own_cols.T.reshape(-1)])
    small = jnp.pad(small, (0, 160)).reshape(8, 128)
    at_row = jnp.arange(1536)
    moved = (at_row % 96) // 4 * 64 + at_row // 96 * 4 + at_row % 4
    move = (moved[:, None] == at_row[None, :]).astype(BF)

    def unpacked(small):
        small = small.reshape(16, 8, 8, 128)
        whole_rows = small[:, 0, :6].reshape(16, 12, 64).swapaxes(0, 1).reshape(12, D)
        whole_rows = to_own(whole_rows.astype(F32))
        gains, shifts = whole_rows[:4].reshape(2, 2, D), whole_rows[4:].reshape(2, 4, D)
        whole_cols = dot(small[:, :, 6, :96].swapaxes(0, 1).reshape(8, 1536), move)
        whole_cols = jnp.dot(col_hot, whole_cols, precision=HIGH)
        whole_cols = whole_cols.reshape(4, 2, LAYERS, 12, 64)
        vecs, qkv_shifts, up_shifts = [], [], []
        for l in range(LAYERS):
            vecs.append(
                jnp.concatenate(
                    [gains[l, 0:1], shifts[l, 0:1], gains[l, 1:2], shifts[l, 1:4]]
                    + [jnp.zeros((2, D), F32)]
                )
            )
            qv = whole_cols[:, :, l, :4].reshape(4, 2, 2, 128)
            qkv_shifts.append(
                jnp.concatenate([qv[:, :, 0], jnp.zeros((4, 2, 128), F32), qv[:, :, 1]], axis=2)
            )
            up_shifts.append(whole_cols[:, :, l, 4:].reshape(4, 2, 512))
        return vecs, qkv_shifts, up_shifts

    h, dh = to_own(hidden_in), to_own(cotangent)
    bufs = joined(
        jnp.concatenate([w_qkv.reshape(64, LAYERS, 384), w_attn_out], axis=2).swapaxes(0, 1),
        w_up.swapaxes(0, 1),
        w_down.swapaxes(0, 1),
    )
    for n in range(COMMON):
        (recv,) = joined(exchange(bufs, n))
        bufs = doubled(bufs, recv)
    first, second = ([b[..., l, :, :] for b in bufs] for l in range(LAYERS))

    recv, h, dh = joined(exchange(first, 4), h, dh)
    first = doubled(first, recv)
    first_hi, first_oth, small = joined(
        exchange(first, 5),
        over_cores_in_turn(first),
        to_each(jnp.broadcast_to(small[None], (128, 8, 128))),
    )

    second, mix_oth, first_hi, small = joined(
        second, swap(first_hi[0], "core"), first_hi, unpacked(small)
    )
    vecs, qkv_shifts, up_shifts = small
    mix0 = (first[0], first_hi[0], first_oth[0], mix_oth)
    (qkv0, ctx0, hm0), rest_oth, recv = joined(
        attn_fwd(core, slopes, h, vecs[0], qkv_shifts[0], mix0),
        over_cores(first_hi[1:]),
        exchange(second, 4),
    )
    second = doubled(second, recv)
    up0, down0 = ((first[i], first_hi[i], first_oth[i], rest_oth[i - 1]) for i in (1, 2))
    (u0, h1), second_hi, second_oth = joined(
        feed_fwd(core, slopes, hm0, vecs[0], up_shifts[0], up0, down0),
        exchange(second, 5),
        over_cores_in_turn(second),
    )
    h1, mix_oth, second_hi = joined(h1, swap(second_hi[0], "core"), second_hi)
    mix1 = (second[0], second_hi[0], second_oth[0], mix_oth)
    (qkv1, ctx1, hm1), rest_oth = joined(
        attn_fwd(core, slopes, h1, vecs[1], qkv_shifts[1], mix1), over_cores(second_hi[1:])
    )
    up1, down1 = ((second[i], second_hi[i], second_oth[i], rest_oth[i - 1]) for i in (1, 2))
    u1, out = feed_fwd(core, slopes, hm1, vecs[1], up_shifts[1], up1, down1)

    def sent(part, hi, n):
        return swap(hi, ORDERS[part][n // 2], n % 2 + 1)

    feed_grads = partial(weight_grads, feed_grad_body, "feed_grad", (1, 2), core, slopes)
    attn_grads = partial(weight_grads, attn_grad_body, "attn_grad", (0,), core, slopes)

    dhm1, gbu1, gvec21, ad1, md1, md1_oth = feed_bwd(core, slopes, dh, hm1, vecs[1], u1, up1, down1)
    (dh, gqv1, gvec11, dc1, az1, az1_oth), ad1_got, md1_got = joined(
        attn_bwd(core, slopes, dhm1, h1, vecs[1], qkv1, ctx1, mix1),
        swap(ad1, "core"),
        swap(md1_oth, "core"),
    )
    (gup1, gdown1), dc1_got, az1_got = joined(
        feed_grads(ad1, ad1_got, md1, md1_got), swap(dc1, "core"), swap(az1_oth, "core")
    )
    up_got, down_got = sent(1, gup1[1], 5), sent(2, gdown1[1], 5)
    (gmix1,) = attn_grads(dc1, dc1_got, az1, az1_got)
    dh, gmix1 = joined(dh, gmix1)
    mix_got = sent(0, gmix1[1], 5)
    dhm0, gbu0, gvec20, ad0, md0, md0_oth = feed_bwd(core, slopes, dh, hm0, vecs[0], u0, up0, down0)
    (dh, gqv0, gvec10, dc0, az0, az0_oth), ad0_got, md0_got, got = joined(
        attn_bwd(core, slopes, dhm0, h, vecs[0], qkv0, ctx0, mix0),
        swap(ad0, "core"),
        swap(md0_oth, "core"),
        [mix_got, up_got, down_got],
    )
    his = [plus(g[0][1], r[1]) for g, r in zip((gmix1, gup1, gdown1), got)]
    ad0, his = joined(ad0, his)
    (gup0, gdown0), dc0_got, az0_got, got1, lay1 = joined(
        feed_grads(ad0, ad0_got, md0, md0_got),
        swap(dc0, "core"),
        swap(az0_oth, "core"),
        [sent(i, his[i], 4) for i in range(3)],
        [(g[0], r) for g, r in zip((gmix1, gup1, gdown1), got)],
    )
    up_got, down_got = sent(1, gup0[1], 5), sent(2, gdown0[1], 5)
    (gmix0,) = attn_grads(dc0, dc0_got, az0, az0_got)
    mix_got = sent(0, gmix0[1], 5)
    rows = jnp.concatenate(
        [
            v
            for v1, v2 in ((gvec10, gvec20), (gvec11, gvec21))
            for v in (v1[0:1], v2[0:1], v1[1:2], v2[1:2], v1[2:3], v2[2:3])
        ]
    )
    cols = jnp.concatenate(
        [
            v
            for gqv, gbu in ((gqv0, gbu0), (gqv1, gbu1))
            for v in (gqv[:, :, :128], gqv[:, :, 256:], gbu)
        ],
        axis=2,
    ).reshape(8, 1536)
    rows = dot(rows.astype(BF), lane_hot.astype(BF)).astype(BF)
    rows = rows.reshape(12, 16, 64).swapaxes(0, 1).reshape(16, 1, 768)
    cols = dot_nt(dot_tn(col_hot.astype(BF), cols.astype(BF)).astype(BF), move).astype(BF)
    cols = cols.reshape(8, 16, 96).swapaxes(0, 1)
    small = jnp.concatenate([jnp.broadcast_to(rows, (16, 8, 768)), cols], axis=2)
    small = jnp.pad(small, ((0, 0), (0, 0), (0, 160))).reshape(128, 8, 128)
    dc0, lay1, got1 = joined(dc0, lay1, got1)
    got, small, grad_in, hidden_out, lay1 = joined(
        [mix_got, up_got, down_got],
        to_each(small),
        from_own(dh),
        from_own(out),
        [
            (lo[0].astype(F32) + r[0].astype(F32) + r1.astype(F32)).astype(BF)
            for (lo, r), r1 in zip(lay1, got1)
        ],
    )
    small = jnp.sum(small.astype(F32), axis=0).reshape(-1)
    rows = small[:768].reshape(12, 64).T.reshape(64, LAYERS, 6)
    cols = small[768:864].reshape(24, 4).T.reshape(4, LAYERS, 12)
    lay0 = [halves(g[0], r) for g, r in zip((gmix0, gup0, gdown0), got)]
    (got,) = joined([sent(i, lay0[i][1], 4) for i in range(3)])
    both = []
    for (lo, _), r, s1 in zip(lay0, got, lay1):
        hi, lo, r, s1 = joined(jnp.stack([plus(lo[1], r[1]), s1[1]], axis=3), lo, r, s1)
        both.append((jnp.stack([plus(lo[0], r[0]), s1[0]], axis=3), hi))
    for n in (3, 2, 1):
        (got,) = joined([sent(i, both[i][1], n) for i in range(3)])
        both = [halves(s[0], g) for s, g in zip(both, got)]
    (got,) = joined([sent(i, both[i][1], 0) for i in range(3)])
    mixes, ups, downs = (
        jnp.swapaxes(s[0].astype(F32) + g.astype(F32), 0, 1) for s, g in zip(both, got)
    )
    return (
        hidden_out,
        grad_in,
        mixes[:, :, :384].reshape(64, LAYERS, 3, 128),
        mixes[:, :, 384:],
        ups,
        downs,
        cols[:, :, :4].reshape(4, LAYERS, 2, 2),
        cols[:, :, 4:],
        rows[:, :, :2],
        rows[:, :, 2:],
    )


def solution(mesh):
    torus = Mesh(mesh.devices.reshape(SIZES), AXES)
    token = P((*DP, *TENSOR), None)
    placed = (
        token,
        P(DP, None, None, TENSOR),
        P(DP, None, TENSOR),
        P(DP, None, TENSOR),
        P(DP, None, TENSOR),
        P(DP, None, None, TENSOR),
        P(DP, None, TENSOR),
        P(DP, None, None),
        P(DP, None, None),
        token,
    )
    outs = (token, token, *placed[1:9])
    return jax.shard_map(shards, mesh=torus, in_specs=placed, out_specs=outs, check_vma=False)
```

```python
import itertools
from functools import partial

import jax
import jax.numpy as jnp
import numpy as np
from jax import lax
from jax.experimental import pallas as pl
from jax.experimental.pallas import tpu as pltpu
from jax.sharding import Mesh
from jax.sharding import PartitionSpec as P

AXES = ("ylo", "z", "core", "x", "yhi")
SIZES = (2, 4, 2, 4, 2)
DP = ("ylo", "z", "core")
TENSOR = ("x", "yhi")
ORDERS = ("xyz", "yzx", "zxy")
LAYERS = 2
COMMON = 4
TOK = 160
D = 1024
HEADS = 16
EPS = 1e-05
BF, F32 = jnp.bfloat16, jnp.float32
HIGH = lax.Precision.HIGHEST


def pairs(axis, step):
    out = []
    for ylo, z, core, x, yhi in itertools.product(*map(range, SIZES)):
        c = {"x": x, "y": 2 * yhi + ylo, "z": z, "core": core}
        if axis == "core":
            c["core"] ^= 1
        else:
            c[axis] ^= 1 if (step == 1) == (core == 0) else 3
        src = np.ravel_multi_index((ylo, z, core, x, yhi), SIZES)
        dst = np.ravel_multi_index((c["y"] & 1, c["z"], c["core"], c["x"], c["y"] >> 1), SIZES)
        out.append((int(src), int(dst)))
    return out


def swap(v, axis, step=0):
    return lax.ppermute(v, AXES, pairs(axis, step))


def joined(*values):
    return lax.optimization_barrier(values)


def exchange(bufs, n):
    return [swap(b, ORDERS[i][n // 2], n % 2 + 1) for i, b in enumerate(bufs)]


def doubled(bufs, recv):
    return [lax.optimization_barrier(jnp.stack([b, r])) for b, r in zip(bufs, recv)]


def over_cores(values):
    return [swap(v, "core") for v in values]


def over_cores_in_turn(values):
    one, two = over_cores(values[:2])
    one, last = joined(one, values[2])
    return [one, two, swap(last, "core")]


def to_each(v):
    return lax.all_to_all(v, AXES, 0, 0, tiled=True)


def plus(a, b):
    return (a.astype(F32) + b.astype(F32)).astype(BF)


def halves(lo, recv):
    hi, lo, recv = joined(plus(lo[1], recv[1]), lo, recv)
    return plus(lo[0], recv[0]), hi


def norm(h):
    center = jnp.mean(h, axis=-1, keepdims=True)
    c = h - center
    var = jnp.mean(c * c, axis=-1, keepdims=True)
    inv = lax.rsqrt(var + EPS)
    return c * inv, inv


def dot(a, b):
    return lax.dot_general(a, b, (((1,), (0,)), ((), ())), preferred_element_type=F32)


def dot_nt(a, b):
    return lax.dot_general(a, b, (((1,), (1,)), ((), ())), preferred_element_type=F32)


def dot_tn(a, b):
    return lax.dot_general(a, b, (((0,), (0,)), ((), ())), preferred_element_type=F32)


def turned(x):
    return jnp.transpose(x.astype(F32)).astype(BF)


BITS = tuple(itertools.product((0, 1), repeat=2))


def placed_at(core, half, y2, y1):
    if y1 == y2:
        return y1
    c = core if half == 0 else 1 - core
    return c if y1 else 1 - c


def each_block(part, step, quad):
    a, b = step // 2, step % 2
    for half in range(len(quad) // 2):
        lo, hi = quad[2 * half], quad[2 * half + 1]
        for (z2, z1), (y2, y1) in itertools.product(BITS, BITS):
            row = half * 8 + (y1 ^ y2) * 4 + z2 * 2 + z1
            if part == 0:
                yield None, half, y2, y1, row, (lo, hi)[z2], (z1 * 4 + y2 * 2 + y1, 0)
            elif part == 2:
                yield None, half, y2, y1, row, (lo, hi)[y2], (y1, 0, z2 * 2 + z1)
            else:
                which = a if half == 0 else b
                for x2 in (0, 1):
                    yield which == x2, half, y2, y1, row, (lo, hi)[x2], (0, z2 * 2 + z1, y2 * 2 + y1)


def by_condition(part, step, quad, fn):
    if part != 1:
        for _, *rest in each_block(part, step, quad):
            fn(*rest)
        return
    groups = {}
    for cond, half, *rest in each_block(part, step, quad):
        groups.setdefault((half, id(rest[3])), (cond, []))[1].append((half, *rest))
    for cond, items in groups.values():

        @pl.when(cond)
        def _(items=items):
            for it in items:
                fn(*it)


def assemble(part, step, core, quad, w_ref):
    def put(half, y2, y1, row, ref, index):
        w_ref[placed_at(core, half, y2, y1), row * 64 : row * 64 + 64, :] = ref[index]

    by_condition(part, step, quad, put)


def disassemble(part, step, core, quad, w_ref):
    def get(half, y2, y1, row, ref, index):
        ref[index] = w_ref[placed_at(core, half, y2, y1), row * 64 : row * 64 + 64, :]

    by_condition(part, step, quad, get)


def merged(part, quad):
    shape = {0: (8, 4, 64, 512), 1: (2, 4, 4, 64, 512), 2: (2, 4, 4, 64, 512)}[part]
    return tuple(q.reshape(shape) for q in quad)


def unmerged(quad):
    return tuple(q.reshape(2, 2, 2, 2, 2, 64, 512) for q in quad)


def quad_shapes(part):
    shape = {0: (8, 4, 64, 512), 1: (2, 4, 4, 64, 512), 2: (2, 4, 4, 64, 512)}[part]
    return [jax.ShapeDtypeStruct(shape, BF)] * 4


def quad_specs(part):
    def own(s):
        return s

    def oth(s):
        return (s % 2) * 2 + s // 2

    if part == 0:
        return [
            pl.BlockSpec((8, 1, 64, 512), lambda s, *_, f=f: (0, f(s), 0, 0))
            for f in (own, own, oth, oth)
        ]
    if part == 2:
        return [
            pl.BlockSpec((2, 1, 4, 64, 512), lambda s, *_, f=f: (0, f(s), 0, 0, 0))
            for f in (own, own, oth, oth)
        ]
    maps = (
        lambda s: jnp.minimum(s, 1),
        lambda s: jnp.maximum(s - 2, 0),
        lambda s: s // 2,
        lambda s: s // 2,
    )
    return [
        pl.BlockSpec((1, 4, 4, 64, 512), lambda s, *_, f=f: (f(s), 0, 0, 0, 0)) for f in maps
    ]


def whole(shape):
    zeros = (0,) * len(shape)
    return pl.BlockSpec(shape, lambda s, *_: zeros)


def per_step(shape):
    zeros = (0,) * (len(shape) - 1)
    return pl.BlockSpec((1, *shape[1:]), lambda s, *_: (s, *zeros))


def call(body, name, core, slopes, ins, in_specs, outs, out_specs, scratch):
    return pl.pallas_call(
        body,
        name=name,
        out_shape=outs,
        grid_spec=pltpu.PrefetchScalarGridSpec(
            num_scalar_prefetch=2,
            grid=(4,),
            in_specs=in_specs,
            out_specs=out_specs,
            scratch_shapes=scratch,
        ),
        cost_estimate=pl.CostEstimate(flops=1 << 20, transcendentals=0, bytes_accessed=1 << 18),
        compiler_params=pltpu.CompilerParams(
            dimension_semantics=("arbitrary",), vmem_limit_bytes=48 << 20
        ),
    )(core, slopes, *ins)


def sds(shape, dtype=F32):
    return jax.ShapeDtypeStruct(shape, dtype)


def scores_of(q, k, slope):
    s = dot_nt(q, k) * 0.125
    row = lax.broadcasted_iota(jnp.int32, (TOK, TOK), 0)
    col = lax.broadcasted_iota(jnp.int32, (TOK, TOK), 1)
    s = s + slope * (col - row).astype(F32)
    return jnp.where(col <= row, s, -jnp.inf)


def chance_of(q, k, slope):
    s = scores_of(q, k, slope)
    e = jnp.exp(s - jnp.max(s, axis=-1, keepdims=True))
    return e * (1.0 / jnp.sum(e, axis=-1, keepdims=True))


def attn_fwd_body(core_ref, slope_ref, h_ref, vec_ref, bias_ref, *rest):
    quad, (qkv_ref, ctx_ref, hm_ref), (w_ref, a_ref) = rest[:4], rest[4:7], rest[7:]
    s, core = pl.program_id(0), core_ref[0]

    @pl.when(s == 0)
    def _():
        n, _ = norm(h_ref[...])
        a_ref[...] = (n * vec_ref[0:1, :] + vec_ref[1:2, :]).astype(BF)
        hm_ref[...] = h_ref[...] + vec_ref[4:5, :]

    assemble(0, s, core, quad, w_ref)
    total = jnp.zeros((TOK, D), F32)
    for g in (0, 1):
        qkv = (dot(a_ref[...], w_ref[g, :, 0:384]) + bias_ref[0, g : g + 1, :]).astype(BF)
        qkv_ref[0, g] = qkv
        ctx = []
        for hd in (0, 1):
            q, k, v = (qkv[:, j * 128 + hd * 64 : j * 128 + hd * 64 + 64] for j in range(3))
            p = chance_of(q, k, slope_ref[s * 4 + g * 2 + hd]).astype(BF)
            ctx.append(dot(p, v))
        ctx = jnp.concatenate(ctx, axis=1).astype(BF)
        ctx_ref[0, g] = ctx
        total = total + dot_nt(ctx, w_ref[g, :, 384:512])
    hm_ref[...] += total


def attn_fwd(core, slopes, h, vec, bias, quad):
    return call(
        attn_fwd_body,
        "attn_fwd",
        core,
        slopes,
        (h, vec, bias, *merged(0, quad)),
        [whole((TOK, D)), whole((8, D)), per_step((4, 2, 384))] + quad_specs(0),
        [sds((4, 2, TOK, 384), BF), sds((4, 2, TOK, 128), BF), sds((TOK, D))],
        [per_step((4, 2, TOK, 384)), per_step((4, 2, TOK, 128)), whole((TOK, D))],
        [pltpu.VMEM((2, D, 512), BF), pltpu.VMEM((TOK, D), BF)],
    )


C0, C1 = 0.7978845608, 0.044715


def gelu_parts(u):
    t = jnp.tanh(C0 * (u + C1 * (u * u * u)))
    return 0.5 * u * (1.0 + t), t


def feed_fwd_body(core_ref, slope_ref, hm_ref, vec_ref, bias_ref, *rest):
    up, down, (u_ref, out_ref), (wu_ref, wd_ref, m_ref) = rest[:4], rest[4:8], rest[8:10], rest[10:]
    s, core = pl.program_id(0), core_ref[0]

    @pl.when(s == 0)
    def _():
        n, _ = norm(hm_ref[...])
        m_ref[...] = (n * vec_ref[2:3, :] + vec_ref[3:4, :]).astype(BF)
        out_ref[...] = hm_ref[...] + vec_ref[5:6, :]

    assemble(1, s, core, up, wu_ref)
    assemble(2, s, core, down, wd_ref)
    total = jnp.zeros((TOK, D), F32)
    for g in (0, 1):
        u = dot(m_ref[...], wu_ref[g]) + bias_ref[0, g : g + 1, :]
        u_ref[0, g] = u
        act, _ = gelu_parts(u)
        total = total + dot_nt(act.astype(BF), wd_ref[g])
    out_ref[...] += total


def feed_fwd(core, slopes, hm, vec, bias, up, down):
    return call(
        feed_fwd_body,
        "feed_fwd",
        core,
        slopes,
        (hm, vec, bias, *merged(1, up), *merged(2, down)),
        [whole((TOK, D)), whole((8, D)), per_step((4, 2, 512))] + quad_specs(1) + quad_specs(2),
        [sds((4, 2, TOK, 512)), sds((TOK, D))],
        [per_step((4, 2, TOK, 512)), whole((TOK, D))],
        [pltpu.VMEM((2, D, 512), BF), pltpu.VMEM((2, D, 512), BF), pltpu.VMEM((TOK, D), BF)],
    )


def norm_back(up, n, inv, gain):
    scaled = up * gain
    center = jnp.mean(scaled, axis=-1, keepdims=True)
    spread = jnp.mean(scaled * n, axis=-1, keepdims=True)
    return inv * (scaled - center - n * spread)


def col_sum(x):
    return jnp.sum(x, axis=0, keepdims=True)


def keep_halves(own_ref, oth_ref, i, x):
    own_ref[i] = x[:, :512]
    oth_ref[i] = x[:, 512:]


def feed_bwd_body(core_ref, slope_ref, dh_ref, hm_ref, vec_ref, u_ref, *rest):
    up, down = rest[:4], rest[4:8]
    dhm_ref, gbu_ref, gvec_ref, ad_ref, own_ref, oth_ref = rest[8:14]
    wu_ref, wd_ref, dm_ref = rest[14:]
    s, core = pl.program_id(0), core_ref[0]
    dy = dh_ref[...].astype(BF)

    @pl.when(s == 0)
    def _():
        n, _ = norm(hm_ref[...])
        m = (n * vec_ref[2:3, :] + vec_ref[3:4, :]).astype(BF)
        keep_halves(own_ref, oth_ref, 0, m)
        keep_halves(own_ref, oth_ref, 1, dy)
        dm_ref[...] = jnp.zeros((TOK, D), F32)

    assemble(1, s, core, up, wu_ref)
    assemble(2, s, core, down, wd_ref)
    total = jnp.zeros((TOK, D), F32)
    for g in (0, 1):
        u = u_ref[0, g]
        act, t = gelu_parts(u)
        slope = 0.5 * (1.0 + t) + (0.5 * C0) * u * (1.0 - t * t) * (1.0 + (3.0 * C1) * (u * u))
        du = dot(dy, wd_ref[g]) * slope
        gbu_ref[0, g : g + 1, :] = col_sum(du)
        dub = du.astype(BF)
        ad_ref[0, g, 0] = dub
        ad_ref[0, g, 1] = act.astype(BF)
        total = total + dot_nt(dub, wu_ref[g])
    dm_ref[...] += total

    @pl.when(s == 3)
    def _():
        n, inv = norm(hm_ref[...])
        dm, dh = dm_ref[...], dh_ref[...]
        dhm_ref[...] = dh + norm_back(dm, n, inv, vec_ref[2:3, :])
        gvec_ref[...] = jnp.zeros((8, D), F32)
        gvec_ref[0:1, :] = col_sum(dm * n)
        gvec_ref[1:2, :] = col_sum(dm)
        gvec_ref[2:3, :] = col_sum(dh)


def feed_bwd(core, slopes, dh, hm, vec, u, up, down):
    half = (2, TOK, 512)
    return call(
        feed_bwd_body,
        "feed_bwd",
        core,
        slopes,
        (dh, hm, vec, u, *merged(1, up), *merged(2, down)),
        [whole((TOK, D)), whole((TOK, D)), whole((8, D)), per_step((4, 2, TOK, 512))]
        + quad_specs(1)
        + quad_specs(2),
        [sds((TOK, D)), sds((4, 2, 512)), sds((8, D)), sds((4, 2, 2, TOK, 512), BF)]
        + [sds(half, BF)] * 2,
        [whole((TOK, D)), per_step((4, 2, 512)), whole((8, D)), per_step((4, 2, 2, TOK, 512))]
        + [whole(half)] * 2,
        [pltpu.VMEM((2, D, 512), BF)] * 2 + [pltpu.VMEM((TOK, D), F32)],
    )


def attn_bwd_body(core_ref, slope_ref, dhm_ref, h_ref, vec_ref, qkv_ref, ctx_ref, *rest):
    quad, (dh_ref, gqv_ref, gvec_ref, dc_ref, own_ref, oth_ref) = rest[:4], rest[4:10]
    w_ref, da_ref = rest[10:]
    s, core = pl.program_id(0), core_ref[0]
    dz = dhm_ref[...].astype(BF)

    @pl.when(s == 0)
    def _():
        n, _ = norm(h_ref[...])
        a = (n * vec_ref[0:1, :] + vec_ref[1:2, :]).astype(BF)
        keep_halves(own_ref, oth_ref, 0, a)
        keep_halves(own_ref, oth_ref, 1, dz)
        da_ref[...] = jnp.zeros((TOK, D), F32)

    assemble(0, s, core, quad, w_ref)
    total = jnp.zeros((TOK, D), F32)
    for g in (0, 1):
        qkv = qkv_ref[0, g]
        dctx = dot(dz, w_ref[g, :, 384:512]).astype(BF)
        grads = [[], [], []]
        for hd in (0, 1):
            q, k, v = (qkv[:, j * 128 + hd * 64 : j * 128 + hd * 64 + 64] for j in range(3))
            dc = dctx[:, hd * 64 : hd * 64 + 64]
            p = chance_of(q, k, slope_ref[s * 4 + g * 2 + hd])
            dp = dot_nt(dc, v)
            delta = jnp.sum(p * dp, axis=-1, keepdims=True)
            ds = (p * (dp - delta) * 0.125).astype(BF)
            grads[0].append(dot(ds, k))
            grads[1].append(dot_tn(ds, q))
            grads[2].append(dot_tn(p.astype(BF), dc))
        dqkv = jnp.concatenate([g_ for three in grads for g_ in three], axis=1)
        gqv_ref[0, g : g + 1, :] = col_sum(dqkv)
        dqkv = dqkv.astype(BF)
        dc_ref[0, g, :, 0:384] = dqkv
        dc_ref[0, g, :, 384:512] = ctx_ref[0, g]
        total = total + dot_nt(dqkv, w_ref[g, :, 0:384])
    da_ref[...] += total

    @pl.when(s == 3)
    def _():
        n, inv = norm(h_ref[...])
        da, dhm = da_ref[...], dhm_ref[...]
        dh_ref[...] = dhm + norm_back(da, n, inv, vec_ref[0:1, :])
        gvec_ref[...] = jnp.zeros((8, D), F32)
        gvec_ref[0:1, :] = col_sum(da * n)
        gvec_ref[1:2, :] = col_sum(da)
        gvec_ref[2:3, :] = col_sum(dhm)


def attn_bwd(core, slopes, dhm, h, vec, qkv, ctx, quad):
    half = (2, TOK, 512)
    return call(
        attn_bwd_body,
        "attn_bwd",
        core,
        slopes,
        (dhm, h, vec, qkv, ctx, *merged(0, quad)),
        [
            whole((TOK, D)),
            whole((TOK, D)),
            whole((8, D)),
            per_step((4, 2, TOK, 384)),
            per_step((4, 2, TOK, 128)),
        ]
        + quad_specs(0),
        [sds((TOK, D)), sds((4, 2, 384)), sds((8, D)), sds((4, 2, TOK, 512), BF)]
        + [sds(half, BF)] * 2,
        [whole((TOK, D)), per_step((4, 2, 384)), whole((8, D)), per_step((4, 2, TOK, 512))]
        + [whole(half)] * 2,
        [pltpu.VMEM((2, D, 512), BF), pltpu.VMEM((TOK, D), F32)],
    )


def both_tokens(mine, theirs):
    return turned(jnp.concatenate([mine, theirs], axis=0))


def feed_grad_body(core_ref, slope_ref, ad_ref, ad2_ref, own_ref, own2_ref, *rest):
    gup, gdown, (mt_ref, dyt_ref, gu_ref, gd_ref) = rest[:2], rest[2:4], rest[4:]
    s, core = pl.program_id(0), core_ref[0]

    @pl.when(s == 0)
    def _():
        mt_ref[...] = both_tokens(own_ref[0], own2_ref[0])
        dyt_ref[...] = both_tokens(own_ref[1], own2_ref[1])

    for g in (0, 1):
        du = jnp.concatenate([ad_ref[0, g, 0], ad2_ref[0, g, 0]], axis=0)
        act = jnp.concatenate([ad_ref[0, g, 1], ad2_ref[0, g, 1]], axis=0)
        gu_ref[g] = dot(mt_ref[...], du).astype(BF)
        gd_ref[g] = dot(dyt_ref[...], act).astype(BF)
    disassemble(1, s, core, gup, gu_ref)
    disassemble(2, s, core, gdown, gd_ref)


def attn_grad_body(core_ref, slope_ref, dc_ref, dc2_ref, own_ref, own2_ref, *rest):
    gmix, (at_ref, dzt_ref, gw_ref) = rest[:2], rest[2:]
    s, core = pl.program_id(0), core_ref[0]

    @pl.when(s == 0)
    def _():
        at_ref[...] = both_tokens(own_ref[0], own2_ref[0])
        dzt_ref[...] = both_tokens(own_ref[1], own2_ref[1])

    for g in (0, 1):
        dc = jnp.concatenate([dc_ref[0, g], dc2_ref[0, g]], axis=0)
        gw_ref[g, :, 0:384] = dot(at_ref[...], dc[:, 0:384]).astype(BF)
        gw_ref[g, :, 384:512] = dot(dzt_ref[...], dc[:, 384:512]).astype(BF)
    disassemble(0, s, core, gmix, gw_ref)


def weight_grads(body, name, parts, core, slopes, cols, cols2, rows, rows2):
    zeros = (0,) * (cols.ndim - 1)
    crossed = pl.BlockSpec((1, *cols.shape[1:]), lambda s, *_: ((s % 2) * 2 + s // 2, *zeros))
    outs = call(
        body,
        name,
        core,
        slopes,
        (cols, cols2, rows, rows2),
        [per_step(cols.shape), crossed, whole(rows.shape), whole(rows.shape)],
        [v for part in parts for v in quad_shapes(part)[:2]],
        [v for part in parts for v in quad_specs(part)[:2]],
        [pltpu.VMEM((512, 2 * TOK), BF)] * 2 + [pltpu.VMEM((2, 512, 512), BF)] * len(parts),
    )
    return [unmerged(outs[2 * i : 2 * i + 2]) for i in range(len(parts))]


def orders():
    at = {a: lax.axis_index(a) for a in AXES}
    rows = []
    for half, low, z2, z1 in itertools.product((0, 1), repeat=4):
        core = at["core"] ^ half
        z = at["z"] ^ jnp.where(core == 0, z1 ^ (3 * z2), (3 * z1) ^ z2)
        rows.append(((at["ylo"] ^ low) * 4 + z) * 2 + core)
    cols = []
    for x2, x1, g in itertools.product((0, 1), repeat=3):
        x = at["x"] ^ jnp.where(at["core"] == 0, x1 ^ (3 * x2), (3 * x1) ^ x2)
        cols.append(x * 2 + (at["yhi"] ^ g))
    return at, jnp.stack(rows), jnp.stack(cols)


def one_hot(index, count):
    return (index[:, None] == jnp.arange(count)[None, :]).astype(F32)


def shards(
    hidden_in, w_qkv, w_attn_out, w_up, w_down, qv_bias, up_bias, ln_gain, row_bias, cotangent
):
    at, rows, cols = orders()
    core = at["core"].reshape(1).astype(jnp.int32)
    lanes = (rows[:, None] * 64 + jnp.arange(64)[None, :]).reshape(-1)
    lane_hot = one_hot(lanes, D)

    def to_own(v):
        return lax.dot_general(v, lane_hot, (((1,), (1,)), ((), ())), precision=HIGH)

    def from_own(v):
        return jnp.dot(v, lane_hot, precision=HIGH)

    heads = cols[:, None] * 2 + jnp.arange(2)[None, :]
    slopes = jnp.exp2(-8.0 * (heads.astype(F32) + 1.0) / HEADS).reshape(-1)

    p = (at["ylo"] * 4 + at["z"]) * 2 + at["core"]
    col_hot = one_hot(cols, 8)
    own_rows = jnp.concatenate([ln_gain.reshape(64, 4), row_bias.reshape(64, 8)], axis=1)
    own_cols = jnp.concatenate([qv_bias.reshape(4, 2, 4), up_bias], axis=2).reshape(4, 24)
    small = jnp.concatenate([own_rows.T.reshape(-1), own_cols.T.reshape(-1)])
    small = jnp.pad(small, (0, 160)).reshape(8, 128)
    at_row = jnp.arange(1536)
    moved = (at_row % 96) // 4 * 64 + at_row // 96 * 4 + at_row % 4
    move = (moved[:, None] == at_row[None, :]).astype(BF)

    def unpacked(small):
        small = small.reshape(16, 8, 8, 128)
        whole_rows = small[:, 0, :6].reshape(16, 12, 64).swapaxes(0, 1).reshape(12, D)
        whole_rows = to_own(whole_rows.astype(F32))
        gains, shifts = whole_rows[:4].reshape(2, 2, D), whole_rows[4:].reshape(2, 4, D)
        whole_cols = dot(small[:, :, 6, :96].swapaxes(0, 1).reshape(8, 1536), move)
        whole_cols = jnp.dot(col_hot, whole_cols, precision=HIGH)
        whole_cols = whole_cols.reshape(4, 2, LAYERS, 12, 64)
        vecs, qkv_shifts, up_shifts = [], [], []
        for l in range(LAYERS):
            vecs.append(
                jnp.concatenate(
                    [gains[l, 0:1], shifts[l, 0:1], gains[l, 1:2], shifts[l, 1:4]]
                    + [jnp.zeros((2, D), F32)]
                )
            )
            qv = whole_cols[:, :, l, :4].reshape(4, 2, 2, 128)
            qkv_shifts.append(
                jnp.concatenate([qv[:, :, 0], jnp.zeros((4, 2, 128), F32), qv[:, :, 1]], axis=2)
            )
            up_shifts.append(whole_cols[:, :, l, 4:].reshape(4, 2, 512))
        return vecs, qkv_shifts, up_shifts

    h, dh = to_own(hidden_in), to_own(cotangent)
    bufs = joined(
        jnp.concatenate([w_qkv.reshape(64, LAYERS, 384), w_attn_out], axis=2).swapaxes(0, 1),
        w_up.swapaxes(0, 1),
        w_down.swapaxes(0, 1),
    )
    for n in range(COMMON):
        (recv,) = joined(exchange(bufs, n))
        bufs = doubled(bufs, recv)
    first, second = ([b[..., l, :, :] for b in bufs] for l in range(LAYERS))

    recv, h, dh = joined(exchange(first, 4), h, dh)
    first = doubled(first, recv)
    first_hi, first_oth, small = joined(
        exchange(first, 5),
        over_cores_in_turn(first),
        to_each(jnp.broadcast_to(small[None], (128, 8, 128))),
    )

    second, mix_oth, first_hi, small = joined(
        second, swap(first_hi[0], "core"), first_hi, unpacked(small)
    )
    vecs, qkv_shifts, up_shifts = small
    mix0 = (first[0], first_hi[0], first_oth[0], mix_oth)
    (qkv0, ctx0, hm0), rest_oth, recv = joined(
        attn_fwd(core, slopes, h, vecs[0], qkv_shifts[0], mix0),
        over_cores(first_hi[1:]),
        exchange(second, 4),
    )
    second = doubled(second, recv)
    up0, down0 = ((first[i], first_hi[i], first_oth[i], rest_oth[i - 1]) for i in (1, 2))
    (u0, h1), second_hi, second_oth = joined(
        feed_fwd(core, slopes, hm0, vecs[0], up_shifts[0], up0, down0),
        exchange(second, 5),
        over_cores_in_turn(second),
    )
    h1, mix_oth, second_hi = joined(h1, swap(second_hi[0], "core"), second_hi)
    mix1 = (second[0], second_hi[0], second_oth[0], mix_oth)
    (qkv1, ctx1, hm1), rest_oth = joined(
        attn_fwd(core, slopes, h1, vecs[1], qkv_shifts[1], mix1), over_cores(second_hi[1:])
    )
    up1, down1 = ((second[i], second_hi[i], second_oth[i], rest_oth[i - 1]) for i in (1, 2))
    u1, out = feed_fwd(core, slopes, hm1, vecs[1], up_shifts[1], up1, down1)

    def sent(part, hi, n):
        return swap(hi, ORDERS[part][n // 2], n % 2 + 1)

    feed_grads = partial(weight_grads, feed_grad_body, "feed_grad", (1, 2), core, slopes)
    attn_grads = partial(weight_grads, attn_grad_body, "attn_grad", (0,), core, slopes)

    dhm1, gbu1, gvec21, ad1, md1, md1_oth = feed_bwd(core, slopes, dh, hm1, vecs[1], u1, up1, down1)
    (dh, gqv1, gvec11, dc1, az1, az1_oth), ad1_got, md1_got = joined(
        attn_bwd(core, slopes, dhm1, h1, vecs[1], qkv1, ctx1, mix1),
        swap(ad1, "core"),
        swap(md1_oth, "core"),
    )
    (gup1, gdown1), dc1_got, az1_got = joined(
        feed_grads(ad1, ad1_got, md1, md1_got), swap(dc1, "core"), swap(az1_oth, "core")
    )
    up_got, down_got = sent(1, gup1[1], 5), sent(2, gdown1[1], 5)
    (gmix1,) = attn_grads(dc1, dc1_got, az1, az1_got)
    dh, gmix1 = joined(dh, gmix1)
    mix_got = sent(0, gmix1[1], 5)
    dhm0, gbu0, gvec20, ad0, md0, md0_oth = feed_bwd(core, slopes, dh, hm0, vecs[0], u0, up0, down0)
    (dh, gqv0, gvec10, dc0, az0, az0_oth), ad0_got, md0_got, got = joined(
        attn_bwd(core, slopes, dhm0, h, vecs[0], qkv0, ctx0, mix0),
        swap(ad0, "core"),
        swap(md0_oth, "core"),
        [mix_got, up_got, down_got],
    )
    his = [plus(g[0][1], r[1]) for g, r in zip((gmix1, gup1, gdown1), got)]
    ad0, his = joined(ad0, his)
    (gup0, gdown0), dc0_got, az0_got, got1, lay1 = joined(
        feed_grads(ad0, ad0_got, md0, md0_got),
        swap(dc0, "core"),
        swap(az0_oth, "core"),
        [sent(i, his[i], 4) for i in range(3)],
        [(g[0], r) for g, r in zip((gmix1, gup1, gdown1), got)],
    )
    up_got, down_got = sent(1, gup0[1], 5), sent(2, gdown0[1], 5)
    (gmix0,) = attn_grads(dc0, dc0_got, az0, az0_got)
    gmix0, out = joined(gmix0, out)
    mix_got = sent(0, gmix0[1], 5)
    rows = jnp.concatenate(
        [
            v
            for v1, v2 in ((gvec10, gvec20), (gvec11, gvec21))
            for v in (v1[0:1], v2[0:1], v1[1:2], v2[1:2], v1[2:3], v2[2:3])
        ]
    )
    cols = jnp.concatenate(
        [
            v
            for gqv, gbu in ((gqv0, gbu0), (gqv1, gbu1))
            for v in (gqv[:, :, :128], gqv[:, :, 256:], gbu)
        ],
        axis=2,
    ).reshape(8, 1536)
    rows = dot(rows.astype(BF), lane_hot.astype(BF)).astype(BF)
    rows = rows.reshape(12, 16, 64).swapaxes(0, 1).reshape(16, 1, 768)
    cols = dot_nt(dot_tn(col_hot.astype(BF), cols.astype(BF)).astype(BF), move).astype(BF)
    cols = cols.reshape(8, 16, 96).swapaxes(0, 1)
    small = jnp.concatenate([jnp.broadcast_to(rows, (16, 8, 768)), cols], axis=2)
    small = jnp.pad(small, ((0, 0), (0, 0), (0, 160))).reshape(128, 8, 128)
    dc0, lay1, got1 = joined(dc0, lay1, got1)
    got, small, grad_in, hidden_out, lay1 = joined(
        [mix_got, up_got, down_got],
        to_each(small),
        from_own(dh),
        from_own(out),
        [
            (lo[0].astype(F32) + r[0].astype(F32) + r1.astype(F32)).astype(BF)
            for (lo, r), r1 in zip(lay1, got1)
        ],
    )
    small = jnp.sum(small.astype(F32), axis=0).reshape(-1)
    rows = small[:768].reshape(12, 64).T.reshape(64, LAYERS, 6)
    cols = small[768:864].reshape(24, 4).T.reshape(4, LAYERS, 12)
    lay0 = [halves(g[0], r) for g, r in zip((gmix0, gup0, gdown0), got)]
    (got,) = joined([sent(i, lay0[i][1], 4) for i in range(3)])
    both = []
    for (lo, _), r, s1 in zip(lay0, got, lay1):
        hi, lo, r, s1 = joined(jnp.stack([plus(lo[1], r[1]), s1[1]], axis=3), lo, r, s1)
        both.append((jnp.stack([plus(lo[0], r[0]), s1[0]], axis=3), hi))
    for n in (3, 2, 1):
        (got,) = joined([sent(i, both[i][1], n) for i in range(3)])
        both = [halves(s[0], g) for s, g in zip(both, got)]
    (got,) = joined([sent(i, both[i][1], 0) for i in range(3)])
    mixes, ups, downs = (
        jnp.swapaxes(s[0].astype(F32) + g.astype(F32), 0, 1) for s, g in zip(both, got)
    )
    return (
        hidden_out,
        grad_in,
        mixes[:, :, :384].reshape(64, LAYERS, 3, 128),
        mixes[:, :, 384:],
        ups,
        downs,
        cols[:, :, :4].reshape(4, LAYERS, 2, 2),
        cols[:, :, 4:],
        rows[:, :, :2],
        rows[:, :, 2:],
    )


def solution(mesh):
    torus = Mesh(mesh.devices.reshape(SIZES), AXES)
    token = P((*DP, *TENSOR), None)
    placed = (
        token,
        P(DP, None, None, TENSOR),
        P(DP, None, TENSOR),
        P(DP, None, TENSOR),
        P(DP, None, TENSOR),
        P(DP, None, None, TENSOR),
        P(DP, None, TENSOR),
        P(DP, None, None),
        P(DP, None, None),
        token,
    )
    outs = (token, token, *placed[1:9])
    return jax.shard_map(shards, mesh=torus, in_specs=placed, out_specs=outs, check_vma=False)
```
